256 devices in a mesh: rep: 32 (over y, z_lo, x), tp: 8 (over z_hi, core).
Axes of the slice: x: 4, y: 4, z: 8 (z_hi: 4, z_lo: 2; z = z_hi * 2 + z_lo), core: 2. Of those that a mesh axis runs over, the one named last changes fastest.
Arguments:
- tokens: bfloat16 [4096, 4096], P('rep'), may hold values from -6 to 6
- targets: bfloat16 [4096, 4096], P('rep'), may hold values from -6 to 6
- frozen_in_matrix: bfloat16 [4096, 8192], P('rep', 'tp'), may hold values from -6 to 6
- base_out: bfloat16 [8192, 4096], P('tp', 'rep'), may hold values from -6 to 6
- factor_down: bfloat16 [32, 16, 4096], P('rep'), may hold values from -6 to 6
- factor_up: bfloat16 [32, 16, 8192], P('rep', None, 'tp'), may hold values from -0.75 to 0.75
Outputs:
- merged: float32 [4096, 8192], P('rep', 'tp')
- new_down: float32 [32, 16, 4096], P('rep')
- new_up: float32 [32, 16, 8192], P('rep', None, 'tp')
The draws below stay inside these ranges and needn't reach their ends.
All inputs are finite; a program needn't handle non-finite values.
Results may differ from the reference program's by a relative error of at most 0.014.
The reference program's roundings to bfloat16 on the way count: a program that leaves them out, or rounds other values in their place, can miss the bound.
Values may be sent and summed in bfloat16 or wider, within the bound.
No kernel may reach another device: no remote copies, remote signals or barrier semaphores. Data moves between devices by JAX's collectives and lax.ppermute only.
A program may use at most 128 MiB of HBM per device.

```python
import jax
import jax.numpy as jnp
from jax import lax

MODEL_WIDTH = 4096
FF = 8192
RANK = 16
TOK_DEV = 128
REPLICA_COUNT = 32
TOKENS = 4096


def shard_levels(rng, shape, split, least, top_value):
    level, own = 1.0, jax.random.fold_in(rng, 6)
    for position, parts in split:
        draws = jnp.exp(jax.random.uniform(jax.random.fold_in(own, position), (parts,), jnp.float32, least / len(split), top_value / len(split)))
        level = level * jnp.repeat(draws, shape[position] // parts).reshape([-1 if axis == position else 1 for axis in range(len(shape))])
    return level


def gaussian(key, shape, scale, reach, shards=(), dtype=jnp.bfloat16):
    result = jax.random.normal(key, shape, jnp.float32) * scale
    if len(shards) > 0:
        result = shard_levels(key, shape, shards, -0.22, 0.18) * result
    return jnp.clip(result, min=-reach, max=reach).astype(dtype)


def setup_inputs(seed: int = 0) -> dict:
    seeds = jax.random.split(jax.random.key(seed), 7)
    tokens = gaussian(seeds[0], (TOKENS, MODEL_WIDTH), 1.0, 6.0, ((0, 32),))
    targets = gaussian(seeds[1], (TOKENS, MODEL_WIDTH), 1.0, 6.0, ((0, 32),))
    frozen_in_matrix = gaussian(seeds[2], (MODEL_WIDTH, FF), 1.0, 6.0, ((0, 32), (1, 8)))
    base_out = gaussian(seeds[3], (FF, MODEL_WIDTH), 1.0, 6.0, ((0, 8), (1, 32)))
    factor_down = gaussian(seeds[4], (REPLICA_COUNT, RANK, MODEL_WIDTH), 1.0, 6.0, ((0, 32),))
    factor_up = gaussian(seeds[5], (REPLICA_COUNT, RANK, FF), 0.125, 0.75, ((0, 32), (2, 8)))
    return {"tokens": tokens, "targets": targets, "frozen_in_matrix": frozen_in_matrix, "base_out": base_out, "factor_down": factor_down, "factor_up": factor_up}


adapter_scale = 2.0
rate_down = 25.0
rate_up = 0.75


def replica_step(inputs, frozen_in_matrix, base_out):
    tokens, targets, factor_a, second_factor = inputs
    projection_result = jnp.dot(tokens, factor_a.T, preferred_element_type=jnp.float32).astype(jnp.bfloat16)
    preact = (jnp.dot(tokens, frozen_in_matrix, preferred_element_type=jnp.float32)
              + adapter_scale * jnp.dot(projection_result, second_factor, preferred_element_type=jnp.float32)) * (MODEL_WIDTH ** -0.5)
    hidden = jnp.maximum(preact, 0.0).astype(jnp.bfloat16)
    output = jnp.dot(hidden, base_out, preferred_element_type=jnp.float32) * (FF ** -0.5)
    out_grad = ((output - targets.astype(jnp.float32)) / TOK_DEV).astype(jnp.bfloat16)
    hid_full = jnp.dot(out_grad, base_out.T, preferred_element_type=jnp.float32) * (FF ** -0.5)
    hidden_gradient = jnp.where(preact > 0, hid_full, 0.0).astype(jnp.bfloat16)
    up_gradient = (adapter_scale * MODEL_WIDTH ** -0.5) * jnp.dot(projection_result.T, hidden_gradient, preferred_element_type=jnp.float32)
    backward_parts = jnp.dot(hidden_gradient, second_factor.T, preferred_element_type=jnp.float32)
    down_gradient = (adapter_scale * MODEL_WIDTH ** -0.5) * jnp.dot(backward_parts.T, tokens.astype(jnp.float32), precision=lax.Precision.HIGHEST)
    new_a = factor_a.astype(jnp.float32) - rate_down * down_gradient
    new_b = second_factor.astype(jnp.float32) - rate_up * up_gradient
    return new_a, new_b


def reference(tokens, targets, frozen_in_matrix, base_out, factor_down, factor_up):
    tok_blocks = tokens.reshape(REPLICA_COUNT, TOK_DEV, MODEL_WIDTH)
    tgt_blocks = targets.reshape(REPLICA_COUNT, TOK_DEV, MODEL_WIDTH)
    new_down, new_up = lax.map(lambda inputs: replica_step(inputs, frozen_in_matrix, base_out),
                               (tok_blocks, tgt_blocks, factor_down, factor_up))
    down_transport = new_down.astype(jnp.bfloat16).reshape(REPLICA_COUNT * RANK, MODEL_WIDTH)
    up_transport = new_up.astype(jnp.bfloat16).reshape(REPLICA_COUNT * RANK, FF)
    merged = frozen_in_matrix.astype(jnp.float32) + (adapter_scale / REPLICA_COUNT) * jnp.dot(down_transport.T, up_transport, preferred_element_type=jnp.float32)
    return merged, new_down, new_up
```

```python
import jax
import jax.numpy as jnp
from jax import lax
from jax.experimental import pallas as pl
from jax.experimental.pallas import tpu as pltpu
from jax.sharding import Mesh
from jax.sharding import PartitionSpec as P

MODEL_WIDTH = 4096
FF = 8192
TOK = 128
RANK = 16
ROWS = 16
BLOCK = 128
REP = ("y", "l", "x")
Z = ("l", "h")
ADAPTER_SCALE = 2.0
RATE_DOWN = 25.0
RATE_UP = 0.75
BF16 = jnp.bfloat16
F32 = jnp.float32

RING = (0, -1, 1, 2)


def dot(a, b):
    return jnp.dot(a, b, preferred_element_type=F32)


def dot_nt(a, b):
    return lax.dot_general(a, b, (((1,), (1,)), ((), ())), preferred_element_type=F32)


def shift(value, axis, by):
    n = lax.axis_size(axis)
    return lax.ppermute(value, axis, [(i, (i + by) % n) for i in range(n)])


def partner(value, axis, mask=1):
    n = lax.axis_size(axis)
    return lax.ppermute(value, axis, [(i, i ^ mask) for i in range(n)])


def along_z(value, target):
    def place(z):
        return (z % 2) * 4 + z // 2

    return lax.ppermute(value, Z, [(place(z), place(target(z) % 8)) for z in range(8)])


def shift_z(value, by):
    return along_z(value, lambda z: z + by)


def other_replica(value):
    return along_z(value, lambda z: z + 1 if z % 2 else z - 1)


def ring_pieces(value, axis):
    half = value.shape[0] // 2
    below = shift(value, axis, 1)
    above = shift(value, axis, -1)
    far_low = shift(below[:half], axis, 1)
    far_high = shift(above[half:], axis, -1)
    return [value, below, above, far_low, far_high]


def gather_grid(value, first, second):
    line = jnp.concatenate(ring_pieces(value, first), axis=0)
    return ring_pieces(line, second)


def ring_direct(value, axis):
    return [value, shift(value, axis, 1), shift(value, axis, -1), shift(value, axis, 2)]


def arrange_kernel(rows_ref, cols_ref, own_ref, oth_ref, pown_ref, poth_ref, x_ref, p_ref):
    p_ref[...] = jnp.zeros_like(p_ref)
    for i in range(16):
        mine = (i // 2) % 2 == 0
        src, psrc = (own_ref, pown_ref) if mine else (oth_ref, poth_ref)
        row = pl.multiple_of(rows_ref[i] * ROWS, ROWS)
        lane = 0 if mine else RANK
        p_ref[pl.ds(i * ROWS, ROWS), lane : lane + RANK] = psrc[pl.ds(row, ROWS), :]
        for j in range(32):
            col = pl.multiple_of(cols_ref[j] * BLOCK, BLOCK)
            x_ref[pl.ds(i * ROWS, ROWS), j * BLOCK : (j + 1) * BLOCK] = src[
                pl.ds(row, ROWS), pl.ds(col, BLOCK)
            ]


def arrange(rows, cols, own, oth, pown, poth):
    smem = pl.BlockSpec(memory_space=pltpu.SMEM)
    vmem = pl.BlockSpec(memory_space=pltpu.VMEM)
    return pl.pallas_call(
        arrange_kernel,
        out_shape=(
            jax.ShapeDtypeStruct((2 * TOK, MODEL_WIDTH), BF16),
            jax.ShapeDtypeStruct((2 * TOK, 2 * RANK), BF16),
        ),
        in_specs=[smem, smem, vmem, vmem, vmem, vmem],
        out_specs=(vmem, vmem),
        name="arrange_tokens",
    )(rows, cols, own, oth, pown, poth)


def pick_cols_kernel(cols_ref, src_ref, out_ref):
    for j in range(32):
        col = pl.multiple_of(cols_ref[j] * BLOCK, BLOCK)
        out_ref[:, j * BLOCK : (j + 1) * BLOCK] = src_ref[:, pl.ds(col, BLOCK)]


def pick_cols(cols, src):
    vmem = pl.BlockSpec(memory_space=pltpu.VMEM)
    return pl.pallas_call(
        pick_cols_kernel,
        out_shape=jax.ShapeDtypeStruct(src.shape, src.dtype),
        in_specs=[pl.BlockSpec(memory_space=pltpu.SMEM), vmem],
        out_specs=vmem,
        name="pick_cols",
    )(cols, src)


def down_kernel(cols_ref, back_ref, x_ref, a_ref, new_ref, wire_ref, all_ref):
    grad = lax.dot_general(
        back_ref[...],
        x_ref[...].astype(F32),
        (((0,), (0,)), ((), ())),
        preferred_element_type=F32,
        precision=lax.Precision.HIGHEST,
    )
    scale = ADAPTER_SCALE * MODEL_WIDTH ** (-0.5)
    new = a_ref[...].astype(F32) - RATE_DOWN * (scale * grad)
    new_ref[...] = new
    all_ref[...] = new.astype(BF16)
    for j in range(32):
        col = pl.multiple_of(cols_ref[j] * BLOCK, BLOCK)
        wire_ref[j] = all_ref[:, pl.ds(col, BLOCK)]


def down_update(cols, back, x, a):
    smem = pl.BlockSpec(memory_space=pltpu.SMEM)
    vmem = pl.BlockSpec(memory_space=pltpu.VMEM)
    return pl.pallas_call(
        down_kernel,
        out_shape=(
            jax.ShapeDtypeStruct((RANK, MODEL_WIDTH), F32),
            jax.ShapeDtypeStruct((32, RANK, BLOCK), BF16),
        ),
        in_specs=[smem, vmem, vmem, vmem],
        out_specs=(vmem, vmem),
        scratch_shapes=[pltpu.VMEM((RANK, MODEL_WIDTH), BF16)],
        name="down_update",
    )(cols, back, x, a)


def reduce_z(part):
    n = part.shape[-1]
    half = n // 2
    arrived = partner(part[:, 1].astype(BF16), "c")
    mine = part[:, 0] + arrived.astype(F32)
    up = shift_z(mine[4, :, :half].astype(BF16), 1)
    down = shift_z(mine[4, :, half:].astype(BF16), -1)
    none = jnp.zeros((ROWS, half), F32)
    up = mine[3] + jnp.concatenate([up.astype(F32), none], axis=1)
    down = mine[5] + jnp.concatenate([none, down.astype(F32)], axis=1)
    for k in (2, 1, 0):
        up = shift_z(up.astype(BF16), 1).astype(F32)
        down = shift_z(down.astype(BF16), -1).astype(F32)
        if k:
            up = mine[k] + up
            down = mine[8 - k] + down
    return mine[0] + (up + down)


def gather_z(value):
    half = value.shape[1] // 2
    below, above = [value], [value]
    for _ in range(3):
        below.append(shift_z(below[-1], 1))
        above.append(shift_z(above[-1], -1))
    far = jnp.concatenate(
        [shift_z(below[-1][:, :half], 1), shift_z(above[-1][:, half:], -1)], axis=1
    )
    return jnp.stack(above[:4] + [far] + below[3:0:-1])


def shards(tokens, targets, w_in, w_out, factor_down, factor_up):
    y, l, x = (lax.axis_index(name) for name in REP)
    h, c = lax.axis_index("h"), lax.axis_index("c")
    z = 2 * h + l
    a = factor_down[0]
    b = factor_up[0]
    width = w_in.shape[1]
    hid = width // 2

    def halves(value):
        mine = lax.dynamic_slice_in_dim(value, l * hid, hid, value.ndim - 1)
        theirs = lax.dynamic_slice_in_dim(value, (1 - l) * hid, hid, value.ndim - 1)
        return mine, theirs

    in_own, in_send = halves(w_in)
    in_oth = partner(in_send, "l")
    out_own, out_send = halves(w_out.T)
    out_oth = partner(out_send, "l")
    b_own, b_send = halves(b)
    b_oth = partner(b_send, "l")
    tokens_oth = other_replica(tokens)
    projected = dot_nt(tokens, a).astype(BF16)
    projected_oth = other_replica(projected)

    in_a = gather_grid(in_own, "x", "y")
    in_b = gather_grid(in_oth, "y", "x")
    out_0 = jnp.where(l == 0, out_own, out_oth)
    out_1 = jnp.where(l == 0, out_oth, out_own)
    wo_a = gather_grid(out_0, "x", "y")
    wo_b = gather_grid(out_1, "y", "x")

    def column(dy, side, dx):
        return ((y + dy) % 4) * 8 + side * 4 + (x + dx) % 4

    x_cols = [column(dy, l, dx) for dy in RING for dx in RING]
    x_cols += [column(dy, 1 - l, dx) for dx in RING for dy in RING]
    t_near = [column(dy, 0, dx) for dy in RING[:3] for dx in RING]
    t_near += [column(dy, 1, dx) for dx in RING[:3] for dy in RING]
    t_far = [column(RING[3], 0, dx) for dx in RING] + [column(dy, 1, RING[3]) for dy in RING]
    rows = []
    for k in range(8):
        zk = (z + k) % 8
        for e in range(2):
            rows.append((zk // 2) * 2 + (c + e) % 2)

    def table(values):
        return jnp.stack([jnp.asarray(v, jnp.int32) for v in values])

    x_rel, p_rel = arrange(table(rows), table(x_cols), tokens, tokens_oth, projected, projected_oth)
    b_both = jnp.concatenate([b_own, b_oth], axis=0)

    preact = ADAPTER_SCALE * dot(p_rel, b_both)
    begin = 0
    for piece in in_a + in_b:
        preact = preact + dot(x_rel[:, begin : begin + piece.shape[0]], piece)
        begin += piece.shape[0]
    preact = preact * MODEL_WIDTH ** (-0.5)
    hidden = jnp.maximum(preact, 0.0).astype(BF16)

    near = wo_a[:3] + wo_b[:3]
    far = wo_a[3:] + wo_b[3:]
    my_row = (h * 2 + c) * ROWS
    my_targets = lax.dynamic_slice_in_dim(targets, my_row, ROWS, 0)
    my_targets = pick_cols(table(t_near + t_far), my_targets)
    shares = []
    for group in (near, far):
        part = jnp.concatenate([dot_nt(hidden, piece) for piece in group], axis=1)
        shares.append(reduce_z(part.reshape(8, 2, ROWS, part.shape[1])))
    share = jnp.concatenate(shares, axis=1) * FF ** (-0.5)
    grad_rows = ((share - my_targets.astype(F32)) / TOK).astype(BF16)
    grad_core = gather_z(grad_rows)
    grad_far = partner(grad_core, "c")
    out_grad = jnp.stack([grad_core, grad_far], axis=1).reshape(2 * TOK, MODEL_WIDTH)

    hid_grad = None
    begin = 0
    for piece in near + far:
        term = dot(out_grad[:, begin : begin + piece.shape[0]], piece)
        hid_grad = term if hid_grad is None else hid_grad + term
        begin += piece.shape[0]
    hid_grad = jnp.where(preact > 0, hid_grad * FF ** (-0.5), 0.0).astype(BF16)

    by_replica = hid_grad.reshape(4, 2, 2 * ROWS, hid)
    grad_own = by_replica[:, 0].reshape(TOK, hid)
    grad_oth = by_replica[:, 1].reshape(TOK, hid)
    p_split = p_rel.reshape(4, 2, 2 * ROWS, 2 * RANK)
    p_own = p_split[:, 0, :, :RANK].reshape(TOK, RANK)
    p_oth = p_split[:, 1, :, RANK:].reshape(TOK, RANK)
    scale = ADAPTER_SCALE * MODEL_WIDTH ** (-0.5)

    def up_update(p, grad, factor):
        g = lax.dot_general(p, grad, (((0,), (0,)), ((), ())), preferred_element_type=F32)
        return factor.astype(F32) - RATE_UP * (scale * g)

    up_own = up_update(p_own, grad_own, b_own)
    up_oth = up_update(p_oth, grad_oth, b_oth)
    back_own = dot_nt(grad_own, b_own)
    back_oth = dot_nt(grad_oth, b_oth)

    def in_order(back, start):
        back = back.reshape(4, 2, ROWS * RANK)
        back = jnp.where(c == 0, back, back[:, ::-1])
        twice = jnp.concatenate([back, back], axis=0)
        return lax.dynamic_slice_in_dim(twice, (4 - start) % 4, 4, 0).reshape(TOK, RANK)

    back_mine = in_order(back_own, h)
    back_theirs = in_order(back_oth, (h + l) % 4)
    back = back_mine + partner(back_theirs, "l")
    back = back + partner(back, "c")
    back = (back + partner(back, "h", 1)) + (partner(back, "h", 2) + partner(back, "h", 3))

    d_cols = [
        ((y + dy) % 4) * 8 + ((l + dl) % 2) * 4 + (x + dx) % 4
        for dx in range(4)
        for dy in range(4)
        for dl in range(2)
    ]
    new_a, wire = down_update(table(d_cols), back, tokens, a)
    wire = wire.reshape(4, 4, 2, RANK, BLOCK)
    wire = jnp.stack([wire[0]] + [shift(wire[s], "x", s) for s in (1, 2, 3)])
    wire = jnp.stack([wire[:, 0]] + [shift(wire[:, s], "y", s) for s in (1, 2, 3)])
    wire = jnp.stack([wire[:, :, 0], partner(wire[:, :, 1], "l")])
    back_order = [0, 1, 3, 2]
    downs = jnp.stack([jnp.stack([wire[:, sy, sx] for sx in back_order]) for sy in back_order])
    downs = downs.reshape(32 * RANK, BLOCK)

    mine = jnp.stack([up_own, up_oth])
    theirs = partner(jnp.stack([up_oth, up_own]), "l")
    low = jnp.where(l == 0, mine, theirs)
    high = jnp.where(l == 0, theirs, mine)
    new_ups = jnp.concatenate([low, high], axis=2)
    new_b = new_ups[0]
    up_wire = new_ups.astype(BF16).reshape(2 * RANK, width)
    left, right = up_wire[:, :hid], up_wire[:, hid:]
    left = jnp.stack(ring_direct(left, "x"))
    left = jnp.stack(ring_direct(left, "y"))
    right = jnp.stack(ring_direct(right, "y"))
    right = jnp.stack(ring_direct(right, "x"))
    right = jnp.swapaxes(right, 0, 1)
    delta = [
        lax.dot_general(
            downs,
            side.reshape(32 * RANK, hid),
            (((0,), (0,)), ((), ())),
            preferred_element_type=F32,
        )
        for side in (left, right)
    ]
    merged = w_in.astype(F32) + ADAPTER_SCALE / 32 * jnp.concatenate(delta, axis=1)
    return merged, new_a[None], new_b[None]


def solution(mesh):
    split = Mesh(mesh.devices.reshape(4, 2, 4, 4, 2), ("y", "l", "x", "h", "c"))
    tp = ("h", "c")
    in_specs = (
        P(REP, None),
        P(REP, None),
        P(REP, tp),
        P(tp, REP),
        P(REP, None, None),
        P(REP, None, tp),
    )
    out_specs = (P(REP, tp), P(REP, None, None), P(REP, None, tp))
    return jax.shard_map(
        shards, mesh=split, in_specs=in_specs, out_specs=out_specs, check_vma=False
    )
```

```python
import jax
import jax.numpy as jnp
from jax import lax
from jax.experimental import pallas as pl
from jax.experimental.pallas import tpu as pltpu
from jax.sharding import Mesh
from jax.sharding import PartitionSpec as P

MODEL_WIDTH = 4096
FF = 8192
TOK = 128
RANK = 16
ROWS = 16
BLOCK = 128
HID = 512
SIDE = MODEL_WIDTH // 2
REP = ("y", "l", "x")
Z = ("l", "h")
ADAPTER_SCALE = 2.0
RATE_DOWN = 25.0
RATE_UP = 0.75
BF16 = jnp.bfloat16
F32 = jnp.float32

RING = (0, -1, 1, 2)


def dot(a, b):
    return jnp.dot(a, b, preferred_element_type=F32)


def dot_nt(a, b):
    return lax.dot_general(a, b, (((1,), (1,)), ((), ())), preferred_element_type=F32)


def dot_tn(a, b):
    return lax.dot_general(a, b, (((0,), (0,)), ((), ())), preferred_element_type=F32)


def shift(value, axis, by):
    n = lax.axis_size(axis)
    return lax.ppermute(value, axis, [(i, (i + by) % n) for i in range(n)])


def partner(value, axis):
    return lax.ppermute(value, axis, [(0, 1), (1, 0)])


def near_z(value):
    def place(z):
        return (z % 2) * 4 + (z % 8) // 2

    return lax.ppermute(
        value, Z, [(place(z), place(z + 1 if z % 2 else z - 1)) for z in range(8)]
    )


def call(kernel, out_shape, *args, scratch=(), name):
    vmem = pl.BlockSpec(memory_space=pltpu.VMEM)
    many = isinstance(out_shape, tuple)
    return pl.pallas_call(
        kernel,
        out_shape=out_shape,
        in_specs=[vmem] * len(args),
        out_specs=(vmem,) * len(out_shape) if many else vmem,
        scratch_shapes=scratch,
        name=name,
    )(*args)


def shape(*dims, dtype=BF16):
    return jax.ShapeDtypeStruct(dims, dtype)


def lanes(start, size):
    return pl.ds(pl.multiple_of(start, BLOCK), size)


def token_row(i):
    h, c = lax.axis_index("h"), lax.axis_index("c")
    j, e = (i // 2) % 4, i % 2
    return pl.multiple_of((((h + j) % 4) * 2 + (c + e) % 2) * ROWS, ROWS)


def column(dy, side, dx):
    y, x = lax.axis_index("y"), lax.axis_index("x")
    return (((y + dy) % 4) * 8 + side * 4 + (x + dx) % 4) * BLOCK


def split_kernel(w_in_ref, w_out_ref, own_ref, send_ref):
    l = lax.axis_index("l")
    for ref, side in ((own_ref, l), (send_ref, 1 - l)):
        ref[:TOK] = w_in_ref[:, lanes(side * HID, HID)]
        ref[TOK:] = w_out_ref[lanes(side * HID, HID), :].T


def arrange_kernel(own_ref, oth_ref, pown_ref, poth_ref, x_ref, p_ref):
    l = lax.axis_index("l")
    cols = [column(dy, l, dx) for dy in RING for dx in RING]
    cols += [column(dy, 1 - l, dx) for dx in RING for dy in RING]
    p_ref[...] = jnp.zeros_like(p_ref)
    for i in range(16):
        src, psrc = (own_ref, pown_ref) if i < 8 else (oth_ref, poth_ref)
        row = token_row(i)
        lane = 0 if i < 8 else RANK
        p_ref[i * ROWS : (i + 1) * ROWS, lane : lane + RANK] = psrc[pl.ds(row, ROWS), :]
        for j in range(32):
            x_ref[i * ROWS : (i + 1) * ROWS, j * BLOCK : (j + 1) * BLOCK] = src[
                pl.ds(row, ROWS), lanes(cols[j], BLOCK)
            ]


def hidden_kernel(x_ref, p_ref, b_ref, *refs):
    pieces, (hidden_ref, mask_ref) = refs[:8], refs[8:]
    total = ADAPTER_SCALE * dot(p_ref[...], b_ref[...])
    for k, piece in enumerate(pieces):
        total = total + dot(x_ref[:, k * HID : (k + 1) * HID], piece[...])
    preact = total * MODEL_WIDTH ** (-0.5)
    hidden_ref[...] = jnp.maximum(preact, 0.0).astype(BF16)
    mask_ref[...] = jnp.where(preact > 0, 1.0, 0.0).astype(BF16)


def output_kernel(hidden_ref, *refs):
    pieces, (keep_ref, send_ref) = refs[:8], refs[8:]
    l = lax.axis_index("l")
    for k, piece in enumerate(pieces):
        part = dot_nt(hidden_ref[...], piece[...]).reshape(8, 2, ROWS, HID)
        if k < 4:
            places = [(l * SIDE + k * HID, 0, HID)]
        else:
            places = [
                ((1 - l) * SIDE + (j * 4 + k - 4) * BLOCK, j * BLOCK, BLOCK) for j in range(4)
            ]
        for to, begin, size in places:
            keep_ref[:, :, lanes(to, size)] = part[:, 0, :, begin : begin + size]
            send_ref[:, :, lanes(to, size)] = part[:, 1, :, begin : begin + size].astype(BF16)


def finish_kernel(mine_ref, r1_ref, r2_ref, r3_ref, targets_ref, out_ref):
    h, c = lax.axis_index("h"), lax.axis_index("c")
    row = pl.multiple_of((h * 2 + c) * ROWS, ROWS)
    j = 0
    for side in range(2):
        for dy in RING:
            for dx in RING:
                here = slice(j * BLOCK, (j + 1) * BLOCK)
                total = mine_ref[:, here]
                for ref in (r1_ref, r2_ref, r3_ref):
                    total = total + ref[:, here].astype(F32)
                target = targets_ref[pl.ds(row, ROWS), lanes(column(dy, side, dx), BLOCK)]
                grad = (total * FF ** (-0.5) - target.astype(F32)) / TOK
                out_ref[:, here] = grad.astype(BF16)
                j += 1


def backward_kernel(q_ref, qc_ref, left_ref, leftc_ref, right_ref, rightc_ref, mask_ref, p_own_ref,
                    p_oth_ref, b_ref, *refs):
    pieces, (up_own_ref, up_oth_ref, wire_ref, back_ref, grad_ref, own_ref, oth_ref) = refs[:8], refs[8:]
    l = lax.axis_index("l")
    for i in range(16):
        j, e = (i // 2) % 4, i % 2
        here = slice(i * ROWS, (i + 1) * ROWS)
        if i < 8:
            grad_ref[here, :] = (q_ref, qc_ref)[e][j]
        else:
            turned = (j + 1 + 2 * l) % 4
            grad_ref[here, :SIDE] = (left_ref, leftc_ref)[e][j]
            grad_ref[here, SIDE:] = (right_ref, rightc_ref)[e][turned]
    total = None
    for k, piece in enumerate(pieces):
        if k < 4:
            part = grad_ref[:, lanes(l * SIDE + k * HID, HID)]
        else:
            part = jnp.concatenate(
                [
                    grad_ref[:, lanes((1 - l) * SIDE + (j * 4 + k - 4) * BLOCK, BLOCK)]
                    for j in range(4)
                ],
                axis=1,
            )
        term = dot(part, piece[...])
        total = term if total is None else total + term
    total = jnp.where(mask_ref[...].astype(F32) > 0, total * FF ** (-0.5), 0.0).astype(BF16)
    for i in range(16):
        ref = own_ref if i < 8 else oth_ref
        ref[pl.ds(token_row(i), ROWS), :] = total[i * ROWS : (i + 1) * ROWS]
    scale = ADAPTER_SCALE * MODEL_WIDTH ** (-0.5)
    sides = (
        (l, own_ref, p_own_ref, up_own_ref, b_ref[:RANK]),
        (1 - l, oth_ref, p_oth_ref, up_oth_ref, b_ref[RANK:]),
    )
    for side, hid_ref, p_ref, up_ref, b in sides:
        up = b.astype(F32) - RATE_UP * (scale * dot(p_ref[...], hid_ref[...]))
        up_ref[...] = up
        wire_ref[side] = up.astype(BF16)
        back = dot_nt(b, hid_ref[...])
        for k in range(8):
            back_ref[side * 8 + k] = back


def down_kernel(back_ref, x_ref, a_ref, new_ref, wire_ref):
    terms = [back_ref[k] for k in range(16)]
    while len(terms) > 1:
        terms = [terms[k] + terms[k + 1] for k in range(0, len(terms), 2)]
    rest = terms[0]
    parts = []
    for _ in range(3):
        parts.append(rest.astype(BF16))
        rest = rest - parts[-1].astype(F32)
    stacked = jnp.concatenate(parts, axis=0)
    scale = ADAPTER_SCALE * MODEL_WIDTH ** (-0.5)
    for k in range(8):
        here = slice(k * HID, (k + 1) * HID)
        grad = dot(stacked, x_ref[:, here])
        grad = grad[:RANK] + grad[RANK : 2 * RANK] + grad[2 * RANK :]
        new = a_ref[:, here].astype(F32) - RATE_DOWN * (scale * grad)
        new_ref[:, here] = new
        for j in range(4):
            wire_ref[k * 4 + j] = new[:, j * BLOCK : (j + 1) * BLOCK].astype(BF16)


def merge_kernel(down_ref, up_ref, w_ref, out_ref, d_ref, u_ref):
    for y in range(4):
        for x in range(4):
            for l in range(2):
                at = ((y * 4 + x) * 2 + l) * RANK
                d_ref[at : at + RANK, :] = down_ref[y * 8 + l * 4 + x]
    for side in range(2):
        for y in range(4):
            for x in range(4):
                for l in range(2):
                    at = ((y * 4 + x) * 2 + l) * RANK
                    u_ref[at : at + RANK, :] = up_ref[y * 8 + side * 4 + x, l]
        here = slice(side * HID, (side + 1) * HID)
        delta = dot_tn(d_ref[...], u_ref[...])
        out_ref[:, here] = w_ref[:, here].astype(F32) + ADAPTER_SCALE / 32 * delta


def ring(value, axis, upward):
    below = shift(value, axis, 1)
    above = shift(value, axis, -1)
    far = shift(below, axis, 1) if upward else shift(above, axis, -1)
    return [value, below, above, far]


def ring_direct(value, axis):
    return [value, shift(value, axis, 1), shift(value, axis, -1), shift(value, axis, 2)]


def shards(tokens, targets, w_in, w_out, factor_down, factor_up):
    l = lax.axis_index("l")
    a = factor_down[0]
    b = factor_up[0]

    w_own, w_send = call(
        split_kernel, (shape(2 * TOK, HID), shape(2 * TOK, HID)), w_in, w_out, name="split"
    )
    line_own = ring_direct(w_own, "x")
    w_oth = partner(w_send, "l")
    line_oth = ring_direct(w_oth, "y")

    projected = dot_nt(tokens, a).astype(BF16)
    p_own = projected.T
    b_own = jnp.where(l == 0, b[:, :HID], b[:, HID:])
    b_send = jnp.where(l == 0, b[:, HID:], b[:, :HID])
    arrived = partner(jnp.concatenate([b_send, p_own], axis=1), "l")
    b_oth, p_oth = arrived[:, :HID], arrived[:, HID:]
    b_both = jnp.concatenate([b_own, b_oth], axis=0)
    tokens_oth = near_z(tokens)

    def joined(line, begin):
        return jnp.concatenate([block[begin : begin + TOK] for block in line], axis=0)

    in_pieces = ring(joined(line_own, 0), "y", True) + ring(joined(line_oth, 0), "x", True)
    out_pieces = ring(joined(line_own, TOK), "y", False) + ring(joined(line_oth, TOK), "x", False)

    x_rel, p_rel = call(
        arrange_kernel,
        (shape(2 * TOK, MODEL_WIDTH), shape(2 * TOK, 2 * RANK)),
        tokens, tokens_oth, projected, p_oth.T,
        name="arrange",
    )
    hidden, mask = call(
        hidden_kernel,
        (shape(2 * TOK, HID), shape(2 * TOK, HID)),
        x_rel, p_rel, b_both, *in_pieces,
        name="hidden",
    )
    keep, send = call(
        output_kernel,
        (shape(8, ROWS, MODEL_WIDTH, dtype=F32), shape(8, ROWS, MODEL_WIDTH)),
        hidden, *out_pieces,
        name="output",
    )

    summed = keep + partner(send, "c").astype(F32)
    away = summed[4:].astype(BF16)
    left = partner(away[:, :, :SIDE], "l")
    right = away[:, :, SIDE:]
    right = near_z(jnp.where(l == 0, jnp.roll(right, 1, 0), jnp.roll(right, -1, 0)))
    summed = summed[:4] + jnp.concatenate([left, right], axis=2).astype(F32)
    steps = [shift(summed[j].astype(BF16), "h", j) for j in (1, 2, 3)]
    grad_rows = call(
        finish_kernel, shape(ROWS, MODEL_WIDTH), summed[0], *steps, targets, name="finish"
    )

    q = jnp.stack([grad_rows] + [shift(grad_rows, "h", -j) for j in (1, 2, 3)])
    left = partner(q[:, :, :SIDE], "l")
    right = near_z(q[:, :, SIDE:])
    q_far, left_far, right_far = partner(q, "c"), partner(left, "c"), partner(right, "c")

    up_own, up_oth, up_wire, back = call(
        backward_kernel,
        (
            shape(RANK, HID, dtype=F32),
            shape(RANK, HID, dtype=F32),
            shape(2, RANK, HID),
            shape(16, RANK, TOK, dtype=F32),
        ),
        q, q_far, left, left_far, right, right_far, mask, p_own, p_oth, b_both, *out_pieces,
        scratch=[
            pltpu.VMEM((2 * TOK, MODEL_WIDTH), BF16),
            pltpu.VMEM((TOK, HID), BF16),
            pltpu.VMEM((TOK, HID), BF16),
        ],
        name="backward",
    )
    ups = lax.all_gather(up_wire, REP, axis=0)
    back = lax.all_to_all(back, ("l", "h", "c"), 0, 0, tiled=True)
    new_a, wire = call(
        down_kernel,
        (shape(RANK, MODEL_WIDTH, dtype=F32), shape(32, RANK, BLOCK)),
        back, tokens, a,
        name="down",
    )
    downs = lax.all_to_all(wire, REP, 0, 0, tiled=True)
    up_arrived = partner(up_oth, "l")
    new_b = jnp.where(
        l == 0,
        jnp.concatenate([up_own, up_arrived], axis=1),
        jnp.concatenate([up_arrived, up_own], axis=1),
    )
    merged = call(
        merge_kernel,
        shape(TOK, 2 * HID, dtype=F32),
        downs, ups, w_in,
        scratch=[pltpu.VMEM((32 * RANK, BLOCK), BF16), pltpu.VMEM((32 * RANK, HID), BF16)],
        name="merge",
    )
    return merged, new_a[None], new_b[None]


def solution(mesh):
    split = Mesh(mesh.devices.reshape(4, 2, 4, 4, 2), ("y", "l", "x", "h", "c"))
    tp = ("h", "c")
    in_specs = (
        P(REP, None),
        P(REP, None),
        P(REP, tp),
        P(tp, REP),
        P(REP, None, None),
        P(REP, None, tp),
    )
    out_specs = (P(REP, tp), P(REP, None, None), P(REP, None, tp))
    return jax.shard_map(
        shards, mesh=split, in_specs=in_specs, out_specs=out_specs, check_vma=False
    )
```

```python
import jax
import jax.numpy as jnp
from jax import lax
from jax.experimental import pallas as pl
from jax.experimental.pallas import tpu as pltpu
from jax.sharding import Mesh
from jax.sharding import PartitionSpec as P

MODEL_WIDTH = 4096
FF = 8192
TOK = 128
RANK = 16
ROWS = 16
BLOCK = 128
HID = 512
SIDE = MODEL_WIDTH // 2
REP = ("y", "l", "x")
Z = ("l", "h")
ADAPTER_SCALE = 2.0
RATE_DOWN = 25.0
RATE_UP = 0.75
BF16 = jnp.bfloat16
F32 = jnp.float32

RING = (0, -1, 1, 2)


def dot(a, b):
    return jnp.dot(a, b, preferred_element_type=F32)


def dot_nt(a, b):
    return lax.dot_general(a, b, (((1,), (1,)), ((), ())), preferred_element_type=F32)


def dot_tn(a, b):
    return lax.dot_general(a, b, (((0,), (0,)), ((), ())), preferred_element_type=F32)


def shift(value, axis, by):
    n = lax.axis_size(axis)
    return lax.ppermute(value, axis, [(i, (i + by) % n) for i in range(n)])


def partner(value, axis):
    return lax.ppermute(value, axis, [(0, 1), (1, 0)])


def near_z(value):
    def place(z):
        return (z % 2) * 4 + (z % 8) // 2

    return lax.ppermute(
        value, Z, [(place(z), place(z + 1 if z % 2 else z - 1)) for z in range(8)]
    )


def call(kernel, out_shape, *args, scratch=(), name):
    vmem = pl.BlockSpec(memory_space=pltpu.VMEM)
    many = isinstance(out_shape, tuple)
    return pl.pallas_call(
        kernel,
        out_shape=out_shape,
        in_specs=[vmem] * len(args),
        out_specs=(vmem,) * len(out_shape) if many else vmem,
        scratch_shapes=scratch,
        name=name,
    )(*args)


def shape(*dims, dtype=BF16):
    return jax.ShapeDtypeStruct(dims, dtype)


def lanes(start, size):
    return pl.ds(pl.multiple_of(start, BLOCK), size)


def token_row(i):
    h, c = lax.axis_index("h"), lax.axis_index("c")
    j, e = (i // 2) % 4, i % 2
    return pl.multiple_of((((h + j) % 4) * 2 + (c + e) % 2) * ROWS, ROWS)


def column(dy, side, dx):
    y, x = lax.axis_index("y"), lax.axis_index("x")
    return (((y + dy) % 4) * 8 + side * 4 + (x + dx) % 4) * BLOCK


def send_kernel(w_in_ref, w_out_ref, b_ref, send_ref):
    other = (1 - lax.axis_index("l")) * HID
    send_ref[:TOK] = w_in_ref[:, lanes(other, HID)]
    send_ref[TOK : 2 * TOK] = w_out_ref[lanes(other, HID), :].T
    send_ref[2 * TOK :] = b_ref[:, lanes(other, HID)]


def own_kernel(w_in_ref, w_out_ref, b_ref, send_ref, in_ref, out_ref, b_own_ref):
    mine = lax.axis_index("l") * HID
    in_ref[...] = w_in_ref[:, lanes(mine, HID)]
    out_ref[...] = w_out_ref[lanes(mine, HID), :].T
    b_own_ref[...] = b_ref[:, lanes(mine, HID)]


def pack_kernel(tokens_ref, a_ref, out_ref):
    out_ref[:TOK] = tokens_ref[...]
    out_ref[TOK:, :TOK] = dot_nt(a_ref[...], tokens_ref[...]).astype(BF16)


def arrange_kernel(own_ref, oth_ref, x_ref, p_ref, turned_ref):
    l = lax.axis_index("l")
    for k, ref in enumerate((own_ref, oth_ref)):
        turned_ref[k] = ref[TOK:, :TOK].astype(F32).T.astype(BF16)
    cols = [column(dy, l, dx) for dy in RING for dx in RING]
    cols += [column(dy, 1 - l, dx) for dx in RING for dy in RING]
    p_ref[...] = jnp.zeros_like(p_ref)
    for i in range(16):
        src = own_ref if i < 8 else oth_ref
        row = token_row(i)
        lane = 0 if i < 8 else RANK
        p_ref[i * ROWS : (i + 1) * ROWS, lane : lane + RANK] = turned_ref[
            i // 8, pl.ds(row, ROWS), :
        ]
        for j in range(32):
            x_ref[i * ROWS : (i + 1) * ROWS, j * BLOCK : (j + 1) * BLOCK] = src[
                pl.ds(row, ROWS), lanes(cols[j], BLOCK)
            ]


def near_kernel(x_ref, p_ref, b_own_ref, b_oth_ref, *refs):
    pieces, total_ref = refs[:6], refs[6]
    b = jnp.concatenate([b_own_ref[...], b_oth_ref[...]], axis=0)
    total = ADAPTER_SCALE * dot(p_ref[...], b)
    for k, piece in zip((0, 1, 2, 4, 5, 6), pieces):
        total = total + dot(x_ref[:, k * HID : (k + 1) * HID], piece[...])
    total_ref[...] = total


def hidden_kernel(x_ref, total_ref, own_ref, oth_ref, hidden_ref, mask_ref):
    total = total_ref[...]
    for k, piece in ((3, own_ref), (7, oth_ref)):
        total = total + dot(x_ref[:, k * HID : (k + 1) * HID], piece[...])
    preact = total * MODEL_WIDTH ** (-0.5)
    hidden_ref[...] = jnp.maximum(preact, 0.0).astype(BF16)
    mask_ref[...] = jnp.where(preact > 0, 1.0, 0.0).astype(BF16)


def output_kernel(hidden_ref, *refs):
    pieces, (keep_ref, send_ref) = refs[:8], refs[8:]
    l = lax.axis_index("l")
    for k, piece in enumerate(pieces):
        part = dot_nt(hidden_ref[...], piece[...]).reshape(8, 2, ROWS, HID)
        if k < 4:
            places = [(l * SIDE + (j * 4 + k) * BLOCK, j * BLOCK, BLOCK) for j in range(4)]
        else:
            places = [((1 - l) * SIDE + (k - 4) * HID, 0, HID)]
        for to, begin, size in places:
            keep_ref[:, :, lanes(to, size)] = part[:, 0, :, begin : begin + size]
            send_ref[:, :, lanes(to, size)] = part[:, 1, :, begin : begin + size].astype(BF16)


def finish_kernel(mine_ref, r1_ref, r2_ref, r3_ref, targets_ref, out_ref):
    h, c = lax.axis_index("h"), lax.axis_index("c")
    row = pl.multiple_of((h * 2 + c) * ROWS, ROWS)
    j = 0
    for side in range(2):
        for dy in RING:
            for dx in RING:
                here = slice(j * BLOCK, (j + 1) * BLOCK)
                total = mine_ref[:, here]
                for ref in (r1_ref, r2_ref, r3_ref):
                    total = total + ref[:, here].astype(F32)
                target = targets_ref[pl.ds(row, ROWS), lanes(column(dy, side, dx), BLOCK)]
                grad = (total * FF ** (-0.5) - target.astype(F32)) / TOK
                out_ref[:, here] = grad.astype(BF16)
                j += 1


def backward_kernel(q_ref, qc_ref, left_ref, leftc_ref, right_ref, rightc_ref, mask_ref, own_pack_ref,
                    oth_pack_ref, b_own_ref, b_oth_ref, *refs):
    pieces, (up_own_ref, up_oth_ref, wire_ref, back_ref, grad_ref, own_ref, oth_ref) = refs[:8], refs[8:]
    l = lax.axis_index("l")
    for i in range(16):
        j, e = (i // 2) % 4, i % 2
        here = slice(i * ROWS, (i + 1) * ROWS)
        if i < 8:
            grad_ref[here, :] = (q_ref, qc_ref)[e][j]
        else:
            turned = (j + 1 + 2 * l) % 4
            grad_ref[here, :SIDE] = (left_ref, leftc_ref)[e][j]
            grad_ref[here, SIDE:] = (right_ref, rightc_ref)[e][turned]
    total = None
    for k, piece in enumerate(pieces):
        if k < 4:
            part = jnp.concatenate(
                [grad_ref[:, lanes(l * SIDE + (j * 4 + k) * BLOCK, BLOCK)] for j in range(4)],
                axis=1,
            )
        else:
            part = grad_ref[:, lanes((1 - l) * SIDE + (k - 4) * HID, HID)]
        term = dot(part, piece[...])
        total = term if total is None else total + term
    total = jnp.where(mask_ref[...].astype(F32) > 0, total * FF ** (-0.5), 0.0).astype(BF16)
    for i in range(16):
        ref = own_ref if i < 8 else oth_ref
        ref[pl.ds(token_row(i), ROWS), :] = total[i * ROWS : (i + 1) * ROWS]
    scale = ADAPTER_SCALE * MODEL_WIDTH ** (-0.5)
    sides = (
        (l, own_ref, own_pack_ref, up_own_ref, b_own_ref[...]),
        (1 - l, oth_ref, oth_pack_ref, up_oth_ref, b_oth_ref[...]),
    )
    for side, hid_ref, p_ref, up_ref, b in sides:
        up = b.astype(F32) - RATE_UP * (scale * dot(p_ref[...], hid_ref[...]))
        up_ref[...] = up
        wire_ref[side] = up.astype(BF16)
        back = dot_nt(b, hid_ref[...])
        for k in range(8):
            back_ref[side * 8 + k] = back


def down_kernel(back_ref, x_ref, a_ref, up_ref, new_ref, wire_ref):
    terms = [back_ref[k] for k in range(16)]
    while len(terms) > 1:
        terms = [terms[k] + terms[k + 1] for k in range(0, len(terms), 2)]
    rest = terms[0]
    parts = []
    for _ in range(3):
        parts.append(rest.astype(BF16))
        rest = rest - parts[-1].astype(F32)
    stacked = jnp.concatenate(parts, axis=0)
    scale = ADAPTER_SCALE * MODEL_WIDTH ** (-0.5)
    for k in range(8):
        here = slice(k * HID, (k + 1) * HID)
        grad = dot(stacked, x_ref[:, here])
        grad = grad[:RANK] + grad[RANK : 2 * RANK] + grad[2 * RANK :]
        new = a_ref[:, here].astype(F32) - RATE_DOWN * (scale * grad)
        new_ref[:, here] = new
        for j in range(4):
            wire_ref[k * 4 + j, :, :BLOCK] = new[:, j * BLOCK : (j + 1) * BLOCK].astype(BF16)
            for l in range(2):
                begin = BLOCK + l * HID
                wire_ref[k * 4 + j, :, begin : begin + HID] = up_ref[l]


def merge_kernel(wire_ref, w_ref, out_ref, d_ref, u_ref):
    for y in range(4):
        for x in range(4):
            for l in range(2):
                at = ((y * 4 + x) * 2 + l) * RANK
                d_ref[at : at + RANK, :] = wire_ref[y * 8 + l * 4 + x, :, :BLOCK]
    for side in range(2):
        for y in range(4):
            for x in range(4):
                for l in range(2):
                    at = ((y * 4 + x) * 2 + l) * RANK
                    begin = BLOCK + l * HID
                    u_ref[at : at + RANK, :] = wire_ref[
                        y * 8 + side * 4 + x, :, begin : begin + HID
                    ]
        here = slice(side * HID, (side + 1) * HID)
        delta = dot_tn(d_ref[...], u_ref[...])
        out_ref[:, here] = w_ref[:, here].astype(F32) + ADAPTER_SCALE / 32 * delta


def ring(value, axis):
    below, above = shift(value, axis, 1), shift(value, axis, -1)
    return [value, below, above, shift(below, axis, 1)]


def ring_direct(value, axis):
    return [value, shift(value, axis, 1), shift(value, axis, -1), shift(value, axis, 2)]


def shards(tokens, targets, w_in, w_out, factor_down, factor_up):
    l = lax.axis_index("l")
    a = factor_down[0]
    b = factor_up[0]

    w_send = call(send_kernel, shape(2 * TOK + RANK, HID), w_in, w_out, b, name="send")
    w_oth = partner(w_send, "l")
    in_own, out_own, b_own = call(
        own_kernel,
        (shape(TOK, HID), shape(TOK, HID), shape(RANK, HID)),
        w_in, w_out, b, w_send,
        name="own",
    )
    b_oth = w_oth[2 * TOK :]
    packed = call(pack_kernel, shape(TOK + RANK, MODEL_WIDTH), tokens, a, name="pack")
    packed_oth = near_z(packed)
    in_own = jnp.concatenate(ring(in_own, "x"), axis=0)
    out_own = jnp.concatenate(ring(out_own, "y"), axis=0)
    in_oth = jnp.concatenate(ring_direct(w_oth[:TOK], "y"), axis=0)
    out_oth = jnp.concatenate(ring_direct(w_oth[TOK : 2 * TOK], "x"), axis=0)

    x_rel, p_rel = call(
        arrange_kernel,
        (shape(2 * TOK, MODEL_WIDTH), shape(2 * TOK, 2 * RANK)),
        packed, packed_oth,
        scratch=[pltpu.VMEM((2, TOK, RANK), BF16)],
        name="arrange",
    )

    in_a = [in_own, shift(in_own, "y", 1), shift(in_own, "y", -1)]
    in_b = [in_oth, shift(in_oth, "x", 1), shift(in_oth, "x", -1)]
    out_a = [out_own, shift(out_own, "x", 1), shift(out_own, "x", -1)]
    out_b = [out_oth, shift(out_oth, "y", 1), shift(out_oth, "y", -1)]
    in_a_far = shift(in_a[1], "y", 1)
    in_b_far = shift(in_b[1], "x", 1)
    out_a_far = shift(out_a[2], "x", -1)
    out_b_far = shift(out_b[2], "y", -1)
    out_pieces = out_a + [out_a_far] + out_b + [out_b_far]

    total = call(
        near_kernel,
        shape(2 * TOK, HID, dtype=F32),
        x_rel, p_rel, b_own, b_oth, *in_a, *in_b,
        name="near",
    )
    hidden, mask = call(
        hidden_kernel,
        (shape(2 * TOK, HID), shape(2 * TOK, HID)),
        x_rel, total, in_a_far, in_b_far,
        name="hidden",
    )
    keep, send = call(
        output_kernel,
        (shape(8, ROWS, MODEL_WIDTH, dtype=F32), shape(8, ROWS, MODEL_WIDTH)),
        hidden, *out_pieces,
        name="output",
    )

    summed = keep + partner(send, "c").astype(F32)
    away = summed[4:].astype(BF16)
    left = partner(away[:, :, :SIDE], "l")
    right = away[:, :, SIDE:]
    right = near_z(jnp.where(l == 0, jnp.roll(right, 1, 0), jnp.roll(right, -1, 0)))
    summed = summed[:4] + jnp.concatenate([left, right], axis=2).astype(F32)
    steps = [shift(summed[j].astype(BF16), "h", j) for j in (1, 2, 3)]
    grad_rows = call(
        finish_kernel, shape(ROWS, MODEL_WIDTH), summed[0], *steps, targets, name="finish"
    )

    q = jnp.stack([grad_rows] + [shift(grad_rows, "h", -j) for j in (1, 2, 3)])
    left = partner(q[:, :, :SIDE], "l")
    right = near_z(q[:, :, SIDE:])
    q_far, left_far, right_far = partner(q, "c"), partner(left, "c"), partner(right, "c")

    up_own, up_oth, up_wire, back = call(
        backward_kernel,
        (
            shape(RANK, HID, dtype=F32),
            shape(RANK, HID, dtype=F32),
            shape(2, RANK, HID),
            shape(16, RANK, TOK, dtype=F32),
        ),
        q, q_far, left, left_far, right, right_far, mask, packed[TOK:, :TOK],
        packed_oth[TOK:, :TOK], b_own, b_oth, *out_pieces,
        scratch=[
            pltpu.VMEM((2 * TOK, MODEL_WIDTH), BF16),
            pltpu.VMEM((TOK, HID), BF16),
            pltpu.VMEM((TOK, HID), BF16),
        ],
        name="backward",
    )
    back = lax.all_to_all(back, ("l", "h", "c"), 0, 0, tiled=True)
    new_a, wire = call(
        down_kernel,
        (shape(RANK, MODEL_WIDTH, dtype=F32), shape(32, RANK, BLOCK + 2 * HID)),
        back, tokens, a, up_wire,
        name="down",
    )
    wires = lax.all_to_all(wire, REP, 0, 0, tiled=True)
    up_arrived = partner(up_oth, "l")
    new_b = jnp.where(
        l == 0,
        jnp.concatenate([up_own, up_arrived], axis=1),
        jnp.concatenate([up_arrived, up_own], axis=1),
    )
    merged = call(
        merge_kernel,
        shape(TOK, 2 * HID, dtype=F32),
        wires, w_in,
        scratch=[pltpu.VMEM((32 * RANK, BLOCK), BF16), pltpu.VMEM((32 * RANK, HID), BF16)],
        name="merge",
    )
    return merged, new_a[None], new_b[None]


def solution(mesh):
    split = Mesh(mesh.devices.reshape(4, 2, 4, 4, 2), ("y", "l", "x", "h", "c"))
    tp = ("h", "c")
    in_specs = (
        P(REP, None),
        P(REP, None),
        P(REP, tp),
        P(tp, REP),
        P(REP, None, None),
        P(REP, None, tp),
    )
    out_specs = (P(REP, tp), P(REP, None, None), P(REP, None, tp))
    return jax.shard_map(
        shards, mesh=split, in_specs=in_specs, out_specs=out_specs, check_vma=False
    )
```

```python
import jax
import jax.numpy as jnp
from jax import lax
from jax.experimental import pallas as pl
from jax.experimental.pallas import tpu as pltpu
from jax.sharding import Mesh
from jax.sharding import PartitionSpec as P

MODEL_WIDTH = 4096
FF = 8192
TOK = 128
RANK = 16
ROWS = 16
BLOCK = 128
HID = 512
SIDE = MODEL_WIDTH // 2
REP = ("y", "l", "x")
Z = ("l", "h")
ADAPTER_SCALE = 2.0
RATE_DOWN = 25.0
RATE_UP = 0.75
BF16 = jnp.bfloat16
F32 = jnp.float32

RING = (0, -1, 1, 2)


def dot(a, b):
    return jnp.dot(a, b, preferred_element_type=F32)


def dot_nt(a, b):
    return lax.dot_general(a, b, (((1,), (1,)), ((), ())), preferred_element_type=F32)


def dot_tn(a, b):
    return lax.dot_general(a, b, (((0,), (0,)), ((), ())), preferred_element_type=F32)


def shift(value, axis, by):
    n = lax.axis_size(axis)
    return lax.ppermute(value, axis, [(i, (i + by) % n) for i in range(n)])


def partner(value, axis):
    return lax.ppermute(value, axis, [(0, 1), (1, 0)])


def near_z(value):
    def place(z):
        return (z % 2) * 4 + (z % 8) // 2

    return lax.ppermute(
        value, Z, [(place(z), place(z + 1 if z % 2 else z - 1)) for z in range(8)]
    )


def call(kernel, out_shape, *args, scratch=(), after=(), name):
    vmem = pl.BlockSpec(memory_space=pltpu.VMEM)
    wait = pl.BlockSpec(memory_space=pl.ANY)
    many = isinstance(out_shape, tuple)
    return pl.pallas_call(
        kernel,
        out_shape=out_shape,
        in_specs=[vmem] * len(args) + [wait] * len(after),
        out_specs=(vmem,) * len(out_shape) if many else vmem,
        scratch_shapes=scratch,
        name=name,
    )(*args, *after)


def shape(*dims, dtype=BF16):
    return jax.ShapeDtypeStruct(dims, dtype)


def lanes(start, size):
    return pl.ds(pl.multiple_of(start, BLOCK), size)


def token_row(i):
    h, c = lax.axis_index("h"), lax.axis_index("c")
    j, e = i % 4, i // 8
    return pl.multiple_of((((h + j) % 4) * 2 + (c + e) % 2) * ROWS, ROWS)


def column(dy, side, dx):
    y, x = lax.axis_index("y"), lax.axis_index("x")
    return (((y + dy) % 4) * 8 + side * 4 + (x + dx) % 4) * BLOCK


def send_kernel(w_in_ref, w_out_ref, b_ref, send_ref):
    other = (1 - lax.axis_index("l")) * HID
    send_ref[:TOK] = w_in_ref[:, lanes(other, HID)]
    send_ref[TOK : 2 * TOK] = w_out_ref[lanes(other, HID), :].T
    send_ref[2 * TOK :] = b_ref[:, lanes(other, HID)]


def own_kernel(w_in_ref, w_out_ref, b_ref, send_ref, in_ref, out_ref, b_own_ref):
    mine = lax.axis_index("l") * HID
    in_ref[...] = w_in_ref[:, lanes(mine, HID)]
    out_ref[...] = w_out_ref[lanes(mine, HID), :].T
    b_own_ref[...] = b_ref[:, lanes(mine, HID)]


def pack_kernel(tokens_ref, a_ref, out_ref):
    out_ref[:TOK] = tokens_ref[...]
    out_ref[TOK:, :TOK] = dot_nt(a_ref[...], tokens_ref[...]).astype(BF16)


def arrange_kernel(own_ref, oth_ref, x_ref, p_ref, pt_ref, turned_ref):
    l = lax.axis_index("l")
    for k, ref in enumerate((own_ref, oth_ref)):
        pt_ref[k] = ref[TOK:, :TOK]
        turned_ref[k] = ref[TOK:, :TOK].astype(F32).T.astype(BF16)
    cols = [column(dy, l, dx) for dy in RING for dx in RING]
    cols += [column(dy, 1 - l, dx) for dx in RING for dy in RING]
    p_ref[...] = jnp.zeros_like(p_ref)
    for i in range(16):
        side = (i // 4) % 2
        src = oth_ref if side else own_ref
        row = token_row(i)
        lane = side * RANK
        p_ref[i * ROWS : (i + 1) * ROWS, lane : lane + RANK] = turned_ref[
            side, pl.ds(row, ROWS), :
        ]
        for j in range(32):
            x_ref[i * ROWS : (i + 1) * ROWS, j * BLOCK : (j + 1) * BLOCK] = src[
                pl.ds(row, ROWS), lanes(cols[j], BLOCK)
            ]


def near_kernel(x_ref, p_ref, b_own_ref, b_oth_ref, *refs):
    pieces, total_ref = refs[:6], refs[6]
    b = jnp.concatenate([b_own_ref[...], b_oth_ref[...]], axis=0)
    total = ADAPTER_SCALE * dot(p_ref[...], b)
    for k, piece in zip((0, 1, 2, 4, 5, 6), pieces):
        total = total + dot(x_ref[:, k * HID : (k + 1) * HID], piece[...])
    total_ref[...] = total


def hidden_kernel(x_ref, total_ref, own_ref, oth_ref, hidden_ref, mask_ref):
    total = total_ref[...]
    for k, piece in ((3, own_ref), (7, oth_ref)):
        total = total + dot(x_ref[:, k * HID : (k + 1) * HID], piece[...])
    preact = total * MODEL_WIDTH ** (-0.5)
    hidden_ref[...] = jnp.maximum(preact, 0.0).astype(BF16)
    mask = jnp.where(preact > 0, 1.0, 0.0).astype(BF16)
    for i in range(16):
        mask_ref[(i // 4) % 2, pl.ds(token_row(i), ROWS), :] = mask[i * ROWS : (i + 1) * ROWS]


def output_kernel(hidden_ref, *refs):
    pieces, out_ref = refs[:8], refs[-1]
    l = lax.axis_index("l")
    rows = slice(0, TOK) if out_ref.dtype == F32 else slice(TOK, 2 * TOK)
    for k, piece in enumerate(pieces):
        part = dot_nt(hidden_ref[rows], piece[...]).astype(out_ref.dtype).reshape(8, ROWS, HID)
        if k < 4:
            for j in range(4):
                to = l * SIDE + (j * 4 + k) * BLOCK
                out_ref[:, :, lanes(to, BLOCK)] = part[:, :, j * BLOCK : (j + 1) * BLOCK]
        else:
            out_ref[:, :, lanes((1 - l) * SIDE + (k - 4) * HID, HID)] = part


def finish_kernel(mine_ref, r1_ref, r2_ref, r3_ref, targets_ref, out_ref):
    h, c = lax.axis_index("h"), lax.axis_index("c")
    row = pl.multiple_of((h * 2 + c) * ROWS, ROWS)
    j = 0
    for side in range(2):
        for dy in RING:
            for dx in RING:
                here = slice(j * BLOCK, (j + 1) * BLOCK)
                total = mine_ref[:, here]
                for ref in (r1_ref, r2_ref, r3_ref):
                    total = total + ref[:, here].astype(F32)
                target = targets_ref[pl.ds(row, ROWS), lanes(column(dy, side, dx), BLOCK)]
                grad = (total * FF ** (-0.5) - target.astype(F32)) / TOK
                out_ref[:, here] = grad.astype(BF16)
                j += 1


def backward(grad_ref, mask, pt, b, pieces):
    l = lax.axis_index("l")
    total = None
    for k, piece in enumerate(pieces):
        if k < 4:
            part = jnp.concatenate(
                [grad_ref[:, lanes(l * SIDE + (j * 4 + k) * BLOCK, BLOCK)] for j in range(4)],
                axis=1,
            )
        else:
            part = grad_ref[:, lanes((1 - l) * SIDE + (k - 4) * HID, HID)]
        term = dot(part, piece[...])
        total = term if total is None else total + term
    hid = jnp.where(mask.astype(F32) > 0, total * FF ** (-0.5), 0.0).astype(BF16)
    scale = ADAPTER_SCALE * MODEL_WIDTH ** (-0.5)
    return b.astype(F32) - RATE_UP * (scale * dot(pt, hid)), dot_nt(b, hid)


def backward_own_kernel(q_ref, qc_ref, mask_ref, pt_ref, b_ref, *refs):
    pieces, (up_ref, back_ref, grad_ref) = refs[:8], refs[8:]
    for e, ref in enumerate((q_ref, qc_ref)):
        for j in range(4):
            grad_ref[pl.ds(token_row(e * 8 + j), ROWS), :] = ref[j]
    up_ref[...], back_ref[...] = backward(grad_ref, mask_ref[0], pt_ref[0], b_ref[...], pieces)


def backward_oth_kernel(left_ref, leftc_ref, right_ref, rightc_ref, mask_ref, pt_ref, b_ref,
                        up_own_ref, back_own_ref, *refs):
    pieces, (up_ref, wire_ref, back_ref, grad_ref) = refs[:8], refs[8:]
    l = lax.axis_index("l")
    for e, (left, right) in enumerate(((left_ref, right_ref), (leftc_ref, rightc_ref))):
        for j in range(4):
            rows = pl.ds(token_row(e * 8 + 4 + j), ROWS)
            grad_ref[rows, :SIDE] = left[j]
            grad_ref[rows, SIDE:] = right[(j + 1 + 2 * l) % 4]
    up, back = backward(grad_ref, mask_ref[1], pt_ref[1], b_ref[...], pieces)
    up_ref[...] = up
    wire_ref[l] = up_own_ref[...].astype(BF16)
    wire_ref[1 - l] = up.astype(BF16)
    for k in range(8):
        back_ref[l * 8 + k] = back_own_ref[...]
        back_ref[(1 - l) * 8 + k] = back


def down_kernel(back_ref, x_ref, a_ref, up_ref, new_ref, wire_ref):
    terms = [back_ref[k] for k in range(16)]
    while len(terms) > 1:
        terms = [terms[k] + terms[k + 1] for k in range(0, len(terms), 2)]
    rest = terms[0]
    parts = []
    for _ in range(3):
        parts.append(rest.astype(BF16))
        rest = rest - parts[-1].astype(F32)
    stacked = jnp.concatenate(parts, axis=0)
    scale = ADAPTER_SCALE * MODEL_WIDTH ** (-0.5)
    for k in range(8):
        here = slice(k * HID, (k + 1) * HID)
        grad = dot(stacked, x_ref[:, here])
        grad = grad[:RANK] + grad[RANK : 2 * RANK] + grad[2 * RANK :]
        new = a_ref[:, here].astype(F32) - RATE_DOWN * (scale * grad)
        new_ref[:, here] = new
        for j in range(4):
            wire_ref[k * 4 + j, :, :BLOCK] = new[:, j * BLOCK : (j + 1) * BLOCK].astype(BF16)
            for l in range(2):
                begin = BLOCK + l * HID
                wire_ref[k * 4 + j, :, begin : begin + HID] = up_ref[l]


def merge_kernel(wire_ref, w_ref, out_ref, d_ref, u_ref):
    for y in range(4):
        for x in range(4):
            for l in range(2):
                at = ((y * 4 + x) * 2 + l) * RANK
                d_ref[at : at + RANK, :] = wire_ref[y * 8 + l * 4 + x, :, :BLOCK]
    for side in range(2):
        for y in range(4):
            for x in range(4):
                for l in range(2):
                    at = ((y * 4 + x) * 2 + l) * RANK
                    begin = BLOCK + l * HID
                    u_ref[at : at + RANK, :] = wire_ref[
                        y * 8 + side * 4 + x, :, begin : begin + HID
                    ]
        here = slice(side * HID, (side + 1) * HID)
        delta = dot_tn(d_ref[...], u_ref[...])
        out_ref[:, here] = w_ref[:, here].astype(F32) + ADAPTER_SCALE / 32 * delta


def ring(value, axis):
    below, above = shift(value, axis, 1), shift(value, axis, -1)
    return [value, below, above, shift(below, axis, 1)]


def ring_direct(value, axis):
    return [value, shift(value, axis, 1), shift(value, axis, -1), shift(value, axis, 2)]


def shards(tokens, targets, w_in, w_out, factor_down, factor_up):
    l = lax.axis_index("l")
    a = factor_down[0]
    b = factor_up[0]

    w_send = call(send_kernel, shape(2 * TOK + RANK, HID), w_in, w_out, b, name="send")
    w_oth = partner(w_send, "l")
    in_own, out_own, b_own = call(
        own_kernel,
        (shape(TOK, HID), shape(TOK, HID), shape(RANK, HID)),
        w_in, w_out, b, w_send,
        name="own",
    )
    b_oth = w_oth[2 * TOK :]
    packed = call(pack_kernel, shape(TOK + RANK, MODEL_WIDTH), tokens, a, name="pack")
    packed_oth = near_z(packed)
    in_own = jnp.concatenate(ring(in_own, "x"), axis=0)
    out_own = jnp.concatenate(ring(out_own, "y"), axis=0)
    in_oth = jnp.concatenate(ring_direct(w_oth[:TOK], "y"), axis=0)
    out_oth = jnp.concatenate(ring_direct(w_oth[TOK : 2 * TOK], "x"), axis=0)

    x_rel, p_rel, pt = call(
        arrange_kernel,
        (shape(2 * TOK, MODEL_WIDTH), shape(2 * TOK, 2 * RANK), shape(2, RANK, TOK)),
        packed, packed_oth,
        scratch=[pltpu.VMEM((2, TOK, RANK), BF16)],
        name="arrange",
    )

    in_a = [in_own, shift(in_own, "y", 1), shift(in_own, "y", -1)]
    in_b = [in_oth, shift(in_oth, "x", 1), shift(in_oth, "x", -1)]
    out_a = [out_own, shift(out_own, "x", 1), shift(out_own, "x", -1)]
    out_b = [out_oth, shift(out_oth, "y", 1), shift(out_oth, "y", -1)]
    in_a[1], x_rel, p_rel = lax.optimization_barrier((in_a[1], x_rel, p_rel))
    in_a_far = shift(in_a[1], "y", 1)
    in_b_far = shift(in_b[1], "x", 1)
    total = call(
        near_kernel,
        shape(2 * TOK, HID, dtype=F32),
        x_rel, p_rel, b_own, b_oth, *in_a, *in_b,
        name="near",
    )
    out_a[2], out_b[2], total = lax.optimization_barrier((out_a[2], out_b[2], total))
    out_a_far = shift(out_a[2], "x", -1)
    out_b_far = shift(out_b[2], "y", -1)
    out_pieces = out_a + [out_a_far] + out_b + [out_b_far]
    hidden, mask = call(
        hidden_kernel,
        (shape(2 * TOK, HID), shape(2, TOK, HID)),
        x_rel, total, in_a_far, in_b_far,
        name="hidden",
    )
    send = call(
        output_kernel, shape(8, ROWS, MODEL_WIDTH), hidden, *out_pieces, name="output_send"
    )
    arrived = partner(send, "c")
    keep = call(
        output_kernel,
        shape(8, ROWS, MODEL_WIDTH, dtype=F32),
        hidden, *out_pieces,
        after=[send],
        name="output_keep",
    )

    summed = keep + arrived.astype(F32)
    away = summed[4:].astype(BF16)
    left = partner(away[:, :, :SIDE], "l")
    right = away[:, :, SIDE:]
    right = near_z(jnp.where(l == 0, jnp.roll(right, 1, 0), jnp.roll(right, -1, 0)))
    summed = summed[:4] + jnp.concatenate([left, right], axis=2).astype(F32)
    steps = [shift(summed[j].astype(BF16), "h", j) for j in (1, 2, 3)]
    grad_rows = call(
        finish_kernel, shape(ROWS, MODEL_WIDTH), summed[0], *steps, targets, name="finish"
    )

    q = jnp.stack([grad_rows] + [shift(grad_rows, "h", -j) for j in (1, 2, 3)])
    left = partner(q[:, :, :SIDE], "l")
    right = near_z(q[:, :, SIDE:])
    q_far, left_far, right_far = partner(q, "c"), partner(left, "c"), partner(right, "c")

    up_own, back_own = call(
        backward_own_kernel,
        (shape(RANK, HID, dtype=F32), shape(RANK, TOK, dtype=F32)),
        q, q_far, mask, pt, b_own, *out_pieces,
        scratch=[pltpu.VMEM((TOK, MODEL_WIDTH), BF16)],
        name="backward_own",
    )
    up_oth, up_wire, back = call(
        backward_oth_kernel,
        (
            shape(RANK, HID, dtype=F32),
            shape(2, RANK, HID),
            shape(16, RANK, TOK, dtype=F32),
        ),
        left, left_far, right, right_far, mask, pt, b_oth, up_own, back_own, *out_pieces,
        scratch=[pltpu.VMEM((TOK, MODEL_WIDTH), BF16)],
        name="backward_oth",
    )
    back = lax.all_to_all(back, ("l", "h", "c"), 0, 0, tiled=True)
    new_a, wire = call(
        down_kernel,
        (shape(RANK, MODEL_WIDTH, dtype=F32), shape(32, RANK, BLOCK + 2 * HID)),
        back, tokens, a, up_wire,
        name="down",
    )
    wires = lax.all_to_all(wire, REP, 0, 0, tiled=True)
    up_arrived = partner(up_oth, "l")
    new_b = jnp.where(
        l == 0,
        jnp.concatenate([up_own, up_arrived], axis=1),
        jnp.concatenate([up_arrived, up_own], axis=1),
    )
    merged = call(
        merge_kernel,
        shape(TOK, 2 * HID, dtype=F32),
        wires, w_in,
        scratch=[pltpu.VMEM((32 * RANK, BLOCK), BF16), pltpu.VMEM((32 * RANK, HID), BF16)],
        name="merge",
    )
    return merged, new_a[None], new_b[None]


def solution(mesh):
    split = Mesh(mesh.devices.reshape(4, 2, 4, 4, 2), ("y", "l", "x", "h", "c"))
    tp = ("h", "c")
    in_specs = (
        P(REP, None),
        P(REP, None),
        P(REP, tp),
        P(tp, REP),
        P(REP, None, None),
        P(REP, None, tp),
    )
    out_specs = (P(REP, tp), P(REP, None, None), P(REP, None, tp))
    return jax.shard_map(
        shards, mesh=split, in_specs=in_specs, out_specs=out_specs, check_vma=False
    )
```

```python
import jax
import jax.numpy as jnp
from jax import lax
from jax.experimental import pallas as pl
from jax.experimental.pallas import tpu as pltpu
from jax.sharding import Mesh
from jax.sharding import PartitionSpec as P

MODEL_WIDTH = 4096
FF = 8192
TOK = 128
RANK = 16
ROWS = 16
BLOCK = 128
HALF = 64
HID = 512
SIDE = MODEL_WIDTH // 2
REP = ("y", "l", "x")
Z = ("l", "h")
ADAPTER_SCALE = 2.0
RATE_DOWN = 25.0
RATE_UP = 0.75
BF16 = jnp.bfloat16
F32 = jnp.float32

RING = (0, -1, 1, 2)


def dot(a, b):
    return jnp.dot(a, b, preferred_element_type=F32)


def dot_nt(a, b):
    return lax.dot_general(a, b, (((1,), (1,)), ((), ())), preferred_element_type=F32)


def dot_tn(a, b):
    return lax.dot_general(a, b, (((0,), (0,)), ((), ())), preferred_element_type=F32)


def shift(value, axis, by):
    n = lax.axis_size(axis)
    return lax.ppermute(value, axis, [(i, (i + by) % n) for i in range(n)])


def partner(value, axis):
    return lax.ppermute(value, axis, [(0, 1), (1, 0)])


def near_z(value):
    def place(z):
        return (z % 2) * 4 + (z % 8) // 2

    return lax.ppermute(
        value, Z, [(place(z), place(z + 1 if z % 2 else z - 1)) for z in range(8)]
    )


def call(kernel, out_shape, *args, scratch=(), name):
    vmem = pl.BlockSpec(memory_space=pltpu.VMEM)
    many = isinstance(out_shape, tuple)
    return pl.pallas_call(
        kernel,
        out_shape=out_shape,
        in_specs=[vmem] * len(args),
        out_specs=(vmem,) * len(out_shape) if many else vmem,
        scratch_shapes=scratch,
        name=name,
    )(*args)


def shape(*dims, dtype=BF16):
    return jax.ShapeDtypeStruct(dims, dtype)


def lanes(start, size):
    return pl.ds(pl.multiple_of(start, BLOCK), size)


def token_row(i):
    c = lax.axis_index("c")
    h, e = (i // 2) % 4, i % 2
    return pl.multiple_of((h * 2 + (c + e) % 2) * ROWS, ROWS)


def column(dy, side, dx):
    y, x = lax.axis_index("y"), lax.axis_index("x")
    return (((y + dy) % 4) * 8 + side * 4 + (x + dx) % 4) * BLOCK


def send_kernel(w_in_ref, w_out_ref, b_ref, send_ref):
    other = (1 - lax.axis_index("l")) * HID
    send_ref[:TOK] = w_in_ref[:, lanes(other, HID)]
    send_ref[TOK : 2 * TOK] = w_out_ref[lanes(other, HID), :].T
    send_ref[2 * TOK :] = b_ref[:, lanes(other, HID)]


def own_kernel(w_in_ref, w_out_ref, b_ref, send_ref, in_ref, out_ref, b_own_ref):
    mine = lax.axis_index("l") * HID
    in_ref[...] = w_in_ref[:, lanes(mine, HID)]
    out_ref[...] = w_out_ref[lanes(mine, HID), :].T
    b_own_ref[...] = b_ref[:, lanes(mine, HID)]


def pack_kernel(tokens_ref, a_ref, out_ref, p_ref):
    c = lax.axis_index("c")
    p = dot_nt(a_ref[...], tokens_ref[...]).astype(BF16)
    out_ref[:HALF] = tokens_ref[pl.ds(pl.multiple_of(c * HALF, HALF), HALF), :]
    out_ref[HALF:, :TOK] = p
    p_ref[...] = p


def arrange_kernel(own_ref, oth_ref, oth_core_ref, p_own_ref, near_ref, far_ref, p_ref, pt_ref, turned_ref):
    l, c = lax.axis_index("l"), lax.axis_index("c")
    p_oth = oth_ref[HALF:, :TOK]
    pt_ref[0] = p_own_ref[...]
    pt_ref[1] = p_oth
    turned_ref[0] = p_own_ref[...].astype(F32).T.astype(BF16)
    turned_ref[1] = p_oth.astype(F32).T.astype(BF16)
    near = [column(dy, l, dx) for dy in RING[:3] for dx in RING]
    near += [column(dy, 1 - l, dx) for dx in RING[:3] for dy in RING]
    far = [column(RING[3], l, dx) for dx in RING] + [column(dy, 1 - l, RING[3]) for dy in RING]
    p_ref[...] = jnp.zeros_like(p_ref)
    for i in range(16):
        here = slice(i * ROWS, (i + 1) * ROWS)
        row = token_row(i)
        lane = 0 if i < 8 else RANK
        p_ref[here, lane : lane + RANK] = turned_ref[i // 8, pl.ds(row, ROWS), :]
        half = ((i // 2) % 4) // 2
        row_oth = pl.multiple_of(row - half * HALF, ROWS)
        for ref, cols in ((near_ref, near), (far_ref, far)):
            for j, col in enumerate(cols):
                if i < 8:
                    block = own_ref[pl.ds(row, ROWS), lanes(col, BLOCK)]
                else:
                    block = jnp.where(
                        c == half,
                        oth_ref[pl.ds(row_oth, ROWS), lanes(col, BLOCK)],
                        oth_core_ref[pl.ds(row_oth, ROWS), lanes(col, BLOCK)],
                    )
                ref[here, j * BLOCK : (j + 1) * BLOCK] = block


def targets_kernel(targets_ref, out_ref):
    h, c = lax.axis_index("h"), lax.axis_index("c")
    row = pl.multiple_of((h * 2 + c) * ROWS, ROWS)
    cols = [column(dy, side, dx) for side in range(2) for dy in RING for dx in RING]
    for j, col in enumerate(cols):
        out_ref[:, j * BLOCK : (j + 1) * BLOCK] = targets_ref[pl.ds(row, ROWS), lanes(col, BLOCK)]


def near_kernel(x_ref, p_ref, b_own_ref, b_oth_ref, *refs):
    pieces, total_ref = refs[:6], refs[6]
    b = jnp.concatenate([b_own_ref[...], b_oth_ref[...]], axis=0)
    total = ADAPTER_SCALE * dot(p_ref[...], b)
    for k, piece in enumerate(pieces):
        total = total + dot(x_ref[:, k * HID : (k + 1) * HID], piece[...])
    total_ref[...] = total


def hidden_kernel(x_ref, total_ref, own_ref, oth_ref, hidden_ref, mask_ref):
    total = total_ref[...]
    for k, piece in enumerate((own_ref, oth_ref)):
        total = total + dot(x_ref[:, k * HID : (k + 1) * HID], piece[...])
    preact = total * MODEL_WIDTH ** (-0.5)
    hidden_ref[...] = jnp.maximum(preact, 0.0).astype(BF16)
    mask_ref[...] = jnp.where(preact > 0, 1.0, 0.0).astype(BF16)


def output_kernel(hidden_ref, *refs):
    pieces, (keep_ref, send_ref) = refs[:8], refs[8:]
    l = lax.axis_index("l")
    for k, piece in enumerate(pieces):
        part = dot_nt(hidden_ref[...], piece[...]).reshape(8, 2, ROWS, HID)
        if k < 4:
            places = [(l * SIDE + (j * 4 + k) * BLOCK, j * BLOCK, BLOCK) for j in range(4)]
        else:
            places = [((1 - l) * SIDE + (k - 4) * HID, 0, HID)]
        for to, begin, size in places:
            keep_ref[:, :, lanes(to, size)] = part[:, 0, :, begin : begin + size]
            send_ref[:, :, lanes(to, size)] = part[:, 1, :, begin : begin + size].astype(BF16)


def backward_kernel(q_ref, qc_ref, left_ref, leftc_ref, right_ref, rightc_ref, mask_ref, pt_ref,
                    b_own_ref, b_oth_ref, *refs):
    pieces, (up_own_ref, up_oth_ref, wire_ref, back_ref, grad_ref, own_ref, oth_ref) = refs[:8], refs[8:]
    l = lax.axis_index("l")
    for i in range(16):
        j, e = (i // 2) % 4, i % 2
        here = slice(i * ROWS, (i + 1) * ROWS)
        if i < 8:
            grad_ref[here, :] = (q_ref, qc_ref)[e][j]
        else:
            grad_ref[here, :SIDE] = (left_ref, leftc_ref)[e][j]
            grad_ref[here, SIDE:] = (right_ref, rightc_ref)[e][j]
    total = None
    for k, piece in enumerate(pieces):
        if k < 4:
            part = jnp.concatenate(
                [grad_ref[:, lanes(l * SIDE + (j * 4 + k) * BLOCK, BLOCK)] for j in range(4)],
                axis=1,
            )
        else:
            part = grad_ref[:, lanes((1 - l) * SIDE + (k - 4) * HID, HID)]
        term = dot(part, piece[...])
        total = term if total is None else total + term
    total = jnp.where(mask_ref[...].astype(F32) > 0, total * FF ** (-0.5), 0.0).astype(BF16)
    for i in range(16):
        ref = own_ref if i < 8 else oth_ref
        ref[pl.ds(token_row(i), ROWS), :] = total[i * ROWS : (i + 1) * ROWS]
    scale = ADAPTER_SCALE * MODEL_WIDTH ** (-0.5)
    sides = (
        (l, own_ref, pt_ref[0], up_own_ref, b_own_ref[...]),
        (1 - l, oth_ref, pt_ref[1], up_oth_ref, b_oth_ref[...]),
    )
    for side, hid_ref, p, up_ref, b in sides:
        up = b.astype(F32) - RATE_UP * (scale * dot(p, hid_ref[...]))
        up_ref[...] = up
        wire_ref[side] = up.astype(BF16)
        back = dot_nt(b, hid_ref[...])
        for k in range(8):
            back_ref[side * 8 + k] = back


def down_kernel(back_ref, x_ref, a_ref, up_ref, new_ref, wire_ref):
    terms = [back_ref[k] for k in range(16)]
    while len(terms) > 1:
        terms = [terms[k] + terms[k + 1] for k in range(0, len(terms), 2)]
    rest = terms[0]
    parts = []
    for _ in range(3):
        parts.append(rest.astype(BF16))
        rest = rest - parts[-1].astype(F32)
    stacked = jnp.concatenate(parts, axis=0)
    scale = ADAPTER_SCALE * MODEL_WIDTH ** (-0.5)
    for k in range(8):
        here = slice(k * HID, (k + 1) * HID)
        grad = dot(stacked, x_ref[:, here])
        grad = grad[:RANK] + grad[RANK : 2 * RANK] + grad[2 * RANK :]
        new = a_ref[:, here].astype(F32) - RATE_DOWN * (scale * grad)
        new_ref[:, here] = new
        for j in range(4):
            wire_ref[k * 4 + j, :, :BLOCK] = new[:, j * BLOCK : (j + 1) * BLOCK].astype(BF16)
            for l in range(2):
                begin = BLOCK + l * HID
                wire_ref[k * 4 + j, :, begin : begin + HID] = up_ref[l]


def merge_kernel(wire_ref, w_ref, out_ref, d_ref, u_ref):
    for y in range(4):
        for x in range(4):
            for l in range(2):
                at = ((y * 4 + x) * 2 + l) * RANK
                d_ref[at : at + RANK, :] = wire_ref[y * 8 + l * 4 + x, :, :BLOCK]
    for side in range(2):
        for y in range(4):
            for x in range(4):
                for l in range(2):
                    at = ((y * 4 + x) * 2 + l) * RANK
                    begin = BLOCK + l * HID
                    u_ref[at : at + RANK, :] = wire_ref[
                        y * 8 + side * 4 + x, :, begin : begin + HID
                    ]
        here = slice(side * HID, (side + 1) * HID)
        delta = dot_tn(d_ref[...], u_ref[...])
        out_ref[:, here] = w_ref[:, here].astype(F32) + ADAPTER_SCALE / 32 * delta


def ring(value, axis):
    below, above = shift(value, axis, 1), shift(value, axis, -1)
    return [value, below, above, shift(below, axis, 1)]


def ring_direct(value, axis):
    return [value, shift(value, axis, 1), shift(value, axis, -1), shift(value, axis, 2)]


def shards(tokens, targets, w_in, w_out, factor_down, factor_up):
    l = lax.axis_index("l")
    a = factor_down[0]
    b = factor_up[0]

    w_send = call(send_kernel, shape(2 * TOK + RANK, HID), w_in, w_out, b, name="send")
    w_oth = partner(w_send, "l")
    in_own, out_own, b_own = call(
        own_kernel,
        (shape(TOK, HID), shape(TOK, HID), shape(RANK, HID)),
        w_in, w_out, b, w_send,
        name="own",
    )
    b_oth = w_oth[2 * TOK :]
    packed, p_own = call(
        pack_kernel, (shape(HALF + RANK, MODEL_WIDTH), shape(RANK, TOK)), tokens, a, name="pack"
    )
    tokens_oth = near_z(packed)
    tokens_oth_core = partner(tokens_oth, "c")
    in_own = jnp.concatenate(ring(in_own, "x"), axis=0)
    out_own = jnp.concatenate(ring(out_own, "y"), axis=0)
    in_oth = jnp.concatenate(ring_direct(w_oth[:TOK], "y"), axis=0)
    out_oth = jnp.concatenate(ring_direct(w_oth[TOK : 2 * TOK], "x"), axis=0)

    x_near, x_far, p_rel, pt = call(
        arrange_kernel,
        (shape(2 * TOK, 3072), shape(2 * TOK, 1024), shape(2 * TOK, 2 * RANK), shape(2, RANK, TOK)),
        tokens, tokens_oth, tokens_oth_core, p_own,
        scratch=[pltpu.VMEM((2, TOK, RANK), BF16)],
        name="arrange",
    )
    my_targets = call(targets_kernel, shape(ROWS, MODEL_WIDTH), targets, name="targets")
    in_oth, x_near, p_rel, my_targets = lax.optimization_barrier(
        (in_oth, x_near, p_rel, my_targets)
    )

    in_a = [in_own, shift(in_own, "y", 1), shift(in_own, "y", -1)]
    in_b = [in_oth, shift(in_oth, "x", 1), shift(in_oth, "x", -1)]
    out_a = [out_own, shift(out_own, "x", 1), shift(out_own, "x", -1)]
    out_b = [out_oth, shift(out_oth, "y", 1), shift(out_oth, "y", -1)]
    in_a_far = shift(in_a[1], "y", 1)
    in_b_far = shift(in_b[1], "x", 1)
    out_a_far = shift(out_a[2], "x", -1)
    out_b_far = shift(out_b[2], "y", -1)
    out_pieces = out_a + [out_a_far] + out_b + [out_b_far]

    total = call(
        near_kernel,
        shape(2 * TOK, HID, dtype=F32),
        x_near, p_rel, b_own, b_oth, *in_a, *in_b,
        name="near",
    )
    hidden, mask = call(
        hidden_kernel,
        (shape(2 * TOK, HID), shape(2 * TOK, HID)),
        x_far, total, in_a_far, in_b_far,
        name="hidden",
    )
    keep, send = call(
        output_kernel,
        (shape(8, ROWS, MODEL_WIDTH, dtype=F32), shape(8, ROWS, MODEL_WIDTH)),
        hidden, *out_pieces,
        name="output",
    )

    summed = keep + partner(send, "c").astype(F32)
    away = summed[4:].astype(BF16)
    left = partner(away[:, :, :SIDE], "l")
    right = away[:, :, SIDE:]
    right = near_z(right)
    summed = summed[:4] + jnp.concatenate([left, right], axis=2).astype(F32)
    shares = lax.all_to_all(summed.astype(BF16), "h", 0, 0, tiled=True)
    share = shares.astype(F32).sum(axis=0) * FF ** (-0.5)
    grad_rows = ((share - my_targets.astype(F32)) / TOK).astype(BF16)

    q = lax.all_to_all(jnp.broadcast_to(grad_rows, (4, ROWS, MODEL_WIDTH)), "h", 0, 0, tiled=True)
    left = partner(q[:, :, :SIDE], "l")
    right = near_z(q[:, :, SIDE:])
    q_far, left_far, right_far = partner(q, "c"), partner(left, "c"), partner(right, "c")

    up_own, up_oth, up_wire, back = call(
        backward_kernel,
        (
            shape(RANK, HID, dtype=F32),
            shape(RANK, HID, dtype=F32),
            shape(2, RANK, HID),
            shape(16, RANK, TOK, dtype=F32),
        ),
        q, q_far, left, left_far, right, right_far, mask, pt, b_own, b_oth, *out_pieces,
        scratch=[
            pltpu.VMEM((2 * TOK, MODEL_WIDTH), BF16),
            pltpu.VMEM((TOK, HID), BF16),
            pltpu.VMEM((TOK, HID), BF16),
        ],
        name="backward",
    )
    back = lax.all_to_all(back, ("l", "h", "c"), 0, 0, tiled=True)
    new_a, wire = call(
        down_kernel,
        (shape(RANK, MODEL_WIDTH, dtype=F32), shape(32, RANK, BLOCK + 2 * HID)),
        back, tokens, a, up_wire,
        name="down",
    )
    wires = lax.all_to_all(wire, REP, 0, 0, tiled=True)
    up_arrived = partner(up_oth, "l")
    new_b = jnp.where(
        l == 0,
        jnp.concatenate([up_own, up_arrived], axis=1),
        jnp.concatenate([up_arrived, up_own], axis=1),
    )
    merged = call(
        merge_kernel,
        shape(TOK, 2 * HID, dtype=F32),
        wires, w_in,
        scratch=[pltpu.VMEM((32 * RANK, BLOCK), BF16), pltpu.VMEM((32 * RANK, HID), BF16)],
        name="merge",
    )
    return merged, new_a[None], new_b[None]


def solution(mesh):
    split = Mesh(mesh.devices.reshape(4, 2, 4, 4, 2), ("y", "l", "x", "h", "c"))
    tp = ("h", "c")
    in_specs = (
        P(REP, None),
        P(REP, None),
        P(REP, tp),
        P(tp, REP),
        P(REP, None, None),
        P(REP, None, tp),
    )
    out_specs = (P(REP, tp), P(REP, None, None), P(REP, None, tp))
    return jax.shard_map(
        shards, mesh=split, in_specs=in_specs, out_specs=out_specs, check_vma=False
    )
```

```python
import jax
import jax.numpy as jnp
from jax import lax
from jax.experimental import pallas as pl
from jax.experimental.pallas import tpu as pltpu
from jax.sharding import Mesh
from jax.sharding import PartitionSpec as P

MODEL_WIDTH = 4096
FF = 8192
TOK = 128
RANK = 16
ROWS = 16
BLOCK = 128
HALF = 64
HID = 512
SIDE = MODEL_WIDTH // 2
REP = ("y", "l", "x")
Z = ("l", "h")
ADAPTER_SCALE = 2.0
RATE_DOWN = 25.0
RATE_UP = 0.75
BF16 = jnp.bfloat16
F32 = jnp.float32

RING = (0, -1, 1, 2)


def dot(a, b):
    return jnp.dot(a, b, preferred_element_type=F32)


def dot_nt(a, b):
    return lax.dot_general(a, b, (((1,), (1,)), ((), ())), preferred_element_type=F32)


def dot_tn(a, b):
    return lax.dot_general(a, b, (((0,), (0,)), ((), ())), preferred_element_type=F32)


def shift(value, axis, by):
    n = lax.axis_size(axis)
    return lax.ppermute(value, axis, [(i, (i + by) % n) for i in range(n)])


def partner(value, axis):
    return lax.ppermute(value, axis, [(0, 1), (1, 0)])


def near_z(value):
    def place(z):
        return (z % 2) * 4 + (z % 8) // 2

    return lax.ppermute(
        value, Z, [(place(z), place(z + 1 if z % 2 else z - 1)) for z in range(8)]
    )


def call(kernel, out_shape, *args, scratch=(), after=(), name):
    vmem = pl.BlockSpec(memory_space=pltpu.VMEM)
    wait = pl.BlockSpec(memory_space=pl.ANY)
    many = isinstance(out_shape, tuple)
    return pl.pallas_call(
        kernel,
        out_shape=out_shape,
        in_specs=[vmem] * len(args) + [wait] * len(after),
        out_specs=(vmem,) * len(out_shape) if many else vmem,
        scratch_shapes=scratch,
        name=name,
    )(*args, *after)


def shape(*dims, dtype=BF16):
    return jax.ShapeDtypeStruct(dims, dtype)


def lanes(start, size):
    return pl.ds(pl.multiple_of(start, BLOCK), size)


def token_row(i):
    c = lax.axis_index("c")
    h, e = (i // 2) % 4, i % 2
    return pl.multiple_of((h * 2 + (c + e) % 2) * ROWS, ROWS)


def column(dy, side, dx):
    y, x = lax.axis_index("y"), lax.axis_index("x")
    return (((y + dy) % 4) * 8 + side * 4 + (x + dx) % 4) * BLOCK


def send_kernel(w_in_ref, w_out_ref, b_ref, send_ref):
    other = (1 - lax.axis_index("l")) * HID
    send_ref[:TOK] = w_in_ref[:, lanes(other, HID)]
    send_ref[TOK : 2 * TOK] = w_out_ref[lanes(other, HID), :].T
    send_ref[2 * TOK :] = b_ref[:, lanes(other, HID)]


def own_kernel(w_in_ref, w_out_ref, b_ref, send_ref, in_ref, out_ref, b_own_ref):
    mine = lax.axis_index("l") * HID
    in_ref[...] = w_in_ref[:, lanes(mine, HID)]
    out_ref[...] = w_out_ref[lanes(mine, HID), :].T
    b_own_ref[...] = b_ref[:, lanes(mine, HID)]


def pack_kernel(tokens_ref, a_ref, after_ref, out_ref, p_ref):
    c = lax.axis_index("c")
    p = dot_nt(a_ref[...], tokens_ref[...]).astype(BF16)
    out_ref[:HALF] = tokens_ref[pl.ds(pl.multiple_of(c * HALF, HALF), HALF), :]
    out_ref[HALF:, :TOK] = p
    p_ref[...] = p


def arrange_kernel(own_ref, oth_ref, oth_core_ref, p_own_ref, near_ref, far_ref, p_ref, pt_ref, turned_ref):
    c = lax.axis_index("c")
    p_oth = oth_ref[HALF:, :TOK]
    pt_ref[0] = p_own_ref[...]
    pt_ref[1] = p_oth
    turned_ref[0] = p_own_ref[...].astype(F32).T.astype(BF16)
    turned_ref[1] = p_oth.astype(F32).T.astype(BF16)
    near = [column(dy, side, dx) for dy in RING[:3] for dx in RING for side in range(2)]
    far = [column(RING[3], side, dx) for dx in RING for side in range(2)]
    p_ref[...] = jnp.zeros_like(p_ref)
    for i in range(16):
        here = slice(i * ROWS, (i + 1) * ROWS)
        row = token_row(i)
        lane = 0 if i < 8 else RANK
        p_ref[here, lane : lane + RANK] = turned_ref[i // 8, pl.ds(row, ROWS), :]
        half = ((i // 2) % 4) // 2
        row_oth = pl.multiple_of(row - half * HALF, ROWS)
        for ref, cols in ((near_ref, near), (far_ref, far)):
            for j, col in enumerate(cols):
                if i < 8:
                    block = own_ref[pl.ds(row, ROWS), lanes(col, BLOCK)]
                else:
                    block = jnp.where(
                        c == half,
                        oth_ref[pl.ds(row_oth, ROWS), lanes(col, BLOCK)],
                        oth_core_ref[pl.ds(row_oth, ROWS), lanes(col, BLOCK)],
                    )
                ref[here, j * BLOCK : (j + 1) * BLOCK] = block


def targets_kernel(targets_ref, after_ref, out_ref):
    h, c = lax.axis_index("h"), lax.axis_index("c")
    row = pl.multiple_of((h * 2 + c) * ROWS, ROWS)
    cols = [column(dy, side, dx) for dx in RING for dy in RING for side in range(2)]
    for j, col in enumerate(cols):
        out_ref[:, j * BLOCK : (j + 1) * BLOCK] = targets_ref[pl.ds(row, ROWS), lanes(col, BLOCK)]


def near_kernel(x_ref, p_ref, b_own_ref, b_oth_ref, *refs):
    pieces, total_ref = refs[:3], refs[3]
    b = jnp.concatenate([b_own_ref[...], b_oth_ref[...]], axis=0)
    total = ADAPTER_SCALE * dot(p_ref[...], b)
    for k, piece in enumerate(pieces):
        total = total + dot(x_ref[:, k * 1024 : (k + 1) * 1024], piece[...])
    total_ref[...] = total


def hidden_kernel(x_ref, total_ref, low_ref, high_ref, hidden_ref, mask_ref):
    total = total_ref[...]
    for k, piece in enumerate((low_ref, high_ref)):
        total = total + dot(x_ref[:, k * HID : (k + 1) * HID], piece[...])
    preact = total * MODEL_WIDTH ** (-0.5)
    hidden_ref[...] = jnp.maximum(preact, 0.0).astype(BF16)
    mask_ref[...] = jnp.where(preact > 0, 1.0, 0.0).astype(BF16)


def spans(pieces):
    begin = 0
    for piece in pieces:
        yield slice(begin, begin + piece.shape[0]), piece
        begin += piece.shape[0]


def output_kernel(hidden_ref, *refs):
    pieces, (keep_ref, send_ref) = refs[:5], refs[5:]
    for cols, piece in spans(pieces):
        part = dot_nt(hidden_ref[...], piece[...]).reshape(8, 2, ROWS, piece.shape[0])
        keep_ref[:, :, cols] = part[:, 0]
        send_ref[:, :, cols] = part[:, 1].astype(BF16)


def backward_kernel(q_ref, qc_ref, left_ref, leftc_ref, right_ref, rightc_ref, mask_ref, pt_ref,
                    b_own_ref, b_oth_ref, *refs):
    pieces, (up_own_ref, up_oth_ref, wire_ref, back_ref, grad_ref, own_ref, oth_ref) = refs[:5], refs[5:]
    l = lax.axis_index("l")
    for i in range(16):
        j, e = (i // 2) % 4, i % 2
        here = slice(i * ROWS, (i + 1) * ROWS)
        if i < 8:
            grad_ref[here, :] = (q_ref, qc_ref)[e][j]
        else:
            grad_ref[here, :SIDE] = (left_ref, leftc_ref)[e][j]
            grad_ref[here, SIDE:] = (right_ref, rightc_ref)[e][j]
    total = None
    for cols, piece in spans(pieces):
        term = dot(grad_ref[:, cols], piece[...])
        total = term if total is None else total + term
    total = jnp.where(mask_ref[...].astype(F32) > 0, total * FF ** (-0.5), 0.0).astype(BF16)
    for i in range(16):
        ref = own_ref if i < 8 else oth_ref
        ref[pl.ds(token_row(i), ROWS), :] = total[i * ROWS : (i + 1) * ROWS]
    scale = ADAPTER_SCALE * MODEL_WIDTH ** (-0.5)
    sides = (
        (l, own_ref, pt_ref[0], up_own_ref, b_own_ref[...]),
        (1 - l, oth_ref, pt_ref[1], up_oth_ref, b_oth_ref[...]),
    )
    for side, hid_ref, p, up_ref, b in sides:
        up = b.astype(F32) - RATE_UP * (scale * dot(p, hid_ref[...]))
        up_ref[...] = up
        wire_ref[side] = up.astype(BF16)
        back = dot_nt(b, hid_ref[...])
        for k in range(8):
            back_ref[side * 8 + k] = back


def down_kernel(back_ref, x_ref, a_ref, up_ref, new_ref, wire_ref):
    terms = [back_ref[k] for k in range(16)]
    while len(terms) > 1:
        terms = [terms[k] + terms[k + 1] for k in range(0, len(terms), 2)]
    rest = terms[0]
    parts = []
    for _ in range(3):
        parts.append(rest.astype(BF16))
        rest = rest - parts[-1].astype(F32)
    stacked = jnp.concatenate(parts, axis=0)
    scale = ADAPTER_SCALE * MODEL_WIDTH ** (-0.5)
    for k in range(8):
        here = slice(k * HID, (k + 1) * HID)
        grad = dot(stacked, x_ref[:, here])
        grad = grad[:RANK] + grad[RANK : 2 * RANK] + grad[2 * RANK :]
        new = a_ref[:, here].astype(F32) - RATE_DOWN * (scale * grad)
        new_ref[:, here] = new
        for j in range(4):
            wire_ref[k * 4 + j, :, :BLOCK] = new[:, j * BLOCK : (j + 1) * BLOCK].astype(BF16)
            for l in range(2):
                begin = BLOCK + l * HID
                wire_ref[k * 4 + j, :, begin : begin + HID] = up_ref[l]


def merge_kernel(wire_ref, w_ref, out_ref, d_ref, u_ref):
    for y in range(4):
        for x in range(4):
            for l in range(2):
                at = ((y * 4 + x) * 2 + l) * RANK
                d_ref[at : at + RANK, :] = wire_ref[y * 8 + l * 4 + x, :, :BLOCK]
    for side in range(2):
        for y in range(4):
            for x in range(4):
                for l in range(2):
                    at = ((y * 4 + x) * 2 + l) * RANK
                    begin = BLOCK + l * HID
                    u_ref[at : at + RANK, :] = wire_ref[
                        y * 8 + side * 4 + x, :, begin : begin + HID
                    ]
        here = slice(side * HID, (side + 1) * HID)
        delta = dot_tn(d_ref[...], u_ref[...])
        out_ref[:, here] = w_ref[:, here].astype(F32) + ADAPTER_SCALE / 32 * delta


def ring(value, axis):
    below, above = shift(value, axis, 1), shift(value, axis, -1)
    return [value, below, above, shift(below, axis, 1)]


def far_halves(below, above, axis):
    half = below.shape[0] // 2
    return [shift(below[:half], axis, 1), shift(above[half:], axis, -1)]


def shards(tokens, targets, w_in, w_out, factor_down, factor_up):
    l = lax.axis_index("l")
    a = factor_down[0]
    b = factor_up[0]

    w_send = call(send_kernel, shape(2 * TOK + RANK, HID), w_in, w_out, b, name="send")
    w_oth = partner(w_send, "l")
    in_own, out_own, b_own = call(
        own_kernel,
        (shape(TOK, HID), shape(TOK, HID), shape(RANK, HID)),
        w_in, w_out, b, w_send,
        name="own",
    )
    b_oth = w_oth[2 * TOK :]
    packed, p_own = call(
        pack_kernel,
        (shape(HALF + RANK, MODEL_WIDTH), shape(RANK, TOK)),
        tokens, a,
        after=[in_own],
        name="pack",
    )
    tokens_oth = near_z(packed)
    tokens_oth_core = partner(tokens_oth, "c")

    def joined(own, oth):
        return jnp.where(
            l == 0, jnp.concatenate([own, oth], axis=0), jnp.concatenate([oth, own], axis=0)
        )

    in_line = jnp.concatenate(ring(joined(in_own, w_oth[:TOK]), "x"), axis=0)
    out_line = jnp.concatenate(ring(joined(out_own, w_oth[TOK : 2 * TOK]), "y"), axis=0)
    in_near = [in_line, shift(in_line, "y", 1), shift(in_line, "y", -1)]
    out_near = [out_line, shift(out_line, "x", 1), shift(out_line, "x", -1)]

    x_near, x_far, p_rel, pt = call(
        arrange_kernel,
        (shape(2 * TOK, 3072), shape(2 * TOK, 1024), shape(2 * TOK, 2 * RANK), shape(2, RANK, TOK)),
        tokens, tokens_oth, tokens_oth_core, p_own,
        scratch=[pltpu.VMEM((2, TOK, RANK), BF16)],
        name="arrange",
    )
    my_targets = call(
        targets_kernel, shape(ROWS, MODEL_WIDTH), targets, after=[p_rel], name="targets"
    )
    in_near[1], in_near[2], x_near, p_rel, my_targets = lax.optimization_barrier(
        (in_near[1], in_near[2], x_near, p_rel, my_targets)
    )
    in_far = far_halves(in_near[1], in_near[2], "y")
    out_far = far_halves(out_near[1], out_near[2], "x")
    out_pieces = out_near + out_far
    total = call(
        near_kernel,
        shape(2 * TOK, HID, dtype=F32),
        x_near, p_rel, b_own, b_oth, *in_near,
        name="near",
    )
    hidden, mask = call(
        hidden_kernel,
        (shape(2 * TOK, HID), shape(2 * TOK, HID)),
        x_far, total, *in_far,
        name="hidden",
    )
    keep, send = call(
        output_kernel,
        (shape(8, ROWS, MODEL_WIDTH, dtype=F32), shape(8, ROWS, MODEL_WIDTH)),
        hidden, *out_pieces,
        name="output",
    )

    summed = keep + partner(send, "c").astype(F32)
    away = summed[4:].astype(BF16)
    left = partner(away[:, :, :SIDE], "l")
    right = away[:, :, SIDE:]
    right = near_z(right)
    summed = summed[:4] + jnp.concatenate([left, right], axis=2).astype(F32)
    shares = lax.all_to_all(summed.astype(BF16), "h", 0, 0, tiled=True)
    share = shares.astype(F32).sum(axis=0) * FF ** (-0.5)
    grad_rows = ((share - my_targets.astype(F32)) / TOK).astype(BF16)

    q = lax.all_to_all(jnp.broadcast_to(grad_rows, (4, ROWS, MODEL_WIDTH)), "h", 0, 0, tiled=True)
    left = partner(q[:, :, :SIDE], "l")
    right = near_z(q[:, :, SIDE:])
    q_far, left_far, right_far = partner(q, "c"), partner(left, "c"), partner(right, "c")

    up_own, up_oth, up_wire, back = call(
        backward_kernel,
        (
            shape(RANK, HID, dtype=F32),
            shape(RANK, HID, dtype=F32),
            shape(2, RANK, HID),
            shape(16, RANK, TOK, dtype=F32),
        ),
        q, q_far, left, left_far, right, right_far, mask, pt, b_own, b_oth, *out_pieces,
        scratch=[
            pltpu.VMEM((2 * TOK, MODEL_WIDTH), BF16),
            pltpu.VMEM((TOK, HID), BF16),
            pltpu.VMEM((TOK, HID), BF16),
        ],
        name="backward",
    )
    back = lax.all_to_all(back, ("l", "h", "c"), 0, 0, tiled=True)
    new_a, wire = call(
        down_kernel,
        (shape(RANK, MODEL_WIDTH, dtype=F32), shape(32, RANK, BLOCK + 2 * HID)),
        back, tokens, a, up_wire,
        name="down",
    )
    wires = lax.all_to_all(wire, REP, 0, 0, tiled=True)
    up_arrived = partner(up_oth, "l")
    new_b = jnp.where(
        l == 0,
        jnp.concatenate([up_own, up_arrived], axis=1),
        jnp.concatenate([up_arrived, up_own], axis=1),
    )
    merged = call(
        merge_kernel,
        shape(TOK, 2 * HID, dtype=F32),
        wires, w_in,
        scratch=[pltpu.VMEM((32 * RANK, BLOCK), BF16), pltpu.VMEM((32 * RANK, HID), BF16)],
        name="merge",
    )
    return merged, new_a[None], new_b[None]


def solution(mesh):
    split = Mesh(mesh.devices.reshape(4, 2, 4, 4, 2), ("y", "l", "x", "h", "c"))
    tp = ("h", "c")
    in_specs = (
        P(REP, None),
        P(REP, None),
        P(REP, tp),
        P(tp, REP),
        P(REP, None, None),
        P(REP, None, tp),
    )
    out_specs = (P(REP, tp), P(REP, None, None), P(REP, None, tp))
    return jax.shard_map(
        shards, mesh=split, in_specs=in_specs, out_specs=out_specs, check_vma=False
    )
```

```python
import jax
import jax.numpy as jnp
from jax import lax
from jax.experimental import pallas as pl
from jax.experimental.pallas import tpu as pltpu
from jax.sharding import Mesh
from jax.sharding import PartitionSpec as P

MODEL_WIDTH = 4096
FF = 8192
TOK = 128
RANK = 16
ROWS = 16
BLOCK = 128
HALF = 64
HID = 512
SIDE = MODEL_WIDTH // 2
REP = ("y", "l", "x")
Z = ("l", "h")
ADAPTER_SCALE = 2.0
RATE_DOWN = 25.0
RATE_UP = 0.75
BF16 = jnp.bfloat16
F32 = jnp.float32

RING = (0, -1, 1, 2)


def dot(a, b):
    return jnp.dot(a, b, preferred_element_type=F32)


def dot_nt(a, b):
    return lax.dot_general(a, b, (((1,), (1,)), ((), ())), preferred_element_type=F32)


def dot_tn(a, b):
    return lax.dot_general(a, b, (((0,), (0,)), ((), ())), preferred_element_type=F32)


def shift(value, axis, by):
    n = lax.axis_size(axis)
    return lax.ppermute(value, axis, [(i, (i + by) % n) for i in range(n)])


def partner(value, axis):
    return lax.ppermute(value, axis, [(0, 1), (1, 0)])


def near_z(value):
    def place(z):
        return (z % 2) * 4 + (z % 8) // 2

    return lax.ppermute(
        value, Z, [(place(z), place(z + 1 if z % 2 else z - 1)) for z in range(8)]
    )


def call(kernel, out_shape, *args, scratch=(), after=(), name):
    vmem = pl.BlockSpec(memory_space=pltpu.VMEM)
    wait = pl.BlockSpec(memory_space=pl.ANY)
    many = isinstance(out_shape, tuple)
    return pl.pallas_call(
        kernel,
        out_shape=out_shape,
        in_specs=[vmem] * len(args) + [wait] * len(after),
        out_specs=(vmem,) * len(out_shape) if many else vmem,
        scratch_shapes=scratch,
        name=name,
    )(*args, *after)


def shape(*dims, dtype=BF16):
    return jax.ShapeDtypeStruct(dims, dtype)


def lanes(start, size):
    return pl.ds(pl.multiple_of(start, BLOCK), size)


def token_row(i):
    c = lax.axis_index("c")
    h, e = (i // 2) % 4, i % 2
    return pl.multiple_of((h * 2 + (c + e) % 2) * ROWS, ROWS)


def column(dy, side, dx):
    y, x = lax.axis_index("y"), lax.axis_index("x")
    return (((y + dy) % 4) * 8 + side * 4 + (x + dx) % 4) * BLOCK


def send_kernel(w_in_ref, w_out_ref, b_ref, send_ref):
    other = (1 - lax.axis_index("l")) * HID
    send_ref[:TOK] = w_in_ref[:, lanes(other, HID)]
    send_ref[TOK : 2 * TOK] = w_out_ref[lanes(other, HID), :].T
    send_ref[2 * TOK :] = b_ref[:, lanes(other, HID)]


def own_kernel(w_in_ref, w_out_ref, b_ref, send_ref, in_ref, out_ref, b_own_ref):
    mine = lax.axis_index("l") * HID
    in_ref[...] = w_in_ref[:, lanes(mine, HID)]
    out_ref[...] = w_out_ref[lanes(mine, HID), :].T
    b_own_ref[...] = b_ref[:, lanes(mine, HID)]


def pack_kernel(tokens_ref, a_ref, after_ref, out_ref, p_ref):
    c = lax.axis_index("c")
    p = dot_nt(a_ref[...], tokens_ref[...]).astype(BF16)
    out_ref[:HALF] = tokens_ref[pl.ds(pl.multiple_of(c * HALF, HALF), HALF), :]
    out_ref[HALF:, :TOK] = p
    p_ref[...] = p


def arrange_kernel(own_ref, oth_ref, oth_core_ref, p_own_ref, near_ref, far_ref, p_ref, pt_ref, turned_ref):
    c = lax.axis_index("c")
    p_oth = oth_ref[HALF:, :TOK]
    pt_ref[0] = p_own_ref[...]
    pt_ref[1] = p_oth
    turned_ref[0] = p_own_ref[...].astype(F32).T.astype(BF16)
    turned_ref[1] = p_oth.astype(F32).T.astype(BF16)
    near = [column(dy, side, dx) for dy in RING[:3] for dx in RING for side in range(2)]
    far = [column(RING[3], side, dx) for dx in RING for side in range(2)]
    p_ref[...] = jnp.zeros_like(p_ref)
    for i in range(16):
        here = slice(i * ROWS, (i + 1) * ROWS)
        row = token_row(i)
        lane = 0 if i < 8 else RANK
        p_ref[here, lane : lane + RANK] = turned_ref[i // 8, pl.ds(row, ROWS), :]
        half = ((i // 2) % 4) // 2
        row_oth = pl.multiple_of(row - half * HALF, ROWS)
        for ref, cols in ((near_ref, near), (far_ref, far)):
            for j, col in enumerate(cols):
                if i < 8:
                    block = own_ref[pl.ds(row, ROWS), lanes(col, BLOCK)]
                else:
                    block = jnp.where(
                        c == half,
                        oth_ref[pl.ds(row_oth, ROWS), lanes(col, BLOCK)],
                        oth_core_ref[pl.ds(row_oth, ROWS), lanes(col, BLOCK)],
                    )
                ref[here, j * BLOCK : (j + 1) * BLOCK] = block


def targets_kernel(targets_ref, after_ref, out_ref):
    h, c = lax.axis_index("h"), lax.axis_index("c")
    row = pl.multiple_of((h * 2 + c) * ROWS, ROWS)
    cols = [column(dy, side, dx) for dx in RING for dy in RING for side in range(2)]
    for j, col in enumerate(cols):
        out_ref[:, j * BLOCK : (j + 1) * BLOCK] = targets_ref[pl.ds(row, ROWS), lanes(col, BLOCK)]


def near_kernel(x_ref, p_ref, b_own_ref, b_oth_ref, *refs):
    pieces, total_ref = refs[:6], refs[6]
    b = jnp.concatenate([b_own_ref[...], b_oth_ref[...]], axis=0)
    total = ADAPTER_SCALE * dot(p_ref[...], b)
    for cols, piece in spans(pieces):
        total = total + dot(x_ref[:, cols], piece[...])
    total_ref[...] = total


def hidden_kernel(x_ref, total_ref, low_ref, high_ref, hidden_ref, mask_ref):
    total = total_ref[...]
    for cols, piece in spans((low_ref, high_ref)):
        total = total + dot(x_ref[:, cols], piece[...])
    preact = total * MODEL_WIDTH ** (-0.5)
    hidden_ref[...] = jnp.maximum(preact, 0.0).astype(BF16)
    mask_ref[...] = jnp.where(preact > 0, 1.0, 0.0).astype(BF16)


def spans(pieces):
    begin = 0
    for piece in pieces:
        yield slice(begin, begin + piece.shape[0]), piece
        begin += piece.shape[0]


def output_kernel(hidden_ref, *refs):
    pieces, (keep_ref, send_ref) = refs[:8], refs[8:]
    for cols, piece in spans(pieces):
        part = dot_nt(hidden_ref[...], piece[...]).reshape(8, 2, ROWS, piece.shape[0])
        keep_ref[:, :, cols] = part[:, 0]
        send_ref[:, :, cols] = part[:, 1].astype(BF16)


def backward_kernel(q_ref, qc_ref, left_ref, leftc_ref, right_ref, rightc_ref, mask_ref, pt_ref,
                    b_own_ref, b_oth_ref, *refs):
    pieces, (up_ref, back_ref, grad_ref, own_ref, oth_ref) = refs[:8], refs[8:]
    for i in range(16):
        j, e = (i // 2) % 4, i % 2
        here = slice(i * ROWS, (i + 1) * ROWS)
        if i < 8:
            grad_ref[here, :] = (q_ref, qc_ref)[e][j]
        else:
            grad_ref[here, :SIDE] = (left_ref, leftc_ref)[e][j]
            grad_ref[here, SIDE:] = (right_ref, rightc_ref)[e][j]
    total = None
    for cols, piece in spans(pieces):
        term = dot(grad_ref[:, cols], piece[...])
        total = term if total is None else total + term
    total = jnp.where(mask_ref[...].astype(F32) > 0, total * FF ** (-0.5), 0.0).astype(BF16)
    for i in range(16):
        ref = own_ref if i < 8 else oth_ref
        ref[pl.ds(token_row(i), ROWS), :] = total[i * ROWS : (i + 1) * ROWS]
    scale = ADAPTER_SCALE * MODEL_WIDTH ** (-0.5)
    for side, (hid_ref, b_ref) in enumerate(((own_ref, b_own_ref), (oth_ref, b_oth_ref))):
        grad = dot(pt_ref[side], hid_ref[...])
        up_ref[side] = b_ref[...].astype(F32) - RATE_UP * (scale * grad)
        back_ref[side] = dot_nt(b_ref[...], hid_ref[...])


def ups_kernel(mine_ref, arrived_ref, new_ref, wire_ref):
    l = lax.axis_index("l")
    for ref, half in ((mine_ref, l), (arrived_ref, 1 - l)):
        new_ref[:, lanes(half * HID, HID)] = ref[0]
        for side, row in ((0, l * RANK), (1, (1 - l) * RANK)):
            rows = pl.ds(pl.multiple_of(row, RANK), RANK)
            wire_ref[rows, lanes(half * HID, HID)] = ref[side].astype(BF16)


def down_kernel(t0_ref, t1_ref, t2_ref, t3_ref, x_ref, a_ref, new_ref, wire_ref):
    rest = (t0_ref[...] + t1_ref[...]) + (t2_ref[...] + t3_ref[...])
    parts = []
    for _ in range(3):
        parts.append(rest.astype(BF16))
        rest = rest - parts[-1].astype(F32)
    stacked = jnp.concatenate(parts, axis=0)
    scale = ADAPTER_SCALE * MODEL_WIDTH ** (-0.5)
    for k in range(8):
        here = slice(k * HID, (k + 1) * HID)
        grad = dot(stacked, x_ref[:, here])
        grad = grad[:RANK] + grad[RANK : 2 * RANK] + grad[2 * RANK :]
        new = a_ref[:, here].astype(F32) - RATE_DOWN * (scale * grad)
        new_ref[:, here] = new
        for j in range(4):
            wire_ref[k * 4 + j] = new[:, j * BLOCK : (j + 1) * BLOCK].astype(BF16)


def merge_kernel(wire_ref, u0_ref, u1_ref, u2_ref, u3_ref, w_ref, out_ref, d_ref):
    y, x = lax.axis_index("y"), lax.axis_index("x")
    total = None
    for k, (dy, u_ref) in enumerate(zip(RING, (u0_ref, u1_ref, u2_ref, u3_ref))):
        for j, dx in enumerate(RING):
            for l in range(2):
                at = ((k * 4 + j) * 2 + l) * RANK
                d_ref[at : at + RANK, :] = wire_ref[((y + dy) % 4) * 8 + l * 4 + (x + dx) % 4]
        term = dot_tn(d_ref[k * TOK : (k + 1) * TOK, :], u_ref[...])
        total = term if total is None else total + term
    out_ref[...] = w_ref[...].astype(F32) + ADAPTER_SCALE / 32 * total


def gather_grid(value, first, second):
    below, above = shift(value, first, 1), shift(value, first, -1)
    low = jnp.concatenate([value, below], axis=0)
    high = jnp.concatenate([above, shift(below, first, 1)], axis=0)
    near = [low, high]
    for by in (1, -1):
        near += [shift(low, second, by), shift(high, second, by)]
    return near, [shift(near[2], second, 1), shift(near[5], second, -1)]


def ring_direct(value, axis):
    return [value, shift(value, axis, 1), shift(value, axis, -1), shift(value, axis, 2)]


def swap(value, mask):
    return lax.ppermute(value, "h", [(i, i ^ mask) for i in range(4)])


def shards(tokens, targets, w_in, w_out, factor_down, factor_up):
    l = lax.axis_index("l")
    a = factor_down[0]
    b = factor_up[0]

    w_send = call(send_kernel, shape(2 * TOK + RANK, HID), w_in, w_out, b, name="send")
    w_oth = partner(w_send, "l")
    in_own, out_own, b_own = call(
        own_kernel,
        (shape(TOK, HID), shape(TOK, HID), shape(RANK, HID)),
        w_in, w_out, b, w_send,
        name="own",
    )
    b_oth = w_oth[2 * TOK :]
    packed, p_own = call(
        pack_kernel,
        (shape(HALF + RANK, MODEL_WIDTH), shape(RANK, TOK)),
        tokens, a,
        after=[in_own],
        name="pack",
    )
    tokens_oth = near_z(packed)
    tokens_oth_core = partner(tokens_oth, "c")

    def joined(own, oth):
        return jnp.where(
            l == 0, jnp.concatenate([own, oth], axis=0), jnp.concatenate([oth, own], axis=0)
        )

    in_near, in_far = gather_grid(joined(in_own, w_oth[:TOK]), "x", "y")
    out_near, out_far = gather_grid(joined(out_own, w_oth[TOK : 2 * TOK]), "y", "x")
    out_pieces = out_near + out_far

    x_near, x_far, p_rel, pt = call(
        arrange_kernel,
        (shape(2 * TOK, 3072), shape(2 * TOK, 1024), shape(2 * TOK, 2 * RANK), shape(2, RANK, TOK)),
        tokens, tokens_oth, tokens_oth_core, p_own,
        scratch=[pltpu.VMEM((2, TOK, RANK), BF16)],
        name="arrange",
    )
    total = call(
        near_kernel,
        shape(2 * TOK, HID, dtype=F32),
        x_near, p_rel, b_own, b_oth, *in_near,
        name="near",
    )
    hidden, mask = call(
        hidden_kernel,
        (shape(2 * TOK, HID), shape(2 * TOK, HID)),
        x_far, total, *in_far,
        name="hidden",
    )
    keep, send = call(
        output_kernel,
        (shape(8, ROWS, MODEL_WIDTH, dtype=F32), shape(8, ROWS, MODEL_WIDTH)),
        hidden, *out_pieces,
        name="output",
    )

    my_targets = call(
        targets_kernel, shape(ROWS, MODEL_WIDTH), targets, after=[send], name="targets"
    )

    summed = keep + partner(send, "c").astype(F32)
    away = summed[4:].astype(BF16)
    left = partner(away[:, :, :SIDE], "l")
    right = away[:, :, SIDE:]
    right = near_z(right)
    summed = summed[:4] + jnp.concatenate([left, right], axis=2).astype(F32)
    shares = lax.all_to_all(summed.astype(BF16), "h", 0, 0, tiled=True)
    share = shares.astype(F32).sum(axis=0) * FF ** (-0.5)
    grad_rows = ((share - my_targets.astype(F32)) / TOK).astype(BF16)

    q = lax.all_to_all(jnp.broadcast_to(grad_rows, (4, ROWS, MODEL_WIDTH)), "h", 0, 0, tiled=True)
    left = partner(q[:, :, :SIDE], "l")
    right = near_z(q[:, :, SIDE:])
    q_far, left_far, right_far = partner(q, "c"), partner(left, "c"), partner(right, "c")

    ups, back = call(
        backward_kernel,
        (shape(2, RANK, HID, dtype=F32), shape(2, RANK, TOK, dtype=F32)),
        q, q_far, left, left_far, right, right_far, mask, pt, b_own, b_oth, *out_pieces,
        scratch=[
            pltpu.VMEM((2 * TOK, MODEL_WIDTH), BF16),
            pltpu.VMEM((TOK, HID), BF16),
            pltpu.VMEM((TOK, HID), BF16),
        ],
        name="backward",
    )
    back = back + partner(back, "c")
    ups_arrived = partner(ups[::-1], "l")
    back = back[0] + partner(back[1], "l")
    back = [back] + [swap(back, mask) for mask in (1, 2, 3)]
    new_b, up_wire = call(
        ups_kernel,
        (shape(RANK, 2 * HID, dtype=F32), shape(2 * RANK, 2 * HID)),
        ups, ups_arrived,
        name="ups",
    )
    up_line = jnp.concatenate(ring_direct(up_wire, "x"), axis=0)
    up_grid = ring_direct(up_line, "y")
    new_a, wire = call(
        down_kernel,
        (shape(RANK, MODEL_WIDTH, dtype=F32), shape(32, RANK, BLOCK)),
        *back, tokens, a,
        name="down",
    )
    wires = lax.all_to_all(wire, REP, 0, 0, tiled=True)
    merged = call(
        merge_kernel,
        shape(TOK, 2 * HID, dtype=F32),
        wires, *up_grid, w_in,
        scratch=[pltpu.VMEM((32 * RANK, BLOCK), BF16)],
        name="merge",
    )
    return merged, new_a[None], new_b[None]


def solution(mesh):
    split = Mesh(mesh.devices.reshape(4, 2, 4, 4, 2), ("y", "l", "x", "h", "c"))
    tp = ("h", "c")
    in_specs = (
        P(REP, None),
        P(REP, None),
        P(REP, tp),
        P(tp, REP),
        P(REP, None, None),
        P(REP, None, tp),
    )
    out_specs = (P(REP, tp), P(REP, None, None), P(REP, None, tp))
    return jax.shard_map(
        shards, mesh=split, in_specs=in_specs, out_specs=out_specs, check_vma=False
    )
```

```python
import jax
import jax.numpy as jnp
from jax import lax
from jax.experimental import pallas as pl
from jax.experimental.pallas import tpu as pltpu
from jax.sharding import Mesh
from jax.sharding import PartitionSpec as P

MODEL_WIDTH = 4096
FF = 8192
TOK = 128
RANK = 16
ROWS = 16
BLOCK = 128
HALF = 64
HID = 512
SIDE = MODEL_WIDTH // 2
REP = ("y", "l", "x")
Z = ("l", "h")
ADAPTER_SCALE = 2.0
RATE_DOWN = 25.0
RATE_UP = 0.75
BF16 = jnp.bfloat16
F32 = jnp.float32

RING = (0, -1, 1, 2)


def dot(a, b):
    return jnp.dot(a, b, preferred_element_type=F32)


def dot_nt(a, b):
    return lax.dot_general(a, b, (((1,), (1,)), ((), ())), preferred_element_type=F32)


def dot_tn(a, b):
    return lax.dot_general(a, b, (((0,), (0,)), ((), ())), preferred_element_type=F32)


def shift(value, axis, by):
    n = lax.axis_size(axis)
    return lax.ppermute(value, axis, [(i, (i + by) % n) for i in range(n)])


def partner(value, axis):
    return lax.ppermute(value, axis, [(0, 1), (1, 0)])


def near_z(value):
    def place(z):
        return (z % 2) * 4 + (z % 8) // 2

    return lax.ppermute(
        value, Z, [(place(z), place(z + 1 if z % 2 else z - 1)) for z in range(8)]
    )


def call(kernel, out_shape, *args, scratch=(), after=(), stage=(), name):
    vmem = pl.BlockSpec(memory_space=pltpu.VMEM)
    wait = pl.BlockSpec(memory_space=pl.ANY)
    many = isinstance(out_shape, tuple)
    return pl.pallas_call(
        kernel,
        out_shape=out_shape,
        in_specs=[vmem] * len(args) + [wait] * (len(stage) + len(after)),
        out_specs=(vmem,) * len(out_shape) if many else vmem,
        scratch_shapes=[pltpu.VMEM(block.shape, block.dtype) for block in stage]
        + ([pltpu.SemaphoreType.DMA((len(stage),))] if stage else [])
        + list(scratch),
        name=name,
    )(*args, *stage, *after)


def staged(refs, buffers, sems):
    copies = [
        pltpu.make_async_copy(ref, buffer, sems.at[k])
        for k, (ref, buffer) in enumerate(zip(refs, buffers))
    ]
    for copy in copies:
        copy.start()
    return copies


def shape(*dims, dtype=BF16):
    return jax.ShapeDtypeStruct(dims, dtype)


def lanes(start, size):
    return pl.ds(pl.multiple_of(start, BLOCK), size)


def token_row(i):
    c = lax.axis_index("c")
    h, e = (i // 2) % 4, i % 2
    return pl.multiple_of((h * 2 + (c + e) % 2) * ROWS, ROWS)


def column(dy, side, dx):
    y, x = lax.axis_index("y"), lax.axis_index("x")
    return (((y + dy) % 4) * 8 + side * 4 + (x + dx) % 4) * BLOCK


def send_kernel(w_in_ref, w_out_ref, b_ref, send_ref):
    other = (1 - lax.axis_index("l")) * HID
    send_ref[:TOK] = w_in_ref[:, lanes(other, HID)]
    send_ref[TOK : 2 * TOK] = w_out_ref[lanes(other, HID), :].T
    send_ref[2 * TOK :] = b_ref[:, lanes(other, HID)]


def own_kernel(w_in_ref, w_out_ref, b_ref, send_ref, in_ref, out_ref, b_own_ref):
    mine = lax.axis_index("l") * HID
    in_ref[...] = w_in_ref[:, lanes(mine, HID)]
    out_ref[...] = w_out_ref[lanes(mine, HID), :].T
    b_own_ref[...] = b_ref[:, lanes(mine, HID)]


def pack_kernel(tokens_ref, a_ref, after_ref, out_ref, p_ref):
    c = lax.axis_index("c")
    p = dot_nt(a_ref[...], tokens_ref[...]).astype(BF16)
    out_ref[:HALF] = tokens_ref[pl.ds(pl.multiple_of(c * HALF, HALF), HALF), :]
    out_ref[HALF:, :TOK] = p
    p_ref[...] = p


def arrange_kernel(own_ref, oth_ref, oth_core_ref, p_own_ref, near_ref, far_ref, p_ref, pt_ref, turned_ref):
    c = lax.axis_index("c")
    p_oth = oth_ref[HALF:, :TOK]
    pt_ref[0] = p_own_ref[...]
    pt_ref[1] = p_oth
    turned_ref[0] = p_own_ref[...].astype(F32).T.astype(BF16)
    turned_ref[1] = p_oth.astype(F32).T.astype(BF16)
    near = [column(dy, side, dx) for dy in RING[:3] for dx in RING for side in range(2)]
    far = [column(RING[3], side, dx) for dx in RING for side in range(2)]
    p_ref[...] = jnp.zeros_like(p_ref)
    for i in range(16):
        here = slice(i * ROWS, (i + 1) * ROWS)
        row = token_row(i)
        lane = 0 if i < 8 else RANK
        p_ref[here, lane : lane + RANK] = turned_ref[i // 8, pl.ds(row, ROWS), :]
        half = ((i // 2) % 4) // 2
        row_oth = pl.multiple_of(row - half * HALF, ROWS)
        for ref, cols in ((near_ref, near), (far_ref, far)):
            for j, col in enumerate(cols):
                if i < 8:
                    block = own_ref[pl.ds(row, ROWS), lanes(col, BLOCK)]
                else:
                    block = jnp.where(
                        c == half,
                        oth_ref[pl.ds(row_oth, ROWS), lanes(col, BLOCK)],
                        oth_core_ref[pl.ds(row_oth, ROWS), lanes(col, BLOCK)],
                    )
                ref[here, j * BLOCK : (j + 1) * BLOCK] = block


def targets_kernel(targets_ref, after_ref, out_ref):
    h, c = lax.axis_index("h"), lax.axis_index("c")
    row = pl.multiple_of((h * 2 + c) * ROWS, ROWS)
    cols = [column(dy, side, dx) for dx in RING for dy in RING for side in range(2)]
    for j, col in enumerate(cols):
        out_ref[:, j * BLOCK : (j + 1) * BLOCK] = targets_ref[pl.ds(row, ROWS), lanes(col, BLOCK)]


def near_kernel(x_ref, p_ref, b_own_ref, b_oth_ref, *refs):
    pieces, total_ref, buffers, sems = refs[:3], refs[3], refs[4:7], refs[7]
    copies = staged(pieces, buffers, sems)
    b = jnp.concatenate([b_own_ref[...], b_oth_ref[...]], axis=0)
    total = ADAPTER_SCALE * dot(p_ref[...], b)
    for k, piece in enumerate(buffers):
        copies[k].wait()
        total = total + dot(x_ref[:, k * 1024 : (k + 1) * 1024], piece[...])
    total_ref[...] = total


def hidden_kernel(x_ref, total_ref, low_ref, high_ref, hidden_ref, mask_ref):
    total = total_ref[...]
    for k, piece in enumerate((low_ref, high_ref)):
        total = total + dot(x_ref[:, k * HID : (k + 1) * HID], piece[...])
    preact = total * MODEL_WIDTH ** (-0.5)
    hidden_ref[...] = jnp.maximum(preact, 0.0).astype(BF16)
    mask_ref[...] = jnp.where(preact > 0, 1.0, 0.0).astype(BF16)


def spans(pieces):
    begin = 0
    for piece in pieces:
        yield slice(begin, begin + piece.shape[0]), piece
        begin += piece.shape[0]


def output_kernel(hidden_ref, *refs):
    pieces, (keep_ref, send_ref), buffers, sems = refs[:5], refs[5:7], refs[7:12], refs[12]
    copies = staged(pieces, buffers, sems)
    for copy, (cols, piece) in zip(copies, spans(buffers)):
        copy.wait()
        part = dot_nt(hidden_ref[...], piece[...]).reshape(8, 2, ROWS, piece.shape[0])
        keep_ref[:, :, cols] = part[:, 0]
        send_ref[:, :, cols] = part[:, 1].astype(BF16)


def backward_kernel(q_ref, qc_ref, left_ref, leftc_ref, right_ref, rightc_ref, mask_ref, pt_ref,
                    b_own_ref, b_oth_ref, *refs):
    pieces, (up_own_ref, up_oth_ref, wire_ref, back_ref) = refs[:5], refs[5:9]
    buffers, sems, (grad_ref, own_ref, oth_ref) = refs[9:14], refs[14], refs[15:]
    copies = staged(pieces, buffers, sems)
    l = lax.axis_index("l")
    for i in range(16):
        j, e = (i // 2) % 4, i % 2
        here = slice(i * ROWS, (i + 1) * ROWS)
        if i < 8:
            grad_ref[here, :] = (q_ref, qc_ref)[e][j]
        else:
            grad_ref[here, :SIDE] = (left_ref, leftc_ref)[e][j]
            grad_ref[here, SIDE:] = (right_ref, rightc_ref)[e][j]
    total = None
    for copy, (cols, piece) in zip(copies, spans(buffers)):
        copy.wait()
        term = dot(grad_ref[:, cols], piece[...])
        total = term if total is None else total + term
    total = jnp.where(mask_ref[...].astype(F32) > 0, total * FF ** (-0.5), 0.0).astype(BF16)
    for i in range(16):
        ref = own_ref if i < 8 else oth_ref
        ref[pl.ds(token_row(i), ROWS), :] = total[i * ROWS : (i + 1) * ROWS]
    scale = ADAPTER_SCALE * MODEL_WIDTH ** (-0.5)
    sides = (
        (l, own_ref, pt_ref[0], up_own_ref, b_own_ref[...]),
        (1 - l, oth_ref, pt_ref[1], up_oth_ref, b_oth_ref[...]),
    )
    for order, (side, hid_ref, p, up_ref, b) in enumerate(sides):
        up = b.astype(F32) - RATE_UP * (scale * dot(p, hid_ref[...]))
        up_ref[...] = up
        wire_ref[side] = up.astype(BF16)
        back_ref[order] = dot_nt(b, hid_ref[...])


def down_kernel(t0_ref, t1_ref, t2_ref, t3_ref, x_ref, a_ref, new_ref, wire_ref):
    rest = (t0_ref[...] + t1_ref[...]) + (t2_ref[...] + t3_ref[...])
    parts = []
    for _ in range(3):
        parts.append(rest.astype(BF16))
        rest = rest - parts[-1].astype(F32)
    stacked = jnp.concatenate(parts, axis=0)
    scale = ADAPTER_SCALE * MODEL_WIDTH ** (-0.5)
    for k in range(8):
        here = slice(k * HID, (k + 1) * HID)
        grad = dot(stacked, x_ref[:, here])
        grad = grad[:RANK] + grad[RANK : 2 * RANK] + grad[2 * RANK :]
        new = a_ref[:, here].astype(F32) - RATE_DOWN * (scale * grad)
        new_ref[:, here] = new
        for j in range(4):
            wire_ref[k * 4 + j] = new[:, j * BLOCK : (j + 1) * BLOCK].astype(BF16)


def merge_kernel(down_ref, up_ref, w_ref, out_ref, d_ref, u_ref):
    for y in range(4):
        for x in range(4):
            for l in range(2):
                at = ((y * 4 + x) * 2 + l) * RANK
                d_ref[at : at + RANK, :] = down_ref[y * 8 + l * 4 + x]
    for side in range(2):
        for y in range(4):
            for x in range(4):
                for l in range(2):
                    at = ((y * 4 + x) * 2 + l) * RANK
                    u_ref[at : at + RANK, :] = up_ref[y * 8 + side * 4 + x, l]
        here = slice(side * HID, (side + 1) * HID)
        delta = dot_tn(d_ref[...], u_ref[...])
        out_ref[:, here] = w_ref[:, here].astype(F32) + ADAPTER_SCALE / 32 * delta


def ring(value, axis):
    below, above = shift(value, axis, 1), shift(value, axis, -1)
    return [value, below, above, shift(below, axis, 1)]


def halves_kernel(below_ref, above_ref, low_ref, high_ref, sems):
    copies = [
        pltpu.make_async_copy(below_ref.at[:HID], low_ref, sems.at[0]),
        pltpu.make_async_copy(above_ref.at[HID:], high_ref, sems.at[1]),
    ]
    for copy in copies:
        copy.start()
    for copy in copies:
        copy.wait()


def far_halves(below, above, axis):
    anywhere = pl.BlockSpec(memory_space=pl.ANY)
    low, high = pl.pallas_call(
        halves_kernel,
        out_shape=(shape(HID, HID), shape(HID, HID)),
        in_specs=[anywhere] * 2,
        out_specs=(anywhere,) * 2,
        scratch_shapes=[pltpu.SemaphoreType.DMA((2,))],
        name="halves",
    )(below, above)
    return [shift(low, axis, 1), shift(high, axis, -1)]


def swap(value, mask):
    return lax.ppermute(value, "h", [(i, i ^ mask) for i in range(4)])


def shards(tokens, targets, w_in, w_out, factor_down, factor_up):
    l = lax.axis_index("l")
    a = factor_down[0]
    b = factor_up[0]

    w_send = call(send_kernel, shape(2 * TOK + RANK, HID), w_in, w_out, b, name="send")
    w_oth = partner(w_send, "l")
    in_own, out_own, b_own = call(
        own_kernel,
        (shape(TOK, HID), shape(TOK, HID), shape(RANK, HID)),
        w_in, w_out, b, w_send,
        name="own",
    )
    b_oth = w_oth[2 * TOK :]
    packed, p_own = call(
        pack_kernel,
        (shape(HALF + RANK, MODEL_WIDTH), shape(RANK, TOK)),
        tokens, a,
        after=[in_own],
        name="pack",
    )
    tokens_oth = near_z(packed)
    tokens_oth_core = partner(tokens_oth, "c")

    def joined(own, oth):
        return jnp.where(
            l == 0, jnp.concatenate([own, oth], axis=0), jnp.concatenate([oth, own], axis=0)
        )

    in_line = jnp.concatenate(ring(joined(in_own, w_oth[:TOK]), "x"), axis=0)
    out_line = jnp.concatenate(ring(joined(out_own, w_oth[TOK : 2 * TOK]), "y"), axis=0)
    in_near = [in_line, shift(in_line, "y", 1), shift(in_line, "y", -1)]
    out_near = [out_line, shift(out_line, "x", 1), shift(out_line, "x", -1)]

    x_near, x_far, p_rel, pt = call(
        arrange_kernel,
        (shape(2 * TOK, 3072), shape(2 * TOK, 1024), shape(2 * TOK, 2 * RANK), shape(2, RANK, TOK)),
        tokens, tokens_oth, tokens_oth_core, p_own,
        scratch=[pltpu.VMEM((2, TOK, RANK), BF16)],
        name="arrange",
    )
    in_near[1], in_near[2], x_near, p_rel = lax.optimization_barrier(
        (in_near[1], in_near[2], x_near, p_rel)
    )
    in_far = far_halves(in_near[1], in_near[2], "y")
    out_far = far_halves(out_near[1], out_near[2], "x")
    out_pieces = out_near + out_far
    total = call(
        near_kernel,
        shape(2 * TOK, HID, dtype=F32),
        x_near, p_rel, b_own, b_oth,
        stage=in_near,
        name="near",
    )
    hidden, mask = call(
        hidden_kernel,
        (shape(2 * TOK, HID), shape(2 * TOK, HID)),
        x_far, total, *in_far,
        name="hidden",
    )
    keep, send = call(
        output_kernel,
        (shape(8, ROWS, MODEL_WIDTH, dtype=F32), shape(8, ROWS, MODEL_WIDTH)),
        hidden,
        stage=out_pieces,
        name="output",
    )

    my_targets = call(
        targets_kernel, shape(ROWS, MODEL_WIDTH), targets, after=[send], name="targets"
    )

    summed = keep + partner(send, "c").astype(F32)
    away = summed[4:].astype(BF16)
    left = partner(away[:, :, :SIDE], "l")
    right = away[:, :, SIDE:]
    right = near_z(right)
    summed = summed[:4] + jnp.concatenate([left, right], axis=2).astype(F32)
    shares = lax.all_to_all(summed.astype(BF16), "h", 0, 0, tiled=True)
    share = shares.astype(F32).sum(axis=0) * FF ** (-0.5)
    grad_rows = ((share - my_targets.astype(F32)) / TOK).astype(BF16)

    q = lax.all_to_all(jnp.broadcast_to(grad_rows, (4, ROWS, MODEL_WIDTH)), "h", 0, 0, tiled=True)
    left = partner(q[:, :, :SIDE], "l")
    right = near_z(q[:, :, SIDE:])
    q_far, left_far, right_far = partner(q, "c"), partner(left, "c"), partner(right, "c")

    up_own, up_oth, up_wire, back = call(
        backward_kernel,
        (
            shape(RANK, HID, dtype=F32),
            shape(RANK, HID, dtype=F32),
            shape(2, RANK, HID),
            shape(2, RANK, TOK, dtype=F32),
        ),
        q, q_far, left, left_far, right, right_far, mask, pt, b_own, b_oth,
        stage=out_pieces,
        scratch=[
            pltpu.VMEM((2 * TOK, MODEL_WIDTH), BF16),
            pltpu.VMEM((TOK, HID), BF16),
            pltpu.VMEM((TOK, HID), BF16),
        ],
        name="backward",
    )
    ups = lax.all_to_all(
        jnp.broadcast_to(up_wire, (32, 2, RANK, HID)), REP, 0, 0, tiled=True
    )
    back = back + partner(back, "c")
    back = back[0] + partner(back[1], "l")
    back = [back] + [swap(back, mask) for mask in (1, 2, 3)]
    new_a, wire = call(
        down_kernel,
        (shape(RANK, MODEL_WIDTH, dtype=F32), shape(32, RANK, BLOCK)),
        *back, tokens, a,
        name="down",
    )
    wire, ups = lax.optimization_barrier((wire, ups))
    downs = lax.all_to_all(wire, REP, 0, 0, tiled=True)
    up_arrived = partner(up_oth, "l")
    new_b = jnp.where(
        l == 0,
        jnp.concatenate([up_own, up_arrived], axis=1),
        jnp.concatenate([up_arrived, up_own], axis=1),
    )
    merged = call(
        merge_kernel,
        shape(TOK, 2 * HID, dtype=F32),
        downs, ups, w_in,
        scratch=[pltpu.VMEM((32 * RANK, BLOCK), BF16), pltpu.VMEM((32 * RANK, HID), BF16)],
        name="merge",
    )
    return merged, new_a[None], new_b[None]


def solution(mesh):
    split = Mesh(mesh.devices.reshape(4, 2, 4, 4, 2), ("y", "l", "x", "h", "c"))
    tp = ("h", "c")
    in_specs = (
        P(REP, None),
        P(REP, None),
        P(REP, tp),
        P(tp, REP),
        P(REP, None, None),
        P(REP, None, tp),
    )
    out_specs = (P(REP, tp), P(REP, None, None), P(REP, None, tp))
    return jax.shard_map(
        shards, mesh=split, in_specs=in_specs, out_specs=out_specs, check_vma=False
    )
```

```python
import jax
import jax.numpy as jnp
from jax import lax
from jax.experimental import pallas as pl
from jax.experimental.pallas import tpu as pltpu
from jax.sharding import Mesh
from jax.sharding import PartitionSpec as P

MODEL_WIDTH = 4096
FF = 8192
TOK = 128
RANK = 16
ROWS = 16
BLOCK = 128
VMEM_LIMIT = 16 * 2**20
HALF = 64
HID = 512
SIDE = MODEL_WIDTH // 2
REP = ("y", "l", "x")
Z = ("l", "h")
ADAPTER_SCALE = 2.0
RATE_DOWN = 25.0
RATE_UP = 0.75
BF16 = jnp.bfloat16
F32 = jnp.float32

RING = (0, -1, 1, 2)


def dot(a, b):
    return jnp.dot(a, b, preferred_element_type=F32)


def dot_nt(a, b):
    return lax.dot_general(a, b, (((1,), (1,)), ((), ())), preferred_element_type=F32)


def dot_tn(a, b):
    return lax.dot_general(a, b, (((0,), (0,)), ((), ())), preferred_element_type=F32)


def shift(value, axis, by):
    n = lax.axis_size(axis)
    return lax.ppermute(value, axis, [(i, (i + by) % n) for i in range(n)])


def partner(value, axis):
    return lax.ppermute(value, axis, [(0, 1), (1, 0)])


def near_z(value):
    def place(z):
        return (z % 2) * 4 + (z % 8) // 2

    return lax.ppermute(
        value, Z, [(place(z), place(z + 1 if z % 2 else z - 1)) for z in range(8)]
    )


def call(kernel, out_shape, *args, scratch=(), after=(), name):
    vmem = pl.BlockSpec(memory_space=pltpu.VMEM)
    wait = pl.BlockSpec(memory_space=pl.ANY)
    many = isinstance(out_shape, tuple)
    return pl.pallas_call(
        kernel,
        out_shape=out_shape,
        in_specs=[vmem] * len(args) + [wait] * len(after),
        out_specs=(vmem,) * len(out_shape) if many else vmem,
        scratch_shapes=scratch,
        compiler_params=pltpu.CompilerParams(vmem_limit_bytes=VMEM_LIMIT),
        name=name,
    )(*args, *after)


def shape(*dims, dtype=BF16):
    return jax.ShapeDtypeStruct(dims, dtype)


def lanes(start, size):
    return pl.ds(pl.multiple_of(start, BLOCK), size)


def token_row(i):
    c = lax.axis_index("c")
    h, e = (i // 2) % 4, i % 2
    return pl.multiple_of((h * 2 + (c + e) % 2) * ROWS, ROWS)


def column(dy, side, dx):
    y, x = lax.axis_index("y"), lax.axis_index("x")
    return (((y + dy) % 4) * 8 + side * 4 + (x + dx) % 4) * BLOCK


def send_kernel(w_in_ref, w_out_ref, b_ref, send_ref):
    other = (1 - lax.axis_index("l")) * HID
    send_ref[:TOK] = w_in_ref[:, lanes(other, HID)]
    send_ref[TOK : 2 * TOK] = w_out_ref[lanes(other, HID), :].T
    send_ref[2 * TOK :] = b_ref[:, lanes(other, HID)]


def own_kernel(w_in_ref, w_out_ref, b_ref, send_ref, in_ref, out_ref, b_own_ref):
    mine = lax.axis_index("l") * HID
    in_ref[...] = w_in_ref[:, lanes(mine, HID)]
    out_ref[...] = w_out_ref[lanes(mine, HID), :].T
    b_own_ref[...] = b_ref[:, lanes(mine, HID)]


def pack_kernel(tokens_ref, a_ref, after_ref, out_ref, p_ref):
    c = lax.axis_index("c")
    p = dot_nt(a_ref[...], tokens_ref[...]).astype(BF16)
    out_ref[:HALF] = tokens_ref[pl.ds(pl.multiple_of(c * HALF, HALF), HALF), :]
    out_ref[HALF:, :TOK] = p
    p_ref[...] = p


def arrange_kernel(own_ref, oth_ref, oth_core_ref, p_own_ref, near_ref, far_ref, p_ref, pt_ref, turned_ref):
    c = lax.axis_index("c")
    p_oth = oth_ref[HALF:, :TOK]
    pt_ref[0] = p_own_ref[...]
    pt_ref[1] = p_oth
    turned_ref[0] = p_own_ref[...].astype(F32).T.astype(BF16)
    turned_ref[1] = p_oth.astype(F32).T.astype(BF16)
    near = [column(dy, side, dx) for dy in RING[:3] for dx in RING for side in range(2)]
    far = [column(RING[3], side, dx) for dx in RING for side in range(2)]
    p_ref[...] = jnp.zeros_like(p_ref)
    for i in range(16):
        here = slice(i * ROWS, (i + 1) * ROWS)
        row = token_row(i)
        lane = 0 if i < 8 else RANK
        p_ref[here, lane : lane + RANK] = turned_ref[i // 8, pl.ds(row, ROWS), :]
        half = ((i // 2) % 4) // 2
        row_oth = pl.multiple_of(row - half * HALF, ROWS)
        for ref, cols in ((near_ref, near), (far_ref, far)):
            for j, col in enumerate(cols):
                if i < 8:
                    block = own_ref[pl.ds(row, ROWS), lanes(col, BLOCK)]
                else:
                    block = jnp.where(
                        c == half,
                        oth_ref[pl.ds(row_oth, ROWS), lanes(col, BLOCK)],
                        oth_core_ref[pl.ds(row_oth, ROWS), lanes(col, BLOCK)],
                    )
                ref[here, j * BLOCK : (j + 1) * BLOCK] = block


def targets_kernel(targets_ref, after_ref, out_ref):
    h, c = lax.axis_index("h"), lax.axis_index("c")
    row = pl.multiple_of((h * 2 + c) * ROWS, ROWS)
    cols = [column(dy, side, dx) for dx in RING for dy in RING for side in range(2)]
    for j, col in enumerate(cols):
        out_ref[:, j * BLOCK : (j + 1) * BLOCK] = targets_ref[pl.ds(row, ROWS), lanes(col, BLOCK)]


def near_kernel(x_ref, p_ref, b_own_ref, b_oth_ref, *refs):
    pieces, total_ref = refs[:3], refs[3]
    b = jnp.concatenate([b_own_ref[...], b_oth_ref[...]], axis=0)
    total = ADAPTER_SCALE * dot(p_ref[...], b)
    for k, piece in enumerate(pieces):
        total = total + dot(x_ref[:, k * 1024 : (k + 1) * 1024], piece[...])
    total_ref[...] = total


def hidden_kernel(x_ref, total_ref, low_ref, high_ref, hidden_ref, mask_ref):
    total = total_ref[...]
    for k, piece in enumerate((low_ref, high_ref)):
        total = total + dot(x_ref[:, k * HID : (k + 1) * HID], piece[...])
    preact = total * MODEL_WIDTH ** (-0.5)
    hidden_ref[...] = jnp.maximum(preact, 0.0).astype(BF16)
    mask_ref[...] = jnp.where(preact > 0, 1.0, 0.0).astype(BF16)


def spans(pieces):
    begin = 0
    for piece in pieces:
        yield slice(begin, begin + piece.shape[0]), piece
        begin += piece.shape[0]


def output_kernel(hidden_ref, *refs):
    pieces, (keep_ref, send_ref) = refs[:5], refs[5:]
    for cols, piece in spans(pieces):
        part = dot_nt(hidden_ref[...], piece[...]).reshape(8, 2, ROWS, piece.shape[0])
        keep_ref[:, :, cols] = part[:, 0]
        send_ref[:, :, cols] = part[:, 1].astype(BF16)


def backward_kernel(q_ref, qc_ref, left_ref, leftc_ref, right_ref, rightc_ref, mask_ref, pt_ref,
                    b_own_ref, b_oth_ref, *refs):
    pieces, (up_own_ref, up_oth_ref, wire_ref, back_ref, grad_ref, own_ref, oth_ref) = refs[:5], refs[5:]
    l = lax.axis_index("l")
    for i in range(16):
        j, e = (i // 2) % 4, i % 2
        here = slice(i * ROWS, (i + 1) * ROWS)
        if i < 8:
            grad_ref[here, :] = (q_ref, qc_ref)[e][j]
        else:
            grad_ref[here, :SIDE] = (left_ref, leftc_ref)[e][j]
            grad_ref[here, SIDE:] = (right_ref, rightc_ref)[e][j]
    total = None
    for cols, piece in spans(pieces):
        term = dot(grad_ref[:, cols], piece[...])
        total = term if total is None else total + term
    total = jnp.where(mask_ref[...].astype(F32) > 0, total * FF ** (-0.5), 0.0).astype(BF16)
    for i in range(16):
        ref = own_ref if i < 8 else oth_ref
        ref[pl.ds(token_row(i), ROWS), :] = total[i * ROWS : (i + 1) * ROWS]
    scale = ADAPTER_SCALE * MODEL_WIDTH ** (-0.5)
    sides = (
        (l, own_ref, pt_ref[0], up_own_ref, b_own_ref[...]),
        (1 - l, oth_ref, pt_ref[1], up_oth_ref, b_oth_ref[...]),
    )
    for order, (side, hid_ref, p, up_ref, b) in enumerate(sides):
        up = b.astype(F32) - RATE_UP * (scale * dot(p, hid_ref[...]))
        up_ref[...] = up
        wire_ref[side] = up.astype(BF16)
        back_ref[order] = dot_nt(b, hid_ref[...])


def down_kernel(t0_ref, t1_ref, t2_ref, t3_ref, x_ref, a_ref, up_ref, new_ref, wire_ref):
    rest = (t0_ref[...] + t1_ref[...]) + (t2_ref[...] + t3_ref[...])
    parts = []
    for _ in range(3):
        parts.append(rest.astype(BF16))
        rest = rest - parts[-1].astype(F32)
    stacked = jnp.concatenate(parts, axis=0)
    scale = ADAPTER_SCALE * MODEL_WIDTH ** (-0.5)
    for k in range(8):
        here = slice(k * HID, (k + 1) * HID)
        grad = dot(stacked, x_ref[:, here])
        grad = grad[:RANK] + grad[RANK : 2 * RANK] + grad[2 * RANK :]
        new = a_ref[:, here].astype(F32) - RATE_DOWN * (scale * grad)
        new_ref[:, here] = new
        for j in range(4):
            wire_ref[k * 4 + j, :, :BLOCK] = new[:, j * BLOCK : (j + 1) * BLOCK].astype(BF16)
            for l in range(2):
                begin = BLOCK + l * HID
                wire_ref[k * 4 + j, :, begin : begin + HID] = up_ref[l]


def merge_kernel(wire_ref, w_ref, out_ref, d_ref, u_ref):
    for y in range(4):
        for x in range(4):
            for l in range(2):
                at = ((y * 4 + x) * 2 + l) * RANK
                d_ref[at : at + RANK, :] = wire_ref[y * 8 + l * 4 + x, :, :BLOCK]
    for side in range(2):
        for y in range(4):
            for x in range(4):
                for l in range(2):
                    at = ((y * 4 + x) * 2 + l) * RANK
                    begin = BLOCK + l * HID
                    u_ref[at : at + RANK, :] = wire_ref[
                        y * 8 + side * 4 + x, :, begin : begin + HID
                    ]
        here = slice(side * HID, (side + 1) * HID)
        delta = dot_tn(d_ref[...], u_ref[...])
        out_ref[:, here] = w_ref[:, here].astype(F32) + ADAPTER_SCALE / 32 * delta


def ring(value, axis):
    below, above = shift(value, axis, 1), shift(value, axis, -1)
    return [value, below, above, shift(below, axis, 1)]


def halves_kernel(below_ref, above_ref, low_ref, high_ref):
    low_ref[...] = below_ref[...]
    high_ref[...] = above_ref[...]


def far_halves(below, above, axis):
    block = (HID, HID)
    first, second = pl.BlockSpec(block, lambda i: (0, 0)), pl.BlockSpec(block, lambda i: (1, 0))
    low, high = pl.pallas_call(
        halves_kernel,
        grid=(1,),
        out_shape=(shape(*block), shape(*block)),
        in_specs=[first, second],
        out_specs=(first, first),
        compiler_params=pltpu.CompilerParams(vmem_limit_bytes=VMEM_LIMIT),
        name="halves",
    )(below, above)
    return [shift(low, axis, 1), shift(high, axis, -1)]


def swap(value, mask):
    return lax.ppermute(value, "h", [(i, i ^ mask) for i in range(4)])


def shards(tokens, targets, w_in, w_out, factor_down, factor_up):
    l = lax.axis_index("l")
    a = factor_down[0]
    b = factor_up[0]

    w_send = call(send_kernel, shape(2 * TOK + RANK, HID), w_in, w_out, b, name="send")
    w_oth = partner(w_send, "l")
    in_own, out_own, b_own = call(
        own_kernel,
        (shape(TOK, HID), shape(TOK, HID), shape(RANK, HID)),
        w_in, w_out, b, w_send,
        name="own",
    )
    b_oth = w_oth[2 * TOK :]
    packed, p_own = call(
        pack_kernel,
        (shape(HALF + RANK, MODEL_WIDTH), shape(RANK, TOK)),
        tokens, a,
        after=[in_own],
        name="pack",
    )
    tokens_oth = near_z(packed)
    tokens_oth_core = partner(tokens_oth, "c")

    def joined(own, oth):
        return jnp.where(
            l == 0, jnp.concatenate([own, oth], axis=0), jnp.concatenate([oth, own], axis=0)
        )

    in_line = jnp.concatenate(ring(joined(in_own, w_oth[:TOK]), "x"), axis=0)
    out_line = jnp.concatenate(ring(joined(out_own, w_oth[TOK : 2 * TOK]), "y"), axis=0)
    in_near = [in_line, shift(in_line, "y", 1), shift(in_line, "y", -1)]
    out_near = [out_line, shift(out_line, "x", 1), shift(out_line, "x", -1)]

    x_near, x_far, p_rel, pt = call(
        arrange_kernel,
        (shape(2 * TOK, 3072), shape(2 * TOK, 1024), shape(2 * TOK, 2 * RANK), shape(2, RANK, TOK)),
        tokens, tokens_oth, tokens_oth_core, p_own,
        scratch=[pltpu.VMEM((2, TOK, RANK), BF16)],
        name="arrange",
    )
    in_near[1], in_near[2], x_near, p_rel = lax.optimization_barrier(
        (in_near[1], in_near[2], x_near, p_rel)
    )
    in_far = far_halves(in_near[1], in_near[2], "y")
    out_far = far_halves(out_near[1], out_near[2], "x")
    out_pieces = out_near + out_far
    total = call(
        near_kernel,
        shape(2 * TOK, HID, dtype=F32),
        x_near, p_rel, b_own, b_oth, *in_near,
        name="near",
    )
    hidden, mask = call(
        hidden_kernel,
        (shape(2 * TOK, HID), shape(2 * TOK, HID)),
        x_far, total, *in_far,
        name="hidden",
    )
    keep, send = call(
        output_kernel,
        (shape(8, ROWS, MODEL_WIDTH, dtype=F32), shape(8, ROWS, MODEL_WIDTH)),
        hidden, *out_pieces,
        name="output",
    )

    my_targets = call(
        targets_kernel, shape(ROWS, MODEL_WIDTH), targets, after=[p_rel], name="targets"
    )

    summed = keep + partner(send, "c").astype(F32)
    away = summed[4:].astype(BF16)
    left = partner(away[:, :, :SIDE], "l")
    right = away[:, :, SIDE:]
    right = near_z(right)
    summed = summed[:4] + jnp.concatenate([left, right], axis=2).astype(F32)
    shares = lax.all_to_all(summed.astype(BF16), "h", 0, 0, tiled=True)
    share = shares.astype(F32).sum(axis=0) * FF ** (-0.5)
    grad_rows = ((share - my_targets.astype(F32)) / TOK).astype(BF16)

    q = lax.all_to_all(jnp.broadcast_to(grad_rows, (4, ROWS, MODEL_WIDTH)), "h", 0, 0, tiled=True)
    left = partner(q[:, :, :SIDE], "l")
    right = near_z(q[:, :, SIDE:])
    q_far, left_far, right_far = partner(q, "c"), partner(left, "c"), partner(right, "c")

    up_own, up_oth, up_wire, back = call(
        backward_kernel,
        (
            shape(RANK, HID, dtype=F32),
            shape(RANK, HID, dtype=F32),
            shape(2, RANK, HID),
            shape(2, RANK, TOK, dtype=F32),
        ),
        q, q_far, left, left_far, right, right_far, mask, pt, b_own, b_oth, *out_pieces,
        scratch=[
            pltpu.VMEM((2 * TOK, MODEL_WIDTH), BF16),
            pltpu.VMEM((TOK, HID), BF16),
            pltpu.VMEM((TOK, HID), BF16),
        ],
        name="backward",
    )
    back = back + partner(back, "c")
    back = back[0] + partner(back[1], "l")
    back = [back] + [swap(back, mask) for mask in (1, 2, 3)]
    new_a, wire = call(
        down_kernel,
        (shape(RANK, MODEL_WIDTH, dtype=F32), shape(32, RANK, BLOCK + 2 * HID)),
        *back, tokens, a, up_wire,
        name="down",
    )
    wires = lax.all_to_all(wire, REP, 0, 0, tiled=True)
    up_arrived = partner(up_oth, "l")
    new_b = jnp.where(
        l == 0,
        jnp.concatenate([up_own, up_arrived], axis=1),
        jnp.concatenate([up_arrived, up_own], axis=1),
    )
    merged = call(
        merge_kernel,
        shape(TOK, 2 * HID, dtype=F32),
        wires, w_in,
        scratch=[pltpu.VMEM((32 * RANK, BLOCK), BF16), pltpu.VMEM((32 * RANK, HID), BF16)],
        name="merge",
    )
    return merged, new_a[None], new_b[None]


def solution(mesh):
    split = Mesh(mesh.devices.reshape(4, 2, 4, 4, 2), ("y", "l", "x", "h", "c"))
    tp = ("h", "c")
    in_specs = (
        P(REP, None),
        P(REP, None),
        P(REP, tp),
        P(tp, REP),
        P(REP, None, None),
        P(REP, None, tp),
    )
    out_specs = (P(REP, tp), P(REP, None, None), P(REP, None, tp))
    return jax.shard_map(
        shards, mesh=split, in_specs=in_specs, out_specs=out_specs, check_vma=False
    )
```

```python
import jax
import jax.numpy as jnp
from jax import lax
from jax.experimental import pallas as pl
from jax.experimental.pallas import tpu as pltpu
from jax.sharding import Mesh
from jax.sharding import PartitionSpec as P

MODEL_WIDTH = 4096
FF = 8192
TOK = 128
RANK = 16
ROWS = 16
BLOCK = 128
VMEM_LIMIT = 16 * 2**20
HALF = 64
HID = 512
SIDE = MODEL_WIDTH // 2
REP = ("y", "l", "x")
Z = ("l", "h")
ADAPTER_SCALE = 2.0
RATE_DOWN = 25.0
RATE_UP = 0.75
BF16 = jnp.bfloat16
F32 = jnp.float32

RING = (0, -1, 1, 2)


def dot(a, b):
    return jnp.dot(a, b, preferred_element_type=F32)


def dot_nt(a, b):
    return lax.dot_general(a, b, (((1,), (1,)), ((), ())), preferred_element_type=F32)


def dot_tn(a, b):
    return lax.dot_general(a, b, (((0,), (0,)), ((), ())), preferred_element_type=F32)


def shift(value, axis, by):
    n = lax.axis_size(axis)
    return lax.ppermute(value, axis, [(i, (i + by) % n) for i in range(n)])


def partner(value, axis):
    return lax.ppermute(value, axis, [(0, 1), (1, 0)])


def near_z(value):
    def place(z):
        return (z % 2) * 4 + (z % 8) // 2

    return lax.ppermute(
        value, Z, [(place(z), place(z + 1 if z % 2 else z - 1)) for z in range(8)]
    )


def call(kernel, out_shape, *args, scratch=(), after=(), name):
    vmem = pl.BlockSpec(memory_space=pltpu.VMEM)
    wait = pl.BlockSpec(memory_space=pl.ANY)
    many = isinstance(out_shape, tuple)
    return pl.pallas_call(
        kernel,
        out_shape=out_shape,
        in_specs=[vmem] * len(args) + [wait] * len(after),
        out_specs=(vmem,) * len(out_shape) if many else vmem,
        scratch_shapes=scratch,
        compiler_params=pltpu.CompilerParams(vmem_limit_bytes=VMEM_LIMIT),
        name=name,
    )(*args, *after)


def shape(*dims, dtype=BF16):
    return jax.ShapeDtypeStruct(dims, dtype)


def lanes(start, size):
    return pl.ds(pl.multiple_of(start, BLOCK), size)


def token_row(i):
    c = lax.axis_index("c")
    h, e = (i // 2) % 4, i % 2
    return pl.multiple_of((h * 2 + (c + e) % 2) * ROWS, ROWS)


def column(dy, side, dx):
    y, x = lax.axis_index("y"), lax.axis_index("x")
    return (((y + dy) % 4) * 8 + side * 4 + (x + dx) % 4) * BLOCK


def send_kernel(w_in_ref, w_out_ref, b_ref, send_ref):
    other = (1 - lax.axis_index("l")) * HID
    send_ref[:TOK] = w_in_ref[:, lanes(other, HID)]
    send_ref[TOK : 2 * TOK] = w_out_ref[lanes(other, HID), :].T
    send_ref[2 * TOK :] = b_ref[:, lanes(other, HID)]


def own_kernel(w_in_ref, w_out_ref, b_ref, send_ref, in_ref, out_ref, b_own_ref):
    mine = lax.axis_index("l") * HID
    in_ref[...] = w_in_ref[:, lanes(mine, HID)]
    out_ref[...] = w_out_ref[lanes(mine, HID), :].T
    b_own_ref[...] = b_ref[:, lanes(mine, HID)]


def pack_kernel(tokens_ref, a_ref, out_ref, p_ref):
    c = lax.axis_index("c")
    p = dot_nt(a_ref[...], tokens_ref[...]).astype(BF16)
    out_ref[:HALF] = tokens_ref[pl.ds(pl.multiple_of(c * HALF, HALF), HALF), :]
    out_ref[HALF:, :TOK] = p
    p_ref[...] = p


def arrange_kernel(own_ref, oth_ref, oth_core_ref, p_own_ref, near_ref, far_ref, p_ref, pt_ref, turned_ref):
    c = lax.axis_index("c")
    p_oth = oth_ref[HALF:, :TOK]
    pt_ref[0] = p_own_ref[...]
    pt_ref[1] = p_oth
    turned_ref[0] = p_own_ref[...].astype(F32).T.astype(BF16)
    turned_ref[1] = p_oth.astype(F32).T.astype(BF16)
    near = [column(dy, side, dx) for dy in RING[:3] for dx in RING for side in range(2)]
    far = [column(RING[3], side, dx) for dx in RING for side in range(2)]
    p_ref[...] = jnp.zeros_like(p_ref)
    for i in range(16):
        here = slice(i * ROWS, (i + 1) * ROWS)
        row = token_row(i)
        lane = 0 if i < 8 else RANK
        p_ref[here, lane : lane + RANK] = turned_ref[i // 8, pl.ds(row, ROWS), :]
        half = ((i // 2) % 4) // 2
        row_oth = pl.multiple_of(row - half * HALF, ROWS)
        for ref, cols in ((near_ref, near), (far_ref, far)):
            for j, col in enumerate(cols):
                if i < 8:
                    block = own_ref[pl.ds(row, ROWS), lanes(col, BLOCK)]
                else:
                    block = jnp.where(
                        c == half,
                        oth_ref[pl.ds(row_oth, ROWS), lanes(col, BLOCK)],
                        oth_core_ref[pl.ds(row_oth, ROWS), lanes(col, BLOCK)],
                    )
                ref[here, j * BLOCK : (j + 1) * BLOCK] = block


def targets_kernel(targets_ref, after_ref, out_ref):
    h, c = lax.axis_index("h"), lax.axis_index("c")
    row = pl.multiple_of((h * 2 + c) * ROWS, ROWS)
    cols = [column(dy, side, dx) for dx in RING for dy in RING for side in range(2)]
    for j, col in enumerate(cols):
        out_ref[:, j * BLOCK : (j + 1) * BLOCK] = targets_ref[pl.ds(row, ROWS), lanes(col, BLOCK)]


def near_kernel(x_ref, p_ref, b_own_ref, b_oth_ref, *refs):
    pieces, total_ref = refs[:3], refs[3]
    b = jnp.concatenate([b_own_ref[...], b_oth_ref[...]], axis=0)
    total = ADAPTER_SCALE * dot(p_ref[...], b)
    for k, piece in enumerate(pieces):
        total = total + dot(x_ref[:, k * 1024 : (k + 1) * 1024], piece[...])
    total_ref[...] = total


def hidden_kernel(x_ref, total_ref, low_ref, high_ref, hidden_ref, mask_ref):
    total = total_ref[...]
    for k, piece in enumerate((low_ref, high_ref)):
        total = total + dot(x_ref[:, k * HID : (k + 1) * HID], piece[...])
    preact = total * MODEL_WIDTH ** (-0.5)
    hidden_ref[...] = jnp.maximum(preact, 0.0).astype(BF16)
    mask_ref[...] = jnp.where(preact > 0, 1.0, 0.0).astype(BF16)


def spans(pieces):
    begin = 0
    for piece in pieces:
        yield slice(begin, begin + piece.shape[0]), piece
        begin += piece.shape[0]


def output_kernel(hidden_ref, *refs):
    pieces, (keep_ref, send_ref) = refs[:5], refs[5:]
    for cols, piece in spans(pieces):
        part = dot_nt(hidden_ref[...], piece[...]).reshape(8, 2, ROWS, piece.shape[0])
        keep_ref[:, :, cols] = part[:, 0]
        send_ref[:, :, cols] = part[:, 1].astype(BF16)


def backward_kernel(q_ref, qc_ref, left_ref, leftc_ref, right_ref, rightc_ref, mask_ref, pt_ref,
                    b_own_ref, b_oth_ref, *refs):
    pieces, (up_own_ref, up_oth_ref, wire_ref, back_ref, grad_ref, own_ref, oth_ref) = refs[:5], refs[5:]
    l = lax.axis_index("l")
    for i in range(16):
        j, e = (i // 2) % 4, i % 2
        here = slice(i * ROWS, (i + 1) * ROWS)
        if i < 8:
            grad_ref[here, :] = (q_ref, qc_ref)[e][j]
        else:
            grad_ref[here, :SIDE] = (left_ref, leftc_ref)[e][j]
            grad_ref[here, SIDE:] = (right_ref, rightc_ref)[e][j]
    total = None
    for cols, piece in spans(pieces):
        term = dot(grad_ref[:, cols], piece[...])
        total = term if total is None else total + term
    total = jnp.where(mask_ref[...].astype(F32) > 0, total * FF ** (-0.5), 0.0).astype(BF16)
    for i in range(16):
        ref = own_ref if i < 8 else oth_ref
        ref[pl.ds(token_row(i), ROWS), :] = total[i * ROWS : (i + 1) * ROWS]
    scale = ADAPTER_SCALE * MODEL_WIDTH ** (-0.5)
    sides = (
        (l, own_ref, pt_ref[0], up_own_ref, b_own_ref[...]),
        (1 - l, oth_ref, pt_ref[1], up_oth_ref, b_oth_ref[...]),
    )
    for order, (side, hid_ref, p, up_ref, b) in enumerate(sides):
        up = b.astype(F32) - RATE_UP * (scale * dot(p, hid_ref[...]))
        up_ref[...] = up
        wire_ref[side] = up.astype(BF16)
        back_ref[order] = dot_nt(b, hid_ref[...])


def route_kernel(near_ref, left_ref, right_ref, mine_ref, s1_ref, s2_ref, s3_ref):
    h = lax.axis_index("h")
    for j, ref in enumerate((mine_ref, s1_ref, s2_ref, s3_ref)):
        k = (h + j) % 4
        ref[:, :SIDE] = (near_ref[k, :, :SIDE] + left_ref[k].astype(F32)).astype(ref.dtype)
        ref[:, SIDE:] = (near_ref[k, :, SIDE:] + right_ref[k].astype(F32)).astype(ref.dtype)


def down_kernel(t0_ref, t1_ref, t2_ref, t3_ref, x_ref, a_ref, up_ref, new_ref, wire_ref):
    rest = (t0_ref[...] + t1_ref[...]) + (t2_ref[...] + t3_ref[...])
    parts = []
    for _ in range(3):
        parts.append(rest.astype(BF16))
        rest = rest - parts[-1].astype(F32)
    stacked = jnp.concatenate(parts, axis=0)
    scale = ADAPTER_SCALE * MODEL_WIDTH ** (-0.5)
    for k in range(8):
        here = slice(k * HID, (k + 1) * HID)
        grad = dot(stacked, x_ref[:, here])
        grad = grad[:RANK] + grad[RANK : 2 * RANK] + grad[2 * RANK :]
        new = a_ref[:, here].astype(F32) - RATE_DOWN * (scale * grad)
        new_ref[:, here] = new
        for j in range(4):
            wire_ref[k * 4 + j, :, :BLOCK] = new[:, j * BLOCK : (j + 1) * BLOCK].astype(BF16)
            for l in range(2):
                begin = BLOCK + l * HID
                wire_ref[k * 4 + j, :, begin : begin + HID] = up_ref[l]


def merge_kernel(wire_ref, w_ref, out_ref, d_ref, u_ref):
    for y in range(4):
        for x in range(4):
            for l in range(2):
                at = ((y * 4 + x) * 2 + l) * RANK
                d_ref[at : at + RANK, :] = wire_ref[y * 8 + l * 4 + x, :, :BLOCK]
    for side in range(2):
        for y in range(4):
            for x in range(4):
                for l in range(2):
                    at = ((y * 4 + x) * 2 + l) * RANK
                    begin = BLOCK + l * HID
                    u_ref[at : at + RANK, :] = wire_ref[
                        y * 8 + side * 4 + x, :, begin : begin + HID
                    ]
        here = slice(side * HID, (side + 1) * HID)
        delta = dot_tn(d_ref[...], u_ref[...])
        out_ref[:, here] = w_ref[:, here].astype(F32) + ADAPTER_SCALE / 32 * delta


def ring(value, axis):
    below, above = shift(value, axis, 1), shift(value, axis, -1)
    return [value, below, above, shift(below, axis, 1)]


def halves_kernel(below_ref, above_ref, low_ref, high_ref):
    low_ref[...] = below_ref[...]
    high_ref[...] = above_ref[...]


def far_halves(below, above, axis):
    block = (HID, HID)
    first, second = pl.BlockSpec(block, lambda i: (0, 0)), pl.BlockSpec(block, lambda i: (1, 0))
    low, high = pl.pallas_call(
        halves_kernel,
        grid=(1,),
        out_shape=(shape(*block), shape(*block)),
        in_specs=[first, second],
        out_specs=(first, first),
        compiler_params=pltpu.CompilerParams(vmem_limit_bytes=VMEM_LIMIT),
        name="halves",
    )(below, above)
    return [shift(low, axis, 1), shift(high, axis, -1)]


def swap(value, mask):
    return lax.ppermute(value, "h", [(i, i ^ mask) for i in range(4)])


def shards(tokens, targets, w_in, w_out, factor_down, factor_up):
    l = lax.axis_index("l")
    a = factor_down[0]
    b = factor_up[0]

    w_send = call(send_kernel, shape(2 * TOK + RANK, HID), w_in, w_out, b, name="send")
    w_oth = partner(w_send, "l")
    in_own, out_own, b_own = call(
        own_kernel,
        (shape(TOK, HID), shape(TOK, HID), shape(RANK, HID)),
        w_in, w_out, b, w_send,
        name="own",
    )
    b_oth = w_oth[2 * TOK :]
    def line(own, oth, axis):
        pairs = list(zip(ring(own, axis), ring(oth, axis)))
        return jnp.where(
            l == 0,
            jnp.concatenate([block for o, t in pairs for block in (o, t)], axis=0),
            jnp.concatenate([block for o, t in pairs for block in (t, o)], axis=0),
        )

    in_line = line(in_own, w_oth[:TOK], "x")
    out_line = line(out_own, w_oth[TOK : 2 * TOK], "y")
    late_tokens, in_line = lax.optimization_barrier((tokens, in_line))
    packed, p_own = call(
        pack_kernel,
        (shape(HALF + RANK, MODEL_WIDTH), shape(RANK, TOK)),
        late_tokens, a,
        name="pack",
    )
    tokens_oth = near_z(packed)
    tokens_oth_core = partner(tokens_oth, "c")

    in_near = [in_line, shift(in_line, "y", 1), shift(in_line, "y", -1)]
    out_near = [out_line, shift(out_line, "x", 1), shift(out_line, "x", -1)]

    x_near, x_far, p_rel, pt = call(
        arrange_kernel,
        (shape(2 * TOK, 3072), shape(2 * TOK, 1024), shape(2 * TOK, 2 * RANK), shape(2, RANK, TOK)),
        tokens, tokens_oth, tokens_oth_core, p_own,
        scratch=[pltpu.VMEM((2, TOK, RANK), BF16)],
        name="arrange",
    )
    in_near[1], in_near[2], x_near, p_rel = lax.optimization_barrier(
        (in_near[1], in_near[2], x_near, p_rel)
    )
    in_far = far_halves(in_near[1], in_near[2], "y")
    out_far = far_halves(out_near[1], out_near[2], "x")
    out_pieces = out_near + out_far
    total = call(
        near_kernel,
        shape(2 * TOK, HID, dtype=F32),
        x_near, p_rel, b_own, b_oth, *in_near,
        name="near",
    )
    hidden, mask = call(
        hidden_kernel,
        (shape(2 * TOK, HID), shape(2 * TOK, HID)),
        x_far, total, *in_far,
        name="hidden",
    )
    keep, send = call(
        output_kernel,
        (shape(8, ROWS, MODEL_WIDTH, dtype=F32), shape(8, ROWS, MODEL_WIDTH)),
        hidden, *out_pieces,
        name="output",
    )

    my_targets = call(
        targets_kernel, shape(ROWS, MODEL_WIDTH), targets, after=[p_rel], name="targets"
    )

    summed = keep + partner(send, "c").astype(F32)
    away = summed[4:].astype(BF16)
    left = partner(away[:, :, :SIDE], "l")
    right = away[:, :, SIDE:]
    right = near_z(right)
    mine, *steps = call(
        route_kernel,
        (shape(ROWS, MODEL_WIDTH, dtype=F32),) + (shape(ROWS, MODEL_WIDTH),) * 3,
        summed[:4], left, right,
        name="route",
    )
    steps = [shift(step, "h", j + 1).astype(F32) for j, step in enumerate(steps)]
    share = ((mine + steps[0]) + (steps[1] + steps[2])) * FF ** (-0.5)
    grad_rows = ((share - my_targets.astype(F32)) / TOK).astype(BF16)

    q = lax.all_to_all(jnp.broadcast_to(grad_rows, (4, ROWS, MODEL_WIDTH)), "h", 0, 0, tiled=True)
    left = partner(q[:, :, :SIDE], "l")
    right = near_z(q[:, :, SIDE:])
    q_far, left_far, right_far = partner(q, "c"), partner(left, "c"), partner(right, "c")

    up_own, up_oth, up_wire, back = call(
        backward_kernel,
        (
            shape(RANK, HID, dtype=F32),
            shape(RANK, HID, dtype=F32),
            shape(2, RANK, HID),
            shape(2, RANK, TOK, dtype=F32),
        ),
        q, q_far, left, left_far, right, right_far, mask, pt, b_own, b_oth, *out_pieces,
        scratch=[
            pltpu.VMEM((2 * TOK, MODEL_WIDTH), BF16),
            pltpu.VMEM((TOK, HID), BF16),
            pltpu.VMEM((TOK, HID), BF16),
        ],
        name="backward",
    )
    back = back + partner(back, "c")
    back = back[0] + partner(back[1], "l")
    back = [back] + [swap(back, mask) for mask in (1, 2, 3)]
    new_a, wire = call(
        down_kernel,
        (shape(RANK, MODEL_WIDTH, dtype=F32), shape(32, RANK, BLOCK + 2 * HID)),
        *back, tokens, a, up_wire,
        name="down",
    )
    wires = lax.all_to_all(wire, REP, 0, 0, tiled=True)
    up_arrived = partner(up_oth, "l")
    new_b = jnp.where(
        l == 0,
        jnp.concatenate([up_own, up_arrived], axis=1),
        jnp.concatenate([up_arrived, up_own], axis=1),
    )
    merged = call(
        merge_kernel,
        shape(TOK, 2 * HID, dtype=F32),
        wires, w_in,
        scratch=[pltpu.VMEM((32 * RANK, BLOCK), BF16), pltpu.VMEM((32 * RANK, HID), BF16)],
        name="merge",
    )
    return merged, new_a[None], new_b[None]


def solution(mesh):
    split = Mesh(mesh.devices.reshape(4, 2, 4, 4, 2), ("y", "l", "x", "h", "c"))
    tp = ("h", "c")
    in_specs = (
        P(REP, None),
        P(REP, None),
        P(REP, tp),
        P(tp, REP),
        P(REP, None, None),
        P(REP, None, tp),
    )
    out_specs = (P(REP, tp), P(REP, None, None), P(REP, None, tp))
    return jax.shard_map(
        shards, mesh=split, in_specs=in_specs, out_specs=out_specs, check_vma=False
    )
```

```python
import jax
import jax.numpy as jnp
from jax import lax
from jax.experimental import pallas as pl
from jax.experimental.pallas import tpu as pltpu
from jax.sharding import Mesh
from jax.sharding import PartitionSpec as P

MODEL_WIDTH = 4096
FF = 8192
TOK = 128
RANK = 16
ROWS = 16
BLOCK = 128
VMEM_LIMIT = 16 * 2**20
HALF = 64
HID = 512
SIDE = MODEL_WIDTH // 2
REP = ("y", "l", "x")
Z = ("l", "h")
ADAPTER_SCALE = 2.0
RATE_DOWN = 25.0
RATE_UP = 0.75
BF16 = jnp.bfloat16
F32 = jnp.float32

RING = (0, -1, 1, 2)


def dot(a, b):
    return jnp.dot(a, b, preferred_element_type=F32)


def dot_nt(a, b):
    return lax.dot_general(a, b, (((1,), (1,)), ((), ())), preferred_element_type=F32)


def dot_tn(a, b):
    return lax.dot_general(a, b, (((0,), (0,)), ((), ())), preferred_element_type=F32)


def shift(value, axis, by):
    n = lax.axis_size(axis)
    return lax.ppermute(value, axis, [(i, (i + by) % n) for i in range(n)])


def partner(value, axis):
    return lax.ppermute(value, axis, [(0, 1), (1, 0)])


def near_z(value):
    def place(z):
        return (z % 2) * 4 + (z % 8) // 2

    return lax.ppermute(
        value, Z, [(place(z), place(z + 1 if z % 2 else z - 1)) for z in range(8)]
    )


def call(kernel, out_shape, *args, scratch=(), after=(), name):
    vmem = pl.BlockSpec(memory_space=pltpu.VMEM)
    wait = pl.BlockSpec(memory_space=pl.ANY)
    many = isinstance(out_shape, tuple)
    return pl.pallas_call(
        kernel,
        out_shape=out_shape,
        in_specs=[vmem] * len(args) + [wait] * len(after),
        out_specs=(vmem,) * len(out_shape) if many else vmem,
        scratch_shapes=scratch,
        compiler_params=pltpu.CompilerParams(vmem_limit_bytes=VMEM_LIMIT),
        name=name,
    )(*args, *after)


def shape(*dims, dtype=BF16):
    return jax.ShapeDtypeStruct(dims, dtype)


def lanes(start, size):
    return pl.ds(pl.multiple_of(start, BLOCK), size)


def token_row(i):
    c = lax.axis_index("c")
    h, e = (i // 2) % 4, i % 2
    return pl.multiple_of((h * 2 + (c + e) % 2) * ROWS, ROWS)


def column(dy, side, dx):
    y, x = lax.axis_index("y"), lax.axis_index("x")
    return (((y + dy) % 4) * 8 + side * 4 + (x + dx) % 4) * BLOCK


def send_kernel(w_in_ref, w_out_ref, b_ref, send_ref):
    other = (1 - lax.axis_index("l")) * HID
    send_ref[:TOK] = w_in_ref[:, lanes(other, HID)]
    send_ref[TOK : 2 * TOK] = w_out_ref[lanes(other, HID), :].T
    send_ref[2 * TOK :] = b_ref[:, lanes(other, HID)]


def own_kernel(w_in_ref, w_out_ref, b_ref, send_ref, in_ref, out_ref, b_own_ref):
    mine = lax.axis_index("l") * HID
    in_ref[...] = w_in_ref[:, lanes(mine, HID)]
    out_ref[...] = w_out_ref[lanes(mine, HID), :].T
    b_own_ref[...] = b_ref[:, lanes(mine, HID)]


def pack_kernel(tokens_ref, a_ref, after_ref, out_ref, p_ref):
    c = lax.axis_index("c")
    p = dot_nt(a_ref[...], tokens_ref[...]).astype(BF16)
    out_ref[:HALF] = tokens_ref[pl.ds(pl.multiple_of(c * HALF, HALF), HALF), :]
    out_ref[HALF:, :TOK] = p
    p_ref[...] = p


def arrange_kernel(own_ref, oth_ref, oth_core_ref, p_own_ref, near_ref, far_ref, p_ref, pt_ref, turned_ref):
    c = lax.axis_index("c")
    p_oth = oth_ref[HALF:, :TOK]
    pt_ref[0] = p_own_ref[...]
    pt_ref[1] = p_oth
    turned_ref[0] = p_own_ref[...].astype(F32).T.astype(BF16)
    turned_ref[1] = p_oth.astype(F32).T.astype(BF16)
    near = [column(dy, side, dx) for dy in RING[:3] for dx in RING for side in range(2)]
    far = [column(RING[3], side, dx) for dx in RING for side in range(2)]
    p_ref[...] = jnp.zeros_like(p_ref)
    for i in range(16):
        here = slice(i * ROWS, (i + 1) * ROWS)
        row = token_row(i)
        lane = 0 if i < 8 else RANK
        p_ref[here, lane : lane + RANK] = turned_ref[i // 8, pl.ds(row, ROWS), :]
        half = ((i // 2) % 4) // 2
        row_oth = pl.multiple_of(row - half * HALF, ROWS)
        for ref, cols in ((near_ref, near), (far_ref, far)):
            for j, col in enumerate(cols):
                if i < 8:
                    block = own_ref[pl.ds(row, ROWS), lanes(col, BLOCK)]
                else:
                    block = jnp.where(
                        c == half,
                        oth_ref[pl.ds(row_oth, ROWS), lanes(col, BLOCK)],
                        oth_core_ref[pl.ds(row_oth, ROWS), lanes(col, BLOCK)],
                    )
                ref[here, j * BLOCK : (j + 1) * BLOCK] = block


def targets_kernel(targets_ref, after_ref, out_ref):
    h, c = lax.axis_index("h"), lax.axis_index("c")
    row = pl.multiple_of((h * 2 + c) * ROWS, ROWS)
    cols = [column(dy, side, dx) for dx in RING for dy in RING for side in range(2)]
    for j, col in enumerate(cols):
        out_ref[:, j * BLOCK : (j + 1) * BLOCK] = targets_ref[pl.ds(row, ROWS), lanes(col, BLOCK)]


def near_kernel(x_ref, p_ref, b_own_ref, b_oth_ref, *refs):
    pieces, total_ref = refs[:3], refs[3]
    b = jnp.concatenate([b_own_ref[...], b_oth_ref[...]], axis=0)
    total = ADAPTER_SCALE * dot(p_ref[...], b)
    for k, piece in enumerate(pieces):
        total = total + dot(x_ref[:, k * 1024 : (k + 1) * 1024], piece[...])
    total_ref[...] = total


def hidden_kernel(x_ref, total_ref, low_ref, high_ref, hidden_ref, mask_ref):
    total = total_ref[...]
    for k, piece in enumerate((low_ref, high_ref)):
        total = total + dot(x_ref[:, k * HID : (k + 1) * HID], piece[...])
    preact = total * MODEL_WIDTH ** (-0.5)
    hidden_ref[...] = jnp.maximum(preact, 0.0).astype(BF16)
    mask_ref[...] = jnp.where(preact > 0, 1.0, 0.0).astype(BF16)


def spans(pieces):
    begin = 0
    for piece in pieces:
        yield slice(begin, begin + piece.shape[0]), piece
        begin += piece.shape[0]


def output_kernel(hidden_ref, *refs):
    pieces, (keep_ref, send_ref) = refs[:5], refs[5:]
    for cols, piece in spans(pieces):
        part = dot_nt(hidden_ref[...], piece[...]).reshape(8, 2, ROWS, piece.shape[0])
        keep_ref[:, :, cols] = part[:, 0]
        send_ref[:, :, cols] = part[:, 1].astype(BF16)


def backward_kernel(q_ref, qc_ref, left_ref, leftc_ref, right_ref, rightc_ref, mask_ref, pt_ref,
                    b_own_ref, b_oth_ref, *refs):
    pieces, (up_own_ref, up_oth_ref, wire_ref, back_ref, grad_ref, own_ref, oth_ref) = refs[:5], refs[5:]
    l = lax.axis_index("l")
    for i in range(16):
        j, e = (i // 2) % 4, i % 2
        here = slice(i * ROWS, (i + 1) * ROWS)
        if i < 8:
            grad_ref[here, :] = (q_ref, qc_ref)[e][j]
        else:
            grad_ref[here, :SIDE] = (left_ref, leftc_ref)[e][j]
            grad_ref[here, SIDE:] = (right_ref, rightc_ref)[e][j]
    total = None
    for cols, piece in spans(pieces):
        term = dot(grad_ref[:, cols], piece[...])
        total = term if total is None else total + term
    total = jnp.where(mask_ref[...].astype(F32) > 0, total * FF ** (-0.5), 0.0).astype(BF16)
    for i in range(16):
        ref = own_ref if i < 8 else oth_ref
        ref[pl.ds(token_row(i), ROWS), :] = total[i * ROWS : (i + 1) * ROWS]
    scale = ADAPTER_SCALE * MODEL_WIDTH ** (-0.5)
    sides = (
        (l, own_ref, pt_ref[0], up_own_ref, b_own_ref[...]),
        (1 - l, oth_ref, pt_ref[1], up_oth_ref, b_oth_ref[...]),
    )
    for order, (side, hid_ref, p, up_ref, b) in enumerate(sides):
        up = b.astype(F32) - RATE_UP * (scale * dot(p, hid_ref[...]))
        up_ref[...] = up
        wire_ref[side] = up.astype(BF16)
        back_ref[order] = dot_nt(b, hid_ref[...])


def route_kernel(near_ref, left_ref, right_ref, mine_ref, s1_ref, s2_ref, s3_ref):
    h = lax.axis_index("h")
    for j, ref in enumerate((mine_ref, s1_ref, s2_ref, s3_ref)):
        k = (h + j) % 4
        ref[:, :SIDE] = (near_ref[k, :, :SIDE] + left_ref[k].astype(F32)).astype(ref.dtype)
        ref[:, SIDE:] = (near_ref[k, :, SIDE:] + right_ref[k].astype(F32)).astype(ref.dtype)


def down_kernel(t0_ref, t1_ref, t2_ref, t3_ref, x_ref, a_ref, up_ref, new_ref, wire_ref):
    rest = (t0_ref[...] + t1_ref[...]) + (t2_ref[...] + t3_ref[...])
    parts = []
    for _ in range(3):
        parts.append(rest.astype(BF16))
        rest = rest - parts[-1].astype(F32)
    stacked = jnp.concatenate(parts, axis=0)
    scale = ADAPTER_SCALE * MODEL_WIDTH ** (-0.5)
    for k in range(8):
        here = slice(k * HID, (k + 1) * HID)
        grad = dot(stacked, x_ref[:, here])
        grad = grad[:RANK] + grad[RANK : 2 * RANK] + grad[2 * RANK :]
        new = a_ref[:, here].astype(F32) - RATE_DOWN * (scale * grad)
        new_ref[:, here] = new
        for j in range(4):
            wire_ref[k * 4 + j, :, :BLOCK] = new[:, j * BLOCK : (j + 1) * BLOCK].astype(BF16)
            for l in range(2):
                begin = BLOCK + l * HID
                wire_ref[k * 4 + j, :, begin : begin + HID] = up_ref[l]


def merge_kernel(wire_ref, w_ref, out_ref, d_ref, u_ref):
    for y in range(4):
        for x in range(4):
            for l in range(2):
                at = ((y * 4 + x) * 2 + l) * RANK
                d_ref[at : at + RANK, :] = wire_ref[y * 8 + l * 4 + x, :, :BLOCK]
    for side in range(2):
        for y in range(4):
            for x in range(4):
                for l in range(2):
                    at = ((y * 4 + x) * 2 + l) * RANK
                    begin = BLOCK + l * HID
                    u_ref[at : at + RANK, :] = wire_ref[
                        y * 8 + side * 4 + x, :, begin : begin + HID
                    ]
        here = slice(side * HID, (side + 1) * HID)
        delta = dot_tn(d_ref[...], u_ref[...])
        out_ref[:, here] = w_ref[:, here].astype(F32) + ADAPTER_SCALE / 32 * delta


def ring(value, axis):
    below, above = shift(value, axis, 1), shift(value, axis, -1)
    return [value, below, above, shift(below, axis, 1)]


def halves_kernel(below_ref, above_ref, low_ref, high_ref):
    low_ref[...] = below_ref[...]
    high_ref[...] = above_ref[...]


def far_halves(below, above, axis):
    block = (HID, HID)
    first, second = pl.BlockSpec(block, lambda i: (0, 0)), pl.BlockSpec(block, lambda i: (1, 0))
    low, high = pl.pallas_call(
        halves_kernel,
        grid=(1,),
        out_shape=(shape(*block), shape(*block)),
        in_specs=[first, second],
        out_specs=(first, first),
        compiler_params=pltpu.CompilerParams(vmem_limit_bytes=VMEM_LIMIT),
        name="halves",
    )(below, above)
    return [shift(low, axis, 1), shift(high, axis, -1)]


def swap(value, mask):
    return lax.ppermute(value, "h", [(i, i ^ mask) for i in range(4)])


def shards(tokens, targets, w_in, w_out, factor_down, factor_up):
    l = lax.axis_index("l")
    a = factor_down[0]
    b = factor_up[0]

    w_send = call(send_kernel, shape(2 * TOK + RANK, HID), w_in, w_out, b, name="send")
    w_oth = partner(w_send, "l")
    in_own, out_own, b_own = call(
        own_kernel,
        (shape(TOK, HID), shape(TOK, HID), shape(RANK, HID)),
        w_in, w_out, b, w_send,
        name="own",
    )
    b_oth = w_oth[2 * TOK :]
    packed, p_own = call(
        pack_kernel,
        (shape(HALF + RANK, MODEL_WIDTH), shape(RANK, TOK)),
        tokens, a,
        after=[in_own],
        name="pack",
    )
    tokens_oth = near_z(packed)
    tokens_oth_core = partner(tokens_oth, "c")

    def joined(own, oth):
        return jnp.where(
            l == 0, jnp.concatenate([own, oth], axis=0), jnp.concatenate([oth, own], axis=0)
        )

    in_line = jnp.concatenate(ring(joined(in_own, w_oth[:TOK]), "x"), axis=0)
    out_line = jnp.concatenate(ring(joined(out_own, w_oth[TOK : 2 * TOK]), "y"), axis=0)
    in_near = [in_line, shift(in_line, "y", 1), shift(in_line, "y", -1)]
    out_near = [out_line, shift(out_line, "x", 1), shift(out_line, "x", -1)]

    x_near, x_far, p_rel, pt = call(
        arrange_kernel,
        (shape(2 * TOK, 3072), shape(2 * TOK, 1024), shape(2 * TOK, 2 * RANK), shape(2, RANK, TOK)),
        tokens, tokens_oth, tokens_oth_core, p_own,
        scratch=[pltpu.VMEM((2, TOK, RANK), BF16)],
        name="arrange",
    )
    in_near[1], in_near[2], x_near, p_rel = lax.optimization_barrier(
        (in_near[1], in_near[2], x_near, p_rel)
    )
    in_far = far_halves(in_near[1], in_near[2], "y")
    out_far = far_halves(out_near[1], out_near[2], "x")
    out_pieces = out_near + out_far
    total = call(
        near_kernel,
        shape(2 * TOK, HID, dtype=F32),
        x_near, p_rel, b_own, b_oth, *in_near,
        name="near",
    )
    hidden, mask = call(
        hidden_kernel,
        (shape(2 * TOK, HID), shape(2 * TOK, HID)),
        x_far, total, *in_far,
        name="hidden",
    )
    keep, send = call(
        output_kernel,
        (shape(8, ROWS, MODEL_WIDTH, dtype=F32), shape(8, ROWS, MODEL_WIDTH)),
        hidden, *out_pieces,
        name="output",
    )

    my_targets = call(
        targets_kernel, shape(ROWS, MODEL_WIDTH), targets, after=[p_rel], name="targets"
    )

    summed = keep + partner(send, "c").astype(F32)
    away = summed[4:].astype(BF16)
    left = partner(away[:, :, :SIDE], "l")
    right = away[:, :, SIDE:]
    right = near_z(right)
    mine, *steps = call(
        route_kernel,
        (shape(ROWS, MODEL_WIDTH, dtype=F32),) + (shape(ROWS, MODEL_WIDTH),) * 3,
        summed[:4], left, right,
        name="route",
    )
    steps = [shift(step, "h", j + 1).astype(F32) for j, step in enumerate(steps)]
    share = ((mine + steps[0]) + (steps[1] + steps[2])) * FF ** (-0.5)
    grad_rows = ((share - my_targets.astype(F32)) / TOK).astype(BF16)

    q = lax.all_to_all(jnp.broadcast_to(grad_rows, (4, ROWS, MODEL_WIDTH)), "h", 0, 0, tiled=True)
    left = partner(q[:, :, :SIDE], "l")
    right = near_z(q[:, :, SIDE:])
    q_far, left_far, right_far = partner(q, "c"), partner(left, "c"), partner(right, "c")

    up_own, up_oth, up_wire, back = call(
        backward_kernel,
        (
            shape(RANK, HID, dtype=F32),
            shape(RANK, HID, dtype=F32),
            shape(2, RANK, HID),
            shape(2, RANK, TOK, dtype=F32),
        ),
        q, q_far, left, left_far, right, right_far, mask, pt, b_own, b_oth, *out_pieces,
        scratch=[
            pltpu.VMEM((2 * TOK, MODEL_WIDTH), BF16),
            pltpu.VMEM((TOK, HID), BF16),
            pltpu.VMEM((TOK, HID), BF16),
        ],
        name="backward",
    )
    back = back + partner(back, "c")
    back = back[0] + partner(back[1], "l")
    back = [back] + [swap(back, mask) for mask in (1, 2, 3)]
    new_a, wire = call(
        down_kernel,
        (shape(RANK, MODEL_WIDTH, dtype=F32), shape(32, RANK, BLOCK + 2 * HID)),
        *back, tokens, a, up_wire,
        name="down",
    )
    wires = lax.all_to_all(wire, REP, 0, 0, tiled=True)
    up_arrived = partner(up_oth, "l")
    new_b = jnp.where(
        l == 0,
        jnp.concatenate([up_own, up_arrived], axis=1),
        jnp.concatenate([up_arrived, up_own], axis=1),
    )
    merged = call(
        merge_kernel,
        shape(TOK, 2 * HID, dtype=F32),
        wires, w_in,
        scratch=[pltpu.VMEM((32 * RANK, BLOCK), BF16), pltpu.VMEM((32 * RANK, HID), BF16)],
        name="merge",
    )
    return merged, new_a[None], new_b[None]


def solution(mesh):
    split = Mesh(mesh.devices.reshape(4, 2, 4, 4, 2), ("y", "l", "x", "h", "c"))
    tp = ("h", "c")
    in_specs = (
        P(REP, None),
        P(REP, None),
        P(REP, tp),
        P(tp, REP),
        P(REP, None, None),
        P(REP, None, tp),
    )
    out_specs = (P(REP, tp), P(REP, None, None), P(REP, None, tp))
    return jax.shard_map(
        shards, mesh=split, in_specs=in_specs, out_specs=out_specs, check_vma=False
    )
```

```python
import jax
import jax.numpy as jnp
from jax import lax
from jax.experimental import pallas as pl
from jax.experimental.pallas import tpu as pltpu
from jax.sharding import Mesh
from jax.sharding import PartitionSpec as P

MODEL_WIDTH = 4096
FF = 8192
TOK = 128
RANK = 16
ROWS = 16
BLOCK = 128
VMEM_LIMIT = 16 * 2**20
HALF = 64
HID = 512
SIDE = MODEL_WIDTH // 2
REP = ("y", "l", "x")
Z = ("l", "h")
ADAPTER_SCALE = 2.0
RATE_DOWN = 25.0
RATE_UP = 0.75
BF16 = jnp.bfloat16
F32 = jnp.float32

RING = (0, -1, 1, 2)


def dot(a, b):
    return jnp.dot(a, b, preferred_element_type=F32)


def dot_nt(a, b):
    return lax.dot_general(a, b, (((1,), (1,)), ((), ())), preferred_element_type=F32)


def dot_tn(a, b):
    return lax.dot_general(a, b, (((0,), (0,)), ((), ())), preferred_element_type=F32)


def shift(value, axis, by):
    n = lax.axis_size(axis)
    return lax.ppermute(value, axis, [(i, (i + by) % n) for i in range(n)])


def partner(value, axis):
    return lax.ppermute(value, axis, [(0, 1), (1, 0)])


def near_z(value):
    def place(z):
        return (z % 2) * 4 + (z % 8) // 2

    return lax.ppermute(
        value, Z, [(place(z), place(z + 1 if z % 2 else z - 1)) for z in range(8)]
    )


def call(kernel, out_shape, *args, scratch=(), after=(), name):
    vmem = pl.BlockSpec(memory_space=pltpu.VMEM)
    wait = pl.BlockSpec(memory_space=pl.ANY)
    many = isinstance(out_shape, tuple)
    return pl.pallas_call(
        kernel,
        out_shape=out_shape,
        in_specs=[vmem] * len(args) + [wait] * len(after),
        out_specs=(vmem,) * len(out_shape) if many else vmem,
        scratch_shapes=scratch,
        compiler_params=pltpu.CompilerParams(vmem_limit_bytes=VMEM_LIMIT),
        name=name,
    )(*args, *after)


def shape(*dims, dtype=BF16):
    return jax.ShapeDtypeStruct(dims, dtype)


def lanes(start, size):
    return pl.ds(pl.multiple_of(start, BLOCK), size)


def token_row(i):
    c = lax.axis_index("c")
    h, e = (i // 2) % 4, i % 2
    return pl.multiple_of((h * 2 + (c + e) % 2) * ROWS, ROWS)


def column(dy, side, dx):
    y, x = lax.axis_index("y"), lax.axis_index("x")
    return (((y + dy) % 4) * 8 + side * 4 + (x + dx) % 4) * BLOCK


def send_kernel(w_in_ref, w_out_ref, b_ref, send_ref):
    other = (1 - lax.axis_index("l")) * HID
    send_ref[:TOK] = w_in_ref[:, lanes(other, HID)]
    send_ref[TOK : 2 * TOK] = w_out_ref[lanes(other, HID), :].T
    send_ref[2 * TOK :] = b_ref[:, lanes(other, HID)]


def own_kernel(w_in_ref, w_out_ref, b_ref, send_ref, in_ref, out_ref, b_own_ref):
    mine = lax.axis_index("l") * HID
    in_ref[...] = w_in_ref[:, lanes(mine, HID)]
    out_ref[...] = w_out_ref[lanes(mine, HID), :].T
    b_own_ref[...] = b_ref[:, lanes(mine, HID)]


def pack_kernel(tokens_ref, a_ref, after_ref, out_ref, p_ref):
    c = lax.axis_index("c")
    p = dot_nt(a_ref[...], tokens_ref[...]).astype(BF16)
    out_ref[:HALF] = tokens_ref[pl.ds(pl.multiple_of(c * HALF, HALF), HALF), :]
    out_ref[HALF:, :TOK] = p
    p_ref[...] = p


def arrange_kernel(own_ref, oth_ref, oth_core_ref, p_own_ref, near_ref, far_ref, p_ref, pt_ref, turned_ref):
    c = lax.axis_index("c")
    p_oth = oth_ref[HALF:, :TOK]
    pt_ref[0] = p_own_ref[...]
    pt_ref[1] = p_oth
    turned_ref[0] = p_own_ref[...].astype(F32).T.astype(BF16)
    turned_ref[1] = p_oth.astype(F32).T.astype(BF16)
    near = [column(dy, side, dx) for dy in RING[:3] for dx in RING for side in range(2)]
    far = [column(RING[3], side, dx) for dx in RING for side in range(2)]
    p_ref[...] = jnp.zeros_like(p_ref)
    for i in range(16):
        here = slice(i * ROWS, (i + 1) * ROWS)
        row = token_row(i)
        lane = 0 if i < 8 else RANK
        p_ref[here, lane : lane + RANK] = turned_ref[i // 8, pl.ds(row, ROWS), :]
        half = ((i // 2) % 4) // 2
        row_oth = pl.multiple_of(row - half * HALF, ROWS)
        for ref, cols in ((near_ref, near), (far_ref, far)):
            for j, col in enumerate(cols):
                if i < 8:
                    block = own_ref[pl.ds(row, ROWS), lanes(col, BLOCK)]
                else:
                    block = jnp.where(
                        c == half,
                        oth_ref[pl.ds(row_oth, ROWS), lanes(col, BLOCK)],
                        oth_core_ref[pl.ds(row_oth, ROWS), lanes(col, BLOCK)],
                    )
                ref[here, j * BLOCK : (j + 1) * BLOCK] = block


def targets_kernel(targets_ref, after_ref, out_ref):
    h, c = lax.axis_index("h"), lax.axis_index("c")
    row = pl.multiple_of((h * 2 + c) * ROWS, ROWS)
    cols = [column(dy, side, dx) for dx in RING for dy in RING for side in range(2)]
    for j, col in enumerate(cols):
        out_ref[:, j * BLOCK : (j + 1) * BLOCK] = targets_ref[pl.ds(row, ROWS), lanes(col, BLOCK)]


def near_kernel(x_ref, p_ref, b_own_ref, b_oth_ref, *refs):
    pieces, total_ref = refs[:3], refs[3]
    b = jnp.concatenate([b_own_ref[...], b_oth_ref[...]], axis=0)
    total = ADAPTER_SCALE * dot(p_ref[...], b)
    for k, piece in enumerate(pieces):
        total = total + dot(x_ref[:, k * 1024 : (k + 1) * 1024], piece[...])
    total_ref[...] = total


def hidden_kernel(x_ref, total_ref, low_ref, high_ref, hidden_ref, mask_ref):
    total = total_ref[...]
    for k, piece in enumerate((low_ref, high_ref)):
        total = total + dot(x_ref[:, k * HID : (k + 1) * HID], piece[...])
    preact = total * MODEL_WIDTH ** (-0.5)
    hidden_ref[...] = jnp.maximum(preact, 0.0).astype(BF16)
    mask_ref[...] = jnp.where(preact > 0, 1.0, 0.0).astype(BF16)


def spans(pieces):
    begin = 0
    for piece in pieces:
        yield slice(begin, begin + piece.shape[0]), piece
        begin += piece.shape[0]


def output_kernel(hidden_ref, *refs):
    pieces, (keep_ref, send_ref) = refs[:5], refs[5:]
    for cols, piece in spans(pieces):
        part = dot_nt(hidden_ref[...], piece[...]).reshape(8, 2, ROWS, piece.shape[0])
        keep_ref[:, :, cols] = part[:, 0]
        send_ref[:, :, cols] = part[:, 1].astype(BF16)


def backward_kernel(q_ref, qc_ref, left_ref, leftc_ref, right_ref, rightc_ref, mask_ref, pt_ref,
                    b_own_ref, b_oth_ref, *refs):
    pieces, (up_own_ref, up_oth_ref, wire_ref, back_ref, grad_ref, own_ref, oth_ref) = refs[:5], refs[5:]
    l = lax.axis_index("l")
    h = lax.axis_index("h")
    for i in range(16):
        j, e = (i // 2) % 4, i % 2
        here = slice(i * ROWS, (i + 1) * ROWS)
        if i < 8:
            grad_ref[here, :] = (q_ref, qc_ref)[e][(j + 4 - h) % 4]
        else:
            grad_ref[here, :SIDE] = (left_ref, leftc_ref)[e][(j + 4 - h) % 4]
            grad_ref[here, SIDE:] = (right_ref, rightc_ref)[e][(j + 5 - h + 2 * l) % 4]
    total = None
    for cols, piece in spans(pieces):
        term = dot(grad_ref[:, cols], piece[...])
        total = term if total is None else total + term
    total = jnp.where(mask_ref[...].astype(F32) > 0, total * FF ** (-0.5), 0.0).astype(BF16)
    for i in range(16):
        ref = own_ref if i < 8 else oth_ref
        ref[pl.ds(token_row(i), ROWS), :] = total[i * ROWS : (i + 1) * ROWS]
    scale = ADAPTER_SCALE * MODEL_WIDTH ** (-0.5)
    sides = (
        (l, own_ref, pt_ref[0], up_own_ref, b_own_ref[...]),
        (1 - l, oth_ref, pt_ref[1], up_oth_ref, b_oth_ref[...]),
    )
    for order, (side, hid_ref, p, up_ref, b) in enumerate(sides):
        up = b.astype(F32) - RATE_UP * (scale * dot(p, hid_ref[...]))
        up_ref[...] = up
        wire_ref[side] = up.astype(BF16)
        back_ref[order] = dot_nt(b, hid_ref[...])


def route_kernel(near_ref, left_ref, right_ref, mine_ref, s1_ref, s2_ref, s3_ref):
    h = lax.axis_index("h")
    for j, ref in enumerate((mine_ref, s1_ref, s2_ref, s3_ref)):
        k = (h + j) % 4
        ref[:, :SIDE] = (near_ref[k, :, :SIDE] + left_ref[k].astype(F32)).astype(ref.dtype)
        ref[:, SIDE:] = (near_ref[k, :, SIDE:] + right_ref[k].astype(F32)).astype(ref.dtype)


def down_kernel(t0_ref, t1_ref, t2_ref, t3_ref, x_ref, a_ref, up_ref, new_ref, wire_ref):
    rest = (t0_ref[...] + t1_ref[...]) + (t2_ref[...] + t3_ref[...])
    parts = []
    for _ in range(3):
        parts.append(rest.astype(BF16))
        rest = rest - parts[-1].astype(F32)
    stacked = jnp.concatenate(parts, axis=0)
    scale = ADAPTER_SCALE * MODEL_WIDTH ** (-0.5)
    for k in range(8):
        here = slice(k * HID, (k + 1) * HID)
        grad = dot(stacked, x_ref[:, here])
        grad = grad[:RANK] + grad[RANK : 2 * RANK] + grad[2 * RANK :]
        new = a_ref[:, here].astype(F32) - RATE_DOWN * (scale * grad)
        new_ref[:, here] = new
        for j in range(4):
            wire_ref[k * 4 + j, :, :BLOCK] = new[:, j * BLOCK : (j + 1) * BLOCK].astype(BF16)
            for l in range(2):
                begin = BLOCK + l * HID
                wire_ref[k * 4 + j, :, begin : begin + HID] = up_ref[l]


def merge_kernel(wire_ref, w_ref, out_ref, d_ref, u_ref):
    for y in range(4):
        for x in range(4):
            for l in range(2):
                at = ((y * 4 + x) * 2 + l) * RANK
                d_ref[at : at + RANK, :] = wire_ref[y * 8 + l * 4 + x, :, :BLOCK]
    for side in range(2):
        for y in range(4):
            for x in range(4):
                for l in range(2):
                    at = ((y * 4 + x) * 2 + l) * RANK
                    begin = BLOCK + l * HID
                    u_ref[at : at + RANK, :] = wire_ref[
                        y * 8 + side * 4 + x, :, begin : begin + HID
                    ]
        here = slice(side * HID, (side + 1) * HID)
        delta = dot_tn(d_ref[...], u_ref[...])
        out_ref[:, here] = w_ref[:, here].astype(F32) + ADAPTER_SCALE / 32 * delta


def ring(value, axis):
    below, above = shift(value, axis, 1), shift(value, axis, -1)
    return [value, below, above, shift(below, axis, 1)]


def halves_kernel(below_ref, above_ref, low_ref, high_ref):
    low_ref[...] = below_ref[...]
    high_ref[...] = above_ref[...]


def far_halves(below, above, axis):
    block = (HID, HID)
    first, second = pl.BlockSpec(block, lambda i: (0, 0)), pl.BlockSpec(block, lambda i: (1, 0))
    low, high = pl.pallas_call(
        halves_kernel,
        grid=(1,),
        out_shape=(shape(*block), shape(*block)),
        in_specs=[first, second],
        out_specs=(first, first),
        compiler_params=pltpu.CompilerParams(vmem_limit_bytes=VMEM_LIMIT),
        name="halves",
    )(below, above)
    return [shift(low, axis, 1), shift(high, axis, -1)]


def swap(value, mask):
    return lax.ppermute(value, "h", [(i, i ^ mask) for i in range(4)])


def shards(tokens, targets, w_in, w_out, factor_down, factor_up):
    l = lax.axis_index("l")
    a = factor_down[0]
    b = factor_up[0]

    w_send = call(send_kernel, shape(2 * TOK + RANK, HID), w_in, w_out, b, name="send")
    w_oth = partner(w_send, "l")
    in_own, out_own, b_own = call(
        own_kernel,
        (shape(TOK, HID), shape(TOK, HID), shape(RANK, HID)),
        w_in, w_out, b, w_send,
        name="own",
    )
    b_oth = w_oth[2 * TOK :]
    packed, p_own = call(
        pack_kernel,
        (shape(HALF + RANK, MODEL_WIDTH), shape(RANK, TOK)),
        tokens, a,
        after=[in_own],
        name="pack",
    )
    tokens_oth = near_z(packed)
    tokens_oth_core = partner(tokens_oth, "c")

    def joined(own, oth):
        return jnp.where(
            l == 0, jnp.concatenate([own, oth], axis=0), jnp.concatenate([oth, own], axis=0)
        )

    in_line = jnp.concatenate(ring(joined(in_own, w_oth[:TOK]), "x"), axis=0)
    out_line = jnp.concatenate(ring(joined(out_own, w_oth[TOK : 2 * TOK]), "y"), axis=0)
    in_near = [in_line, shift(in_line, "y", 1), shift(in_line, "y", -1)]
    out_near = [out_line, shift(out_line, "x", 1), shift(out_line, "x", -1)]

    x_near, x_far, p_rel, pt = call(
        arrange_kernel,
        (shape(2 * TOK, 3072), shape(2 * TOK, 1024), shape(2 * TOK, 2 * RANK), shape(2, RANK, TOK)),
        tokens, tokens_oth, tokens_oth_core, p_own,
        scratch=[pltpu.VMEM((2, TOK, RANK), BF16)],
        name="arrange",
    )
    in_near[1], in_near[2], x_near, p_rel = lax.optimization_barrier(
        (in_near[1], in_near[2], x_near, p_rel)
    )
    in_far = far_halves(in_near[1], in_near[2], "y")
    out_far = far_halves(out_near[1], out_near[2], "x")
    out_pieces = out_near + out_far
    total = call(
        near_kernel,
        shape(2 * TOK, HID, dtype=F32),
        x_near, p_rel, b_own, b_oth, *in_near,
        name="near",
    )
    hidden, mask = call(
        hidden_kernel,
        (shape(2 * TOK, HID), shape(2 * TOK, HID)),
        x_far, total, *in_far,
        name="hidden",
    )
    keep, send = call(
        output_kernel,
        (shape(8, ROWS, MODEL_WIDTH, dtype=F32), shape(8, ROWS, MODEL_WIDTH)),
        hidden, *out_pieces,
        name="output",
    )

    my_targets = call(
        targets_kernel, shape(ROWS, MODEL_WIDTH), targets, after=[p_rel], name="targets"
    )

    summed = keep + partner(send, "c").astype(F32)
    away = summed[4:].astype(BF16)
    left = partner(away[:, :, :SIDE], "l")
    right = away[:, :, SIDE:]
    right = near_z(right)
    mine, *steps = call(
        route_kernel,
        (shape(ROWS, MODEL_WIDTH, dtype=F32),) + (shape(ROWS, MODEL_WIDTH),) * 3,
        summed[:4], left, right,
        name="route",
    )
    steps = [shift(step, "h", j + 1).astype(F32) for j, step in enumerate(steps)]
    share = ((mine + steps[0]) + (steps[1] + steps[2])) * FF ** (-0.5)
    grad_rows = ((share - my_targets.astype(F32)) / TOK).astype(BF16)

    q = jnp.stack([grad_rows] + [shift(grad_rows, "h", -j) for j in (1, 2, 3)])
    left = partner(q[:, :, :SIDE], "l")
    right = near_z(q[:, :, SIDE:])
    q_far, left_far, right_far = partner(q, "c"), partner(left, "c"), partner(right, "c")

    up_own, up_oth, up_wire, back = call(
        backward_kernel,
        (
            shape(RANK, HID, dtype=F32),
            shape(RANK, HID, dtype=F32),
            shape(2, RANK, HID),
            shape(2, RANK, TOK, dtype=F32),
        ),
        q, q_far, left, left_far, right, right_far, mask, pt, b_own, b_oth, *out_pieces,
        scratch=[
            pltpu.VMEM((2 * TOK, MODEL_WIDTH), BF16),
            pltpu.VMEM((TOK, HID), BF16),
            pltpu.VMEM((TOK, HID), BF16),
        ],
        name="backward",
    )
    back = back + partner(back, "c")
    back = back[0] + partner(back[1], "l")
    back = [back] + [swap(back, mask) for mask in (1, 2, 3)]
    new_a, wire = call(
        down_kernel,
        (shape(RANK, MODEL_WIDTH, dtype=F32), shape(32, RANK, BLOCK + 2 * HID)),
        *back, tokens, a, up_wire,
        name="down",
    )
    wires = lax.all_to_all(wire, REP, 0, 0, tiled=True)
    up_arrived = partner(up_oth, "l")
    new_b = jnp.where(
        l == 0,
        jnp.concatenate([up_own, up_arrived], axis=1),
        jnp.concatenate([up_arrived, up_own], axis=1),
    )
    merged = call(
        merge_kernel,
        shape(TOK, 2 * HID, dtype=F32),
        wires, w_in,
        scratch=[pltpu.VMEM((32 * RANK, BLOCK), BF16), pltpu.VMEM((32 * RANK, HID), BF16)],
        name="merge",
    )
    return merged, new_a[None], new_b[None]


def solution(mesh):
    split = Mesh(mesh.devices.reshape(4, 2, 4, 4, 2), ("y", "l", "x", "h", "c"))
    tp = ("h", "c")
    in_specs = (
        P(REP, None),
        P(REP, None),
        P(REP, tp),
        P(tp, REP),
        P(REP, None, None),
        P(REP, None, tp),
    )
    out_specs = (P(REP, tp), P(REP, None, None), P(REP, None, tp))
    return jax.shard_map(
        shards, mesh=split, in_specs=in_specs, out_specs=out_specs, check_vma=False
    )
```

```python
import jax
import jax.numpy as jnp
from jax import lax
from jax.experimental import pallas as pl
from jax.experimental.pallas import tpu as pltpu
from jax.sharding import Mesh
from jax.sharding import PartitionSpec as P

MODEL_WIDTH = 4096
FF = 8192
TOK = 128
RANK = 16
ROWS = 16
BLOCK = 128
VMEM_LIMIT = 16 * 2**20
HALF = 64
HID = 512
SIDE = MODEL_WIDTH // 2
REP = ("y", "l", "x")
Z = ("l", "h")
ADAPTER_SCALE = 2.0
RATE_DOWN = 25.0
RATE_UP = 0.75
BF16 = jnp.bfloat16
F32 = jnp.float32

RING = (0, -1, 1, 2)


def dot(a, b):
    return jnp.dot(a, b, preferred_element_type=F32)


def dot_nt(a, b):
    return lax.dot_general(a, b, (((1,), (1,)), ((), ())), preferred_element_type=F32)


def dot_tn(a, b):
    return lax.dot_general(a, b, (((0,), (0,)), ((), ())), preferred_element_type=F32)


def shift(value, axis, by):
    n = lax.axis_size(axis)
    return lax.ppermute(value, axis, [(i, (i + by) % n) for i in range(n)])


def partner(value, axis):
    return lax.ppermute(value, axis, [(0, 1), (1, 0)])


def near_z(value):
    def place(z):
        return (z % 2) * 4 + (z % 8) // 2

    return lax.ppermute(
        value, Z, [(place(z), place(z + 1 if z % 2 else z - 1)) for z in range(8)]
    )


def call(kernel, out_shape, *args, scratch=(), after=(), name):
    vmem = pl.BlockSpec(memory_space=pltpu.VMEM)
    wait = pl.BlockSpec(memory_space=pl.ANY)
    many = isinstance(out_shape, tuple)
    return pl.pallas_call(
        kernel,
        out_shape=out_shape,
        in_specs=[vmem] * len(args) + [wait] * len(after),
        out_specs=(vmem,) * len(out_shape) if many else vmem,
        scratch_shapes=scratch,
        compiler_params=pltpu.CompilerParams(vmem_limit_bytes=VMEM_LIMIT),
        name=name,
    )(*args, *after)


def shape(*dims, dtype=BF16):
    return jax.ShapeDtypeStruct(dims, dtype)


def lanes(start, size):
    return pl.ds(pl.multiple_of(start, BLOCK), size)


def token_row(i):
    c = lax.axis_index("c")
    h, e = (i // 2) % 4, i % 2
    return pl.multiple_of((h * 2 + (c + e) % 2) * ROWS, ROWS)


def column(dy, side, dx):
    y, x = lax.axis_index("y"), lax.axis_index("x")
    return (((y + dy) % 4) * 8 + side * 4 + (x + dx) % 4) * BLOCK


def send_kernel(w_in_ref, w_out_ref, b_ref, in_ref, out_ref):
    other = (1 - lax.axis_index("l")) * HID
    in_ref[...] = w_in_ref[:, lanes(other, HID)]
    out_ref[:TOK] = w_out_ref[lanes(other, HID), :].T
    out_ref[TOK:] = b_ref[:, lanes(other, HID)]


def own_kernel(w_in_ref, w_out_ref, b_ref, send_ref, in_ref, out_ref, b_own_ref):
    mine = lax.axis_index("l") * HID
    in_ref[...] = w_in_ref[:, lanes(mine, HID)]
    out_ref[...] = w_out_ref[lanes(mine, HID), :].T
    b_own_ref[...] = b_ref[:, lanes(mine, HID)]


def pack_kernel(tokens_ref, a_ref, after_ref, out_ref, p_ref):
    c = lax.axis_index("c")
    p = dot_nt(a_ref[...], tokens_ref[...]).astype(BF16)
    out_ref[:HALF] = tokens_ref[pl.ds(pl.multiple_of(c * HALF, HALF), HALF), :]
    out_ref[HALF:, :TOK] = p
    p_ref[...] = p


def arrange_kernel(own_ref, oth_ref, oth_core_ref, p_own_ref, near_ref, far_ref, p_ref, pt_ref, turned_ref):
    c = lax.axis_index("c")
    p_oth = oth_ref[HALF:, :TOK]
    pt_ref[0] = p_own_ref[...]
    pt_ref[1] = p_oth
    turned_ref[0] = p_own_ref[...].astype(F32).T.astype(BF16)
    turned_ref[1] = p_oth.astype(F32).T.astype(BF16)
    near = [column(dy, side, dx) for dy in RING[:3] for dx in RING for side in range(2)]
    far = [column(RING[3], side, dx) for dx in RING for side in range(2)]
    p_ref[...] = jnp.zeros_like(p_ref)
    for i in range(16):
        here = slice(i * ROWS, (i + 1) * ROWS)
        row = token_row(i)
        lane = 0 if i < 8 else RANK
        p_ref[here, lane : lane + RANK] = turned_ref[i // 8, pl.ds(row, ROWS), :]
        half = ((i // 2) % 4) // 2
        row_oth = pl.multiple_of(row - half * HALF, ROWS)
        for ref, cols in ((near_ref, near), (far_ref, far)):
            for j, col in enumerate(cols):
                if i < 8:
                    block = own_ref[pl.ds(row, ROWS), lanes(col, BLOCK)]
                else:
                    block = jnp.where(
                        c == half,
                        oth_ref[pl.ds(row_oth, ROWS), lanes(col, BLOCK)],
                        oth_core_ref[pl.ds(row_oth, ROWS), lanes(col, BLOCK)],
                    )
                ref[here, j * BLOCK : (j + 1) * BLOCK] = block


def targets_kernel(targets_ref, after_ref, out_ref):
    h, c = lax.axis_index("h"), lax.axis_index("c")
    row = pl.multiple_of((h * 2 + c) * ROWS, ROWS)
    cols = [column(dy, side, dx) for dx in RING for dy in RING for side in range(2)]
    for j, col in enumerate(cols):
        out_ref[:, j * BLOCK : (j + 1) * BLOCK] = targets_ref[pl.ds(row, ROWS), lanes(col, BLOCK)]


def near_kernel(x_ref, p_ref, b_own_ref, b_oth_ref, *refs):
    pieces, total_ref = refs[:3], refs[3]
    b = jnp.concatenate([b_own_ref[...], b_oth_ref[...]], axis=0)
    total = ADAPTER_SCALE * dot(p_ref[...], b)
    for k, piece in enumerate(pieces):
        total = total + dot(x_ref[:, k * 1024 : (k + 1) * 1024], piece[...])
    total_ref[...] = total


def hidden_kernel(x_ref, total_ref, low_ref, high_ref, hidden_ref, mask_ref):
    total = total_ref[...]
    for k, piece in enumerate((low_ref, high_ref)):
        total = total + dot(x_ref[:, k * HID : (k + 1) * HID], piece[...])
    preact = total * MODEL_WIDTH ** (-0.5)
    hidden_ref[...] = jnp.maximum(preact, 0.0).astype(BF16)
    mask_ref[...] = jnp.where(preact > 0, 1.0, 0.0).astype(BF16)


def spans(pieces):
    begin = 0
    for piece in pieces:
        yield slice(begin, begin + piece.shape[0]), piece
        begin += piece.shape[0]


def output_kernel(hidden_ref, *refs):
    pieces, (keep_ref, send_ref) = refs[:5], refs[5:]
    for cols, piece in spans(pieces):
        part = dot_nt(hidden_ref[...], piece[...]).reshape(8, 2, ROWS, piece.shape[0])
        keep_ref[:, :, cols] = part[:, 0]
        send_ref[:, :, cols] = part[:, 1].astype(BF16)


def backward_kernel(q_ref, qc_ref, left_ref, leftc_ref, right_ref, rightc_ref, mask_ref, pt_ref,
                    b_own_ref, b_oth_ref, *refs):
    pieces, (up_own_ref, up_oth_ref, wire_ref, back_ref, grad_ref, own_ref, oth_ref) = refs[:5], refs[5:]
    l = lax.axis_index("l")
    h = lax.axis_index("h")
    for i in range(16):
        j, e = (i // 2) % 4, i % 2
        here = slice(i * ROWS, (i + 1) * ROWS)
        if i < 8:
            grad_ref[here, :] = (q_ref, qc_ref)[e][(j + 4 - h) % 4]
        else:
            grad_ref[here, :SIDE] = (left_ref, leftc_ref)[e][(j + 4 - h) % 4]
            grad_ref[here, SIDE:] = (right_ref, rightc_ref)[e][(j + 5 - h + 2 * l) % 4]
    total = None
    for cols, piece in spans(pieces):
        term = dot(grad_ref[:, cols], piece[...])
        total = term if total is None else total + term
    total = jnp.where(mask_ref[...].astype(F32) > 0, total * FF ** (-0.5), 0.0).astype(BF16)
    for i in range(16):
        ref = own_ref if i < 8 else oth_ref
        ref[pl.ds(token_row(i), ROWS), :] = total[i * ROWS : (i + 1) * ROWS]
    scale = ADAPTER_SCALE * MODEL_WIDTH ** (-0.5)
    sides = (
        (l, own_ref, pt_ref[0], up_own_ref, b_own_ref[...]),
        (1 - l, oth_ref, pt_ref[1], up_oth_ref, b_oth_ref[...]),
    )
    for order, (side, hid_ref, p, up_ref, b) in enumerate(sides):
        up = b.astype(F32) - RATE_UP * (scale * dot(p, hid_ref[...]))
        up_ref[...] = up
        wire_ref[side] = up.astype(BF16)
        back_ref[order] = dot_nt(b, hid_ref[...])


def route_kernel(near_ref, left_ref, right_ref, mine_ref, s1_ref, s2_ref, s3_ref):
    h = lax.axis_index("h")
    for j, ref in enumerate((mine_ref, s1_ref, s2_ref, s3_ref)):
        k = (h + j) % 4
        ref[:, :SIDE] = (near_ref[k, :, :SIDE] + left_ref[k].astype(F32)).astype(ref.dtype)
        ref[:, SIDE:] = (near_ref[k, :, SIDE:] + right_ref[k].astype(F32)).astype(ref.dtype)


def down_kernel(t0_ref, t1_ref, t2_ref, t3_ref, x_ref, a_ref, up_ref, new_ref, wire_ref):
    rest = (t0_ref[...] + t1_ref[...]) + (t2_ref[...] + t3_ref[...])
    parts = []
    for _ in range(3):
        parts.append(rest.astype(BF16))
        rest = rest - parts[-1].astype(F32)
    stacked = jnp.concatenate(parts, axis=0)
    scale = ADAPTER_SCALE * MODEL_WIDTH ** (-0.5)
    for k in range(8):
        here = slice(k * HID, (k + 1) * HID)
        grad = dot(stacked, x_ref[:, here])
        grad = grad[:RANK] + grad[RANK : 2 * RANK] + grad[2 * RANK :]
        new = a_ref[:, here].astype(F32) - RATE_DOWN * (scale * grad)
        new_ref[:, here] = new
        for j in range(4):
            wire_ref[k * 4 + j, :, :BLOCK] = new[:, j * BLOCK : (j + 1) * BLOCK].astype(BF16)
            for l in range(2):
                begin = BLOCK + l * HID
                wire_ref[k * 4 + j, :, begin : begin + HID] = up_ref[l]


def merge_kernel(wire_ref, w_ref, out_ref, d_ref, u_ref):
    for y in range(4):
        for x in range(4):
            for l in range(2):
                at = ((y * 4 + x) * 2 + l) * RANK
                d_ref[at : at + RANK, :] = wire_ref[y * 8 + l * 4 + x, :, :BLOCK]
    for side in range(2):
        for y in range(4):
            for x in range(4):
                for l in range(2):
                    at = ((y * 4 + x) * 2 + l) * RANK
                    begin = BLOCK + l * HID
                    u_ref[at : at + RANK, :] = wire_ref[
                        y * 8 + side * 4 + x, :, begin : begin + HID
                    ]
        here = slice(side * HID, (side + 1) * HID)
        delta = dot_tn(d_ref[...], u_ref[...])
        out_ref[:, here] = w_ref[:, here].astype(F32) + ADAPTER_SCALE / 32 * delta


def ring(value, axis):
    below, above = shift(value, axis, 1), shift(value, axis, -1)
    return [value, below, above, shift(below, axis, 1)]


def halves_kernel(below_ref, above_ref, low_ref, high_ref):
    low_ref[...] = below_ref[...]
    high_ref[...] = above_ref[...]


def far_halves(below, above, axis):
    block = (HID, HID)
    first, second = pl.BlockSpec(block, lambda i: (0, 0)), pl.BlockSpec(block, lambda i: (1, 0))
    low, high = pl.pallas_call(
        halves_kernel,
        grid=(1,),
        out_shape=(shape(*block), shape(*block)),
        in_specs=[first, second],
        out_specs=(first, first),
        compiler_params=pltpu.CompilerParams(vmem_limit_bytes=VMEM_LIMIT),
        name="halves",
    )(below, above)
    return [shift(low, axis, 1), shift(high, axis, -1)]


def swap(value, mask):
    return lax.ppermute(value, "h", [(i, i ^ mask) for i in range(4)])


def shards(tokens, targets, w_in, w_out, factor_down, factor_up):
    l = lax.axis_index("l")
    a = factor_down[0]
    b = factor_up[0]

    in_send, out_send = call(
        send_kernel, (shape(TOK, HID), shape(TOK + RANK, HID)), w_in, w_out, b, name="send"
    )
    in_oth = partner(in_send, "l")
    out_oth = partner(out_send, "l")
    in_own, out_own, b_own = call(
        own_kernel,
        (shape(TOK, HID), shape(TOK, HID), shape(RANK, HID)),
        w_in, w_out, b, in_send,
        name="own",
    )
    b_oth = out_oth[TOK:]
    packed, p_own = call(
        pack_kernel,
        (shape(HALF + RANK, MODEL_WIDTH), shape(RANK, TOK)),
        tokens, a,
        after=[in_own],
        name="pack",
    )
    tokens_oth = near_z(packed)
    tokens_oth_core = partner(tokens_oth, "c")

    def joined(own, oth):
        return jnp.where(
            l == 0, jnp.concatenate([own, oth], axis=0), jnp.concatenate([oth, own], axis=0)
        )

    in_line = jnp.concatenate(ring(joined(in_own, in_oth), "x"), axis=0)
    out_line = jnp.concatenate(ring(joined(out_own, out_oth[:TOK]), "y"), axis=0)
    in_near = [in_line, shift(in_line, "y", 1), shift(in_line, "y", -1)]
    out_near = [out_line, shift(out_line, "x", 1), shift(out_line, "x", -1)]

    x_near, x_far, p_rel, pt = call(
        arrange_kernel,
        (shape(2 * TOK, 3072), shape(2 * TOK, 1024), shape(2 * TOK, 2 * RANK), shape(2, RANK, TOK)),
        tokens, tokens_oth, tokens_oth_core, p_own,
        scratch=[pltpu.VMEM((2, TOK, RANK), BF16)],
        name="arrange",
    )
    in_near[1], in_near[2], x_near, p_rel = lax.optimization_barrier(
        (in_near[1], in_near[2], x_near, p_rel)
    )
    in_far = far_halves(in_near[1], in_near[2], "y")
    out_far = far_halves(out_near[1], out_near[2], "x")
    out_pieces = out_near + out_far
    total = call(
        near_kernel,
        shape(2 * TOK, HID, dtype=F32),
        x_near, p_rel, b_own, b_oth, *in_near,
        name="near",
    )
    hidden, mask = call(
        hidden_kernel,
        (shape(2 * TOK, HID), shape(2 * TOK, HID)),
        x_far, total, *in_far,
        name="hidden",
    )
    keep, send = call(
        output_kernel,
        (shape(8, ROWS, MODEL_WIDTH, dtype=F32), shape(8, ROWS, MODEL_WIDTH)),
        hidden, *out_pieces,
        name="output",
    )

    my_targets = call(
        targets_kernel, shape(ROWS, MODEL_WIDTH), targets, after=[p_rel], name="targets"
    )

    summed = keep + partner(send, "c").astype(F32)
    away = summed[4:].astype(BF16)
    left = partner(away[:, :, :SIDE], "l")
    right = away[:, :, SIDE:]
    right = near_z(right)
    mine, *steps = call(
        route_kernel,
        (shape(ROWS, MODEL_WIDTH, dtype=F32),) + (shape(ROWS, MODEL_WIDTH),) * 3,
        summed[:4], left, right,
        name="route",
    )
    steps = [shift(step, "h", j + 1).astype(F32) for j, step in enumerate(steps)]
    share = ((mine + steps[0]) + (steps[1] + steps[2])) * FF ** (-0.5)
    grad_rows = ((share - my_targets.astype(F32)) / TOK).astype(BF16)

    q = jnp.stack([grad_rows] + [shift(grad_rows, "h", -j) for j in (1, 2, 3)])
    left = partner(q[:, :, :SIDE], "l")
    right = near_z(q[:, :, SIDE:])
    q_far, left_far, right_far = partner(q, "c"), partner(left, "c"), partner(right, "c")

    up_own, up_oth, up_wire, back = call(
        backward_kernel,
        (
            shape(RANK, HID, dtype=F32),
            shape(RANK, HID, dtype=F32),
            shape(2, RANK, HID),
            shape(2, RANK, TOK, dtype=F32),
        ),
        q, q_far, left, left_far, right, right_far, mask, pt, b_own, b_oth, *out_pieces,
        scratch=[
            pltpu.VMEM((2 * TOK, MODEL_WIDTH), BF16),
            pltpu.VMEM((TOK, HID), BF16),
            pltpu.VMEM((TOK, HID), BF16),
        ],
        name="backward",
    )
    back = back + partner(back, "c")
    back = back[0] + partner(back[1], "l")
    back = [back] + [swap(back, mask) for mask in (1, 2, 3)]
    new_a, wire = call(
        down_kernel,
        (shape(RANK, MODEL_WIDTH, dtype=F32), shape(32, RANK, BLOCK + 2 * HID)),
        *back, tokens, a, up_wire,
        name="down",
    )
    wires = lax.all_to_all(wire, REP, 0, 0, tiled=True)
    up_arrived = partner(up_oth, "l")
    new_b = jnp.where(
        l == 0,
        jnp.concatenate([up_own, up_arrived], axis=1),
        jnp.concatenate([up_arrived, up_own], axis=1),
    )
    merged = call(
        merge_kernel,
        shape(TOK, 2 * HID, dtype=F32),
        wires, w_in,
        scratch=[pltpu.VMEM((32 * RANK, BLOCK), BF16), pltpu.VMEM((32 * RANK, HID), BF16)],
        name="merge",
    )
    return merged, new_a[None], new_b[None]


def solution(mesh):
    split = Mesh(mesh.devices.reshape(4, 2, 4, 4, 2), ("y", "l", "x", "h", "c"))
    tp = ("h", "c")
    in_specs = (
        P(REP, None),
        P(REP, None),
        P(REP, tp),
        P(tp, REP),
        P(REP, None, None),
        P(REP, None, tp),
    )
    out_specs = (P(REP, tp), P(REP, None, None), P(REP, None, tp))
    return jax.shard_map(
        shards, mesh=split, in_specs=in_specs, out_specs=out_specs, check_vma=False
    )
```
